32 devices in a mesh: groups: 2 (over x), space: 16 (over z, y, core).
Axes of the slice: x: 2, y: 2, z: 4, core: 2. Of those that a mesh axis runs over, the one named last changes fastest.
Arguments:
- patches: bfloat16 [8192, 1024], P(('groups', 'space')), parts along dimension 0, may hold values from -6 to 6
- var_order: int32 [64], replicated, may hold values from 0 to 63, each once
- embed_weight: bfloat16 [64, 16, 1024], replicated, may hold values from -1.5 to 1.5
- var_embed: bfloat16 [64, 1024], replicated, may hold values from -2 to 2
- agg_keys: bfloat16 [16, 1024], replicated, may hold values from -9 to 9
- agg_value: bfloat16 [1024, 1024], replicated, may hold values from -0.1875 to 0.1875
- agg_out: bfloat16 [1024, 1024], replicated, may hold values from -0.1875 to 0.1875
- pos_embed: bfloat16 [4096, 1024], P('space'), may hold values from -3 to 3
- norm_gain: float32 [1024], replicated, may hold values from 0.25 to 1.75
- qkv_weight: bfloat16 [1024, 3072], P(None, 'space'), may hold values from -2.6 to 2.6
- attn_out: bfloat16 [1024, 1024], replicated, may hold values from -0.1875 to 0.1875
Outputs:
- encoded: bfloat16 [8192, 1024], P(('groups', 'space')), parts along dimension 0
The draws below stay inside these ranges and needn't reach their ends.
There are 2 independent parts, one for each index of `groups`. The reference program is written for one: setup_inputs(seed, part) draws one part's arguments, and reference() takes and returns one part's arrays. A program takes and returns all parts, laid end to end along the dimension named above; an argument that names none is the same for every part. Nothing has to cross between parts.
Inputs may be any that keep to these rules, and one draw needn't show every extreme that they name: var_order is a permutation of the variables.
All inputs are finite; a program needn't handle non-finite values.
Results may differ from the reference program's by a relative error of at most 0.008.
Values may be sent and summed in bfloat16 or wider, within the bound.
No kernel may reach another device: no remote copies, remote signals or barrier semaphores. Data moves between devices by JAX's collectives and lax.ppermute only.
A program may use at most 128 MiB of HBM per device.

```python
import math
import jax
import jax.numpy as jnp
from jax import lax

VARS = 64
PIX = 16
D = 1024
HEADS = 16
HD = 64
RADIUS = 2
TOK_DEV = 256
TOKENS = 4096
N_SPACE = 16


def paired_draw(key):
    base_key = jax.random.fold_in(jax.random.fold_in(key, 11), 0)
    query_key = jax.random.fold_in(jax.random.fold_in(key, 11), 2)
    embeds = 0.5 * jax.random.truncated_normal(base_key, -4.0, 4.0, (VARS, D), jnp.float32)
    queries = 0.25 * jax.random.truncated_normal(query_key, -4.0, 4.0, (HEADS, D), jnp.float32)
    return (embeds, queries)


def draw_var_embed(key, part):
    embeds, queries = paired_draw(key)
    return embeds.astype(jnp.bfloat16)


def draw_agg_keys(key, part):
    embeds, queries = paired_draw(key)
    return queries.astype(jnp.bfloat16)


def draw_qkv_weight(key, part):
    main_key = jax.random.fold_in(key, 23)
    weights = jax.random.truncated_normal(main_key, -4.0, 4.0, (D, 3 * D), jnp.float32) / jnp.sqrt(float(D))
    return weights.astype(jnp.bfloat16)


def block_levels(key, dims, shards, least, high):
    factor_of = 1.0
    for dim, parts in shards:
        heights = jax.random.uniform(jax.random.fold_in(jax.random.fold_in(key, 6), dim), (parts,), jnp.float32, least / len(shards), high / len(shards))
        factor_of = factor_of * jnp.repeat(jnp.exp(heights), dims[dim] // parts).reshape((-1,) + (1,) * (len(dims) - 1 - dim))
    return factor_of


def gaussian(rng, shape, scale, limit, cuts=(), kind=jnp.bfloat16):
    drawn = scale * jax.random.normal(rng, shape, jnp.float32)
    if cuts:
        drawn = drawn * block_levels(rng, shape, cuts, -0.22, 0.18)
    return jnp.clip(drawn, -limit, limit).astype(kind)


def setup_inputs(seed: int = 0, part: int = 0) -> dict:
    arg_keys = jax.random.split(jax.random.key(seed), 12)
    part_splits = jax.random.split(jax.random.fold_in(arg_keys[11], part), 12)
    return {
        "patches": gaussian(part_splits[0], (TOKENS, VARS * PIX), 1.0, 6.0, ((0, 16),)),
        "var_order": jax.random.permutation(arg_keys[1], VARS).astype(jnp.int32),
        "embed_weight": gaussian(arg_keys[2], (VARS, PIX, D), PIX ** -0.5, 1.5),
        "var_embed": draw_var_embed(jax.random.fold_in(arg_keys[11], 71), part),
        "agg_keys": draw_agg_keys(jax.random.fold_in(arg_keys[11], 71), part),
        "agg_value": gaussian(arg_keys[5], (D, D), D ** -0.5, 0.1875),
        "agg_out": gaussian(arg_keys[6], (D, D), D ** -0.5, 0.1875),
        "pos_embed": gaussian(arg_keys[7], (TOKENS, D), 0.5, 3.0, ((0, 16),)),
        "norm_gain": jnp.clip(1.0 + 0.15 * jax.random.normal(arg_keys[8], (D,), jnp.float32), 0.25, 1.75),
        "qkv_weight": draw_qkv_weight(jax.random.fold_in(arg_keys[11], 71), part),
        "attn_out": gaussian(arg_keys[10], (D, D), D ** -0.5, 0.1875),
    }


def rounded(values):
    return lax.optimization_barrier(values.astype(jnp.bfloat16))

def layer_norm(values, norm_gain):
    average = lax.optimization_barrier(jnp.mean(values, axis=-1, keepdims=True))
    centred = values - average
    spread = lax.optimization_barrier(jnp.mean(centred * centred, axis=-1, keepdims=True))
    return centred * lax.rsqrt(spread + 1e-05) * norm_gain

def reference(patches, var_order, embed_weight, var_embed, agg_keys, agg_value, agg_out, pos_embed, norm_gain, qkv_weight, attn_out):
    select = (var_order[:, None] == jnp.arange(VARS, dtype=jnp.int32)[None, :]).astype(jnp.float32)
    var_table = jnp.einsum('jv,vpd->jpd', select, embed_weight.astype(jnp.float32))
    offsets = jnp.einsum('jv,vd->jd', select, var_embed.astype(jnp.float32))
    score_scale = 1.0 / math.sqrt(HD)
    query_keys = agg_keys.astype(jnp.float32)
    value_heads = agg_value.astype(jnp.float32).reshape(D, HEADS, HD)

    def aggregate(patch_rows):
        pieces = patch_rows.astype(jnp.float32).reshape(TOK_DEV, VARS, PIX)
        embedded = rounded(jnp.einsum('tjp,jpd->tjd', pieces, var_table) + offsets[None]).astype(jnp.float32)
        scores = jnp.einsum('tjd,hd->thj', embedded, query_keys) * score_scale
        attention = rounded(jax.nn.softmax(scores, axis=-1)).astype(jnp.float32)
        pooled = rounded(jnp.einsum('thj,tjd->thd', attention, embedded)).astype(jnp.float32)
        return jnp.einsum('thd,dhe->the', pooled, value_heads).reshape(TOK_DEV, D).astype(jnp.bfloat16)
    values = lax.map(aggregate, patches.reshape(N_SPACE, TOK_DEV, VARS * PIX)).reshape(TOKENS, D)
    tokens_zero = (jnp.dot(values, agg_out, preferred_element_type=jnp.float32) + pos_embed.astype(jnp.float32)).astype(jnp.bfloat16)
    normed = layer_norm(tokens_zero.astype(jnp.float32), norm_gain).astype(jnp.bfloat16)
    projections = jnp.dot(normed, qkv_weight, preferred_element_type=jnp.float32).astype(jnp.bfloat16)
    sectors = projections.reshape(N_SPACE, TOK_DEV, 3 * D)

    def attend(sector):
        own_block = lax.dynamic_index_in_dim(sectors, sector, 0, keepdims=False)
        window_parts = [lax.dynamic_index_in_dim(sectors, (sector + offset) % N_SPACE, 0, keepdims=False) for offset in range(-RADIUS, RADIUS + 1)]
        window = jnp.concatenate(window_parts, axis=0)
        queries = own_block[:, :D].astype(jnp.float32).reshape(TOK_DEV, HEADS, HD)
        key_rows = window[:, D:2 * D].astype(jnp.float32).reshape(-1, HEADS, HD)
        value_rows = window[:, 2 * D:].astype(jnp.float32).reshape(-1, HEADS, HD)
        scores = jnp.einsum('qhe,khe->hqk', queries, key_rows) * score_scale
        attention = rounded(jax.nn.softmax(scores, axis=-1)).astype(jnp.float32)
        context = jnp.einsum('hqk,khe->qhe', attention, value_rows)
        return context.reshape(TOK_DEV, D).astype(jnp.bfloat16)
    context = lax.map(attend, jnp.arange(N_SPACE, dtype=jnp.int32)).reshape(TOKENS, D)
    update = jnp.dot(context, attn_out, preferred_element_type=jnp.float32)
    return (tokens_zero.astype(jnp.float32) + update).astype(jnp.bfloat16)
```

```python
import functools
import math

import jax
import jax.numpy as jnp
from jax import lax
from jax.experimental import pallas as pl
from jax.experimental.pallas import tpu as pltpu
from jax.sharding import PartitionSpec as P

BF16 = jnp.bfloat16
F32 = jnp.float32
LANES = 128
VMEM_LIMIT = 56 * 1024 * 1024


def dot(left, right):
    return jnp.dot(left, right, preferred_element_type=F32)


def dot_t(left, right):
    return lax.dot_general(left, right, (((1,), (1,)), ((), ())), preferred_element_type=F32)


def iota(shape, dim):
    return lax.broadcasted_iota(jnp.int32, shape, dim)


def aggregate_kernel(
    order_ref,
    order_col_ref,
    patches_ref,
    embed_ref,
    var_embed_ref,
    keys_ref,
    value_ref,
    out_w_ref,
    pos_ref,
    gain_ref,
    tokens_ref,
    normed_ref,
    table_ref,
):
    var_count, pixels, width = embed_ref.shape
    heads = keys_ref.shape[0]
    head_size = width // heads
    scale = 1.0 / math.sqrt(head_size)
    tokens = patches_ref.shape[0]
    spread = var_count * heads

    for j in range(var_count):
        table_ref[j] = embed_ref[order_ref[j]]
    table = table_ref[...].reshape(var_count * pixels, width)
    select = (order_col_ref[...] == iota((var_count, var_count), 1)).astype(F32).astype(BF16)
    offsets = dot(select, var_embed_ref[...]).astype(BF16)

    repeat = (iota((LANES, heads), 0) % heads == iota((LANES, heads), 1)).astype(F32).astype(BF16)
    keys = dot(repeat, keys_ref[...]).astype(BF16)
    table_keys = dot_t(table, keys)
    offset_keys = dot_t(offsets, keys)
    high = table_keys.astype(BF16)
    low = (table_keys - high.astype(F32)).astype(BF16)
    patches = patches_ref[...]
    copies = spread // LANES
    rows_of = iota((var_count * pixels, LANES), 0) // pixels
    scores = []
    for block in range(copies):
        cols_of = (iota((var_count * pixels, LANES), 1) + block * LANES) // heads
        here = rows_of == cols_of
        high_b = jnp.where(here, high, jnp.zeros_like(high))
        low_b = jnp.where(here, low, jnp.zeros_like(low))
        channel = (iota((var_count, LANES), 1) + block * LANES) // heads
        row = jnp.sum(
            jnp.where(channel == iota((var_count, LANES), 0), offset_keys, 0.0),
            axis=0,
            keepdims=True,
        )
        scores.append((dot(patches, high_b) + dot(patches, low_b) + row) * scale)

    top = functools.reduce(jnp.maximum, scores)
    step = heads
    while step < LANES:
        top = jnp.maximum(top, pltpu.roll(top, step, 1))
        step *= 2
    exps = [jnp.exp(s - top) for s in scores]
    total = functools.reduce(jnp.add, exps)
    step = heads
    while step < LANES:
        total = total + pltpu.roll(total, step, 1)
        step *= 2
    probs = jnp.concatenate([(e / total).astype(BF16) for e in exps], axis=1)

    table_values = dot(table, value_ref[...]).astype(BF16)
    offset_values = dot(offsets, value_ref[...]).astype(BF16)
    spread_rows = (iota((spread, var_count), 0) // heads == iota((spread, var_count), 1)).astype(F32)
    offset_rows = dot(spread_rows.astype(BF16), offset_values).astype(BF16)
    mine = iota((spread, width), 0) % heads == iota((spread, width), 1) // head_size
    offset_rows = jnp.where(mine, offset_rows, jnp.zeros_like(offset_rows))
    base = dot(probs, offset_rows)

    group = math.gcd(spread, 256)
    row_g, col_g = iota((group, group), 0), iota((group, group), 1)
    same = row_g // heads == col_g // pixels
    left_half = iota((tokens, 2 * head_size), 1) < head_size
    values = []
    for pair in range(heads // 2):
        halves = []
        cols = slice(pair * 2 * head_size, (pair + 1) * 2 * head_size)
        for head in (2 * pair, 2 * pair + 1):
            pick = jnp.where(same & (row_g % heads == head), 1.0, 0.0).astype(BF16)
            weights = jnp.concatenate(
                [
                    dot(probs[:, g * group : (g + 1) * group], pick).astype(BF16)
                    for g in range(spread // group)
                ],
                axis=1,
            )
            halves.append(dot(weights * patches, table_values[:, cols]))
        values.append((jnp.where(left_half, halves[0], halves[1]) + base[:, cols]).astype(BF16))
    values = jnp.concatenate(values, axis=1)

    tokens_zero = (dot(values, out_w_ref[...]) + pos_ref[...].astype(F32)).astype(BF16)
    tokens_ref[...] = tokens_zero
    full = tokens_zero.astype(F32)
    centred = full - jnp.mean(full, axis=-1, keepdims=True)
    variance = jnp.mean(centred * centred, axis=-1, keepdims=True)
    normed_ref[...] = (centred * lax.rsqrt(variance + 1e-05) * gain_ref[...]).astype(BF16)


def aggregate(patches, var_order, embed_weight, var_embed, keys, value, out_w, pos, gain):
    tokens, width = pos.shape
    var_count = embed_weight.shape[0]
    vmem = pl.BlockSpec(memory_space=pltpu.VMEM)
    return pl.pallas_call(
        aggregate_kernel,
        out_shape=[jax.ShapeDtypeStruct((tokens, width), BF16)] * 2,
        in_specs=[pl.BlockSpec(memory_space=pltpu.SMEM)] + [vmem] * 9,
        out_specs=[vmem, vmem],
        scratch_shapes=[pltpu.VMEM(embed_weight.shape, BF16)],
        compiler_params=pltpu.CompilerParams(vmem_limit_bytes=VMEM_LIMIT),
        cost_estimate=pl.CostEstimate(
            flops=12 * width * width * tokens * 4, bytes_accessed=9 << 20, transcendentals=1 << 18
        ),
        name="aggregate",
    )(
        var_order,
        var_order.reshape(var_count, 1),
        patches,
        embed_weight,
        var_embed,
        keys,
        value,
        out_w,
        pos,
        gain.reshape(1, width),
    )


def attend_kernel(
    side_ref,
    own_ref,
    sib_ref,
    left_own_ref,
    left_sib_ref,
    right_own_ref,
    right_sib_ref,
    weight_ref,
    context_ref,
    query_s,
    key_s,
    value_s,
):
    side = side_ref[0]
    tokens = own_ref.shape[0]
    kinds, cols, width = weight_ref.shape
    pairs = cols // LANES
    head_size = LANES // 2
    scale = 1.0 / math.sqrt(head_size)
    pieces = [
        (left_own_ref, side),
        (left_sib_ref, 1 - side),
        (own_ref, 2 + side),
        (sib_ref, 3 - side),
        (right_own_ref, 4 + side),
        (right_sib_ref, 5 - side),
    ]
    ones = jnp.ones((tokens, LANES), BF16)
    for number, (ref, place) in enumerate(pieces):
        rows = ref[...]
        key_s[place] = dot_t(weight_ref[1], rows).astype(BF16)
        value = dot_t(rows, weight_ref[2]).astype(BF16)
        for pair in range(pairs):
            value_s[place, pair] = jnp.concatenate(
                [value[:, pair * LANES : (pair + 1) * LANES], ones], axis=1
            )
        if number in (2, 3):
            query = (dot_t(rows, weight_ref[0]).astype(BF16).astype(F32) * scale).astype(BF16)
            for pair in range(pairs):
                query_s[place - 2, pair] = query[:, pair * LANES : (pair + 1) * LANES]

    left_half = iota((tokens, LANES), 1) < head_size

    def attend(pair, carry):
        row = pl.multiple_of(pair * LANES, LANES)
        for sector in range(2):
            query = query_s[sector, pair]
            halves = []
            for half in range(2):
                keep = left_half if half == 0 else jnp.logical_not(left_half)
                masked = jnp.where(keep, query, jnp.zeros_like(query))
                scores = [
                    dot(masked, key_s[sector + k, pl.ds(row, LANES), :]) for k in range(5)
                ]
                top = jnp.max(functools.reduce(jnp.maximum, scores), axis=-1, keepdims=True)
                acc = None
                for k in range(5):
                    part = dot(jnp.exp(scores[k] - top).astype(BF16), value_s[sector + k, pair])
                    acc = part if acc is None else acc + part
                halves.append(acc[:, :LANES] / acc[:, LANES:])
            context_ref[sector, pair] = jnp.where(left_half, halves[0], halves[1]).astype(BF16)
        return carry

    lax.fori_loop(0, pairs, attend, 0)


def attend(side, pieces, weight):
    tokens, width = pieces[0].shape
    cols = weight.shape[1]
    pairs = cols // LANES
    vmem = pl.BlockSpec(memory_space=pltpu.VMEM)
    return pl.pallas_call(
        attend_kernel,
        out_shape=jax.ShapeDtypeStruct((2, pairs, tokens, LANES), BF16),
        in_specs=[pl.BlockSpec(memory_space=pltpu.SMEM)] + [vmem] * 7,
        out_specs=vmem,
        scratch_shapes=[
            pltpu.VMEM((2, pairs, tokens, LANES), BF16),
            pltpu.VMEM((6, cols, tokens), BF16),
            pltpu.VMEM((6, pairs, tokens, 2 * LANES), BF16),
        ],
        compiler_params=pltpu.CompilerParams(vmem_limit_bytes=VMEM_LIMIT),
        cost_estimate=pl.CostEstimate(
            flops=40 * width * cols * tokens, bytes_accessed=8 << 20, transcendentals=5 << 20
        ),
        name="attend",
    )(side, *pieces, weight)


def finish_kernel(side_ref, tokens_ref, mine_ref, other_ref, weight_ref, out_ref):
    side = side_ref[0]
    pairs, tokens, lanes = mine_ref.shape
    width = tokens_ref.shape[1]

    def part(ref, parity):
        rows = jnp.concatenate([ref[pair] for pair in range(pairs)], axis=1)
        return dot(rows, weight_ref[:, parity].reshape(pairs * lanes, width))

    update = part(mine_ref, side) + part(other_ref, 1 - side)
    out_ref[...] = (tokens_ref[...].astype(F32) + update).astype(BF16)


def finish(side, tokens_zero, mine, other, attn_out):
    tokens, width = tokens_zero.shape
    head_size = LANES // 2
    vmem = pl.BlockSpec(memory_space=pltpu.VMEM)
    return pl.pallas_call(
        finish_kernel,
        out_shape=jax.ShapeDtypeStruct((tokens, width), BF16),
        in_specs=[pl.BlockSpec(memory_space=pltpu.SMEM)] + [vmem] * 4,
        out_specs=vmem,
        compiler_params=pltpu.CompilerParams(vmem_limit_bytes=VMEM_LIMIT),
        cost_estimate=pl.CostEstimate(
            flops=2 * width * width * tokens, bytes_accessed=4 << 20, transcendentals=0
        ),
        name="finish",
    )(side, tokens_zero, mine, other, attn_out.reshape(-1, 2, head_size, width))


def sibling(value):
    length = lax.axis_size("space")
    return lax.ppermute(value, "space", [(i, i ^ 1) for i in range(length)])


def from_chip(value, by):
    length = lax.axis_size("space")
    return lax.ppermute(value, "space", [((i + 2 * by) % length, i) for i in range(length)])


def parity_weight(qkv_weight, side, head_size):
    rows = qkv_weight.T
    gathered = lax.all_gather(rows, "space", axis=0, tiled=True)
    width = gathered.shape[1]
    blocks = gathered.reshape(-1, 2, head_size, width)
    return lax.dynamic_index_in_dim(blocks, side, 1, keepdims=False).reshape(3, -1, width)


def per_device(
    patches,
    var_order,
    embed_weight,
    var_embed,
    agg_keys,
    agg_value,
    agg_out,
    pos_embed,
    norm_gain,
    qkv_weight,
    attn_out,
):
    head_size = embed_weight.shape[2] // agg_keys.shape[0]
    side = lax.axis_index("space") % 2
    side_arg = side.reshape(1).astype(jnp.int32)
    weight = parity_weight(qkv_weight, side, head_size)
    tokens_zero, normed = aggregate(
        patches, var_order, embed_weight, var_embed, agg_keys, agg_value, agg_out, pos_embed, norm_gain
    )
    left = from_chip(normed, -1)
    right = from_chip(normed, 1)
    pieces = (normed, sibling(normed), left, sibling(left), right, sibling(right))
    context = attend(side_arg, pieces, weight)
    mine = lax.dynamic_index_in_dim(context, side, 0, keepdims=False)
    other = sibling(lax.dynamic_index_in_dim(context, 1 - side, 0, keepdims=False))
    return finish(side_arg, tokens_zero, mine, other, attn_out)


def solution(mesh):
    in_specs = (
        P(("groups", "space"), None),
        P(),
        P(),
        P(),
        P(),
        P(),
        P(),
        P("space", None),
        P(),
        P(None, "space"),
        P(),
    )
    out_specs = P(("groups", "space"), None)
    return jax.shard_map(
        per_device, mesh=mesh, in_specs=in_specs, out_specs=out_specs, check_vma=False
    )
```

```python
import functools
import math

import jax
import jax.numpy as jnp
from jax import lax
from jax.experimental import pallas as pl
from jax.experimental.pallas import tpu as pltpu
from jax.sharding import PartitionSpec as P

BF16 = jnp.bfloat16
F32 = jnp.float32
LANES = 128
AGG_VMEM = 24 * 1024 * 1024
ATTEND_VMEM = 40 * 1024 * 1024


def dot(left, right):
    return jnp.dot(left, right, preferred_element_type=F32)


def dot_t(left, right):
    return lax.dot_general(left, right, (((1,), (1,)), ((), ())), preferred_element_type=F32)


def iota(shape, dim):
    return lax.broadcasted_iota(jnp.int32, shape, dim)


def table_kernel(
    order_ref,
    embed_ref,
    var_embed_ref,
    keys_ref,
    value_ref,
    high_ref,
    low_ref,
    row_ref,
    early_values_ref,
    late_values_ref,
    early_offset_ref,
    late_offset_ref,
    table_ref,
):
    var_count, pixels, width = embed_ref.shape
    heads = keys_ref.shape[0]
    head_size = width // heads
    spread = var_count * heads

    line = iota((var_count, var_count), 0)
    order = jnp.zeros((var_count, var_count), jnp.int32)
    for j in range(var_count):
        table_ref[j] = embed_ref[order_ref[j]]
        order = jnp.where(line == j, order_ref[j], order)
    table = table_ref[...].reshape(var_count * pixels, width)
    select = (order == iota((var_count, var_count), 1)).astype(F32).astype(BF16)
    offsets = dot(select, var_embed_ref[...]).astype(BF16)

    repeat = (iota((LANES, heads), 0) % heads == iota((LANES, heads), 1)).astype(F32).astype(BF16)
    keys = dot(repeat, keys_ref[...]).astype(BF16)
    table_keys = dot_t(table, keys)
    offset_keys = dot_t(offsets, keys)
    high = table_keys.astype(BF16)
    low = (table_keys - high.astype(F32)).astype(BF16)
    rows_of = iota((var_count * pixels, LANES), 0) // pixels
    for block in range(spread // LANES):
        cols = slice(block * LANES, (block + 1) * LANES)
        here = rows_of == (iota((var_count * pixels, LANES), 1) + block * LANES) // heads
        high_ref[:, cols] = jnp.where(here, high, jnp.zeros_like(high))
        low_ref[:, cols] = jnp.where(here, low, jnp.zeros_like(low))
        channel = (iota((var_count, LANES), 1) + block * LANES) // heads
        row_ref[:, cols] = jnp.sum(
            jnp.where(channel == iota((var_count, LANES), 0), offset_keys, 0.0),
            axis=0,
            keepdims=True,
        )

    half = width // 2
    early_values_ref[...] = dot(table, value_ref[:, :half]).astype(BF16)
    late_values_ref[...] = dot(table, value_ref[:, half:]).astype(BF16)
    offset_values = dot(offsets, value_ref[...]).astype(BF16)
    spread_rows = (iota((spread, var_count), 0) // heads == iota((spread, var_count), 1)).astype(F32)
    offset_rows = dot(spread_rows.astype(BF16), offset_values).astype(BF16)
    mine = iota((spread, width), 0) % heads == iota((spread, width), 1) // head_size
    offset_rows = jnp.where(mine, offset_rows, jnp.zeros_like(offset_rows))
    early_offset_ref[...] = offset_rows[:, :half]
    late_offset_ref[...] = offset_rows[:, half:]


def mix_heads(probs, patches, table_values, base, first, pairs, heads, head_size, pixels):
    tokens, spread = probs.shape
    group = math.gcd(spread, 256)
    row_g, col_g = iota((group, group), 0), iota((group, group), 1)
    same = row_g // heads == col_g // pixels
    left_half = iota((tokens, 2 * head_size), 1) < head_size
    values = []
    for pair in range(pairs):
        halves = []
        cols = slice(pair * 2 * head_size, (pair + 1) * 2 * head_size)
        for head in (first + 2 * pair, first + 2 * pair + 1):
            pick = jnp.where(same & (row_g % heads == head), 1.0, 0.0).astype(BF16)
            weights = jnp.concatenate(
                [
                    dot(probs[:, g * group : (g + 1) * group], pick).astype(BF16)
                    for g in range(spread // group)
                ],
                axis=1,
            )
            halves.append(dot(weights * patches, table_values[:, cols]))
        values.append((jnp.where(left_half, halves[0], halves[1]) + base[:, cols]).astype(BF16))
    return jnp.concatenate(values, axis=1)


def first_kernel(
    patches_ref, high_ref, low_ref, row_ref, values_ref, offset_ref, probs_ref, half_ref, *, heads
):
    tokens, spread = patches_ref.shape[0], high_ref.shape[1]
    width = patches_ref.shape[1]
    head_size = offset_ref.shape[1] * 2 // heads
    pixels = width * heads // spread
    scale = 1.0 / math.sqrt(head_size)
    patches = patches_ref[...]
    scores = []
    for block in range(spread // LANES):
        cols = slice(block * LANES, (block + 1) * LANES)
        scores.append(
            (dot(patches, high_ref[:, cols]) + dot(patches, low_ref[:, cols]) + row_ref[:, cols])
            * scale
        )
    top = functools.reduce(jnp.maximum, scores)
    step = heads
    while step < LANES:
        top = jnp.maximum(top, pltpu.roll(top, step, 1))
        step *= 2
    exps = [jnp.exp(s - top) for s in scores]
    total = functools.reduce(jnp.add, exps)
    step = heads
    while step < LANES:
        total = total + pltpu.roll(total, step, 1)
        step *= 2
    probs = jnp.concatenate([(e / total).astype(BF16) for e in exps], axis=1)
    probs_ref[...] = probs
    base = dot(probs, offset_ref[...])
    half_ref[...] = mix_heads(
        probs, patches, values_ref, base, 0, heads // 4, heads, head_size, pixels
    )


def second_kernel(
    patches_ref,
    probs_ref,
    half_ref,
    values_ref,
    offset_ref,
    out_w_ref,
    pos_ref,
    gain_ref,
    tokens_ref,
    normed_ref,
    *,
    heads,
):
    spread = probs_ref.shape[1]
    head_size = out_w_ref.shape[0] // heads
    pixels = patches_ref.shape[1] * heads // spread
    probs = probs_ref[...]
    base = dot(probs, offset_ref[...])
    late = mix_heads(
        probs,
        patches_ref[...],
        values_ref,
        base,
        heads // 2,
        heads // 4,
        heads,
        head_size,
        pixels,
    )
    values = jnp.concatenate([half_ref[...], late], axis=1)
    tokens_zero = (dot(values, out_w_ref[...]) + pos_ref[...].astype(F32)).astype(BF16)
    tokens_ref[...] = tokens_zero
    full = tokens_zero.astype(F32)
    centred = full - jnp.mean(full, axis=-1, keepdims=True)
    variance = jnp.mean(centred * centred, axis=-1, keepdims=True)
    normed_ref[...] = (centred * lax.rsqrt(variance + 1e-05) * gain_ref[...]).astype(BF16)


def cost(gflops, mib, exps=0):
    return pl.CostEstimate(
        flops=int(gflops * 1e9), bytes_accessed=int(mib * (1 << 20)), transcendentals=exps
    )


VMEM = pl.BlockSpec(memory_space=pltpu.VMEM)
SMEM = pl.BlockSpec(memory_space=pltpu.SMEM)


def aggregate(patches, var_order, embed_weight, var_embed, keys, value, out_w, pos, gain):
    tokens, width = pos.shape
    var_count, pixels, _ = embed_weight.shape
    heads = keys.shape[0]
    spread = var_count * heads
    half = width // 2
    params = pltpu.CompilerParams(vmem_limit_bytes=AGG_VMEM)
    high, low, row, early_values, late_values, early_offset, late_offset = pl.pallas_call(
        table_kernel,
        out_shape=[
            jax.ShapeDtypeStruct((var_count * pixels, spread), BF16),
            jax.ShapeDtypeStruct((var_count * pixels, spread), BF16),
            jax.ShapeDtypeStruct((1, spread), F32),
            jax.ShapeDtypeStruct((var_count * pixels, half), BF16),
            jax.ShapeDtypeStruct((var_count * pixels, half), BF16),
            jax.ShapeDtypeStruct((spread, half), BF16),
            jax.ShapeDtypeStruct((spread, half), BF16),
        ],
        in_specs=[SMEM] + [VMEM] * 4,
        out_specs=[VMEM] * 7,
        scratch_shapes=[pltpu.VMEM(embed_weight.shape, BF16)],
        compiler_params=params,
        cost_estimate=cost(6, 12),
        name="tables",
    )(var_order, embed_weight, var_embed, keys, value)
    probs, early = pl.pallas_call(
        functools.partial(first_kernel, heads=heads),
        out_shape=[
            jax.ShapeDtypeStruct((tokens, spread), BF16),
            jax.ShapeDtypeStruct((tokens, half), BF16),
        ],
        in_specs=[VMEM] * 6,
        out_specs=[VMEM] * 2,
        compiler_params=params,
        cost_estimate=cost(6, 8, 1 << 18),
        name="early_heads",
    )(patches, high, low, row, early_values, early_offset)
    return pl.pallas_call(
        functools.partial(second_kernel, heads=heads),
        out_shape=[jax.ShapeDtypeStruct((tokens, width), BF16)] * 2,
        in_specs=[VMEM] * 8,
        out_specs=[VMEM] * 2,
        compiler_params=params,
        cost_estimate=cost(6, 8),
        name="late_heads",
    )(patches, probs, early, late_values, late_offset, out_w, pos, gain.reshape(1, width))


def attend_kernel(places_ref, *refs):
    count = len(refs) - 13
    own_ref, sib_ref, left_own_ref, left_sib_ref, right_own_ref, right_sib_ref = refs[:6]
    weight_refs = refs[6 : 6 + count]
    mine_ref, other_ref, query_s, key_s, value_s, weight_s, sems = refs[6 + count :]
    side = places_ref[0]
    copies = [
        pltpu.make_async_copy(ref, weight_s.at[places_ref[1 + i]], sems.at[i])
        for i, ref in enumerate(weight_refs)
    ]
    for copy in copies:
        copy.start()
    for copy in copies:
        copy.wait()
    tokens, width = own_ref.shape
    pairs = mine_ref.shape[0]
    cols = pairs * LANES
    weight = weight_s[...].reshape(3, cols, width)
    head_size = LANES // 2
    scale = 1.0 / math.sqrt(head_size)
    pieces = [
        (left_own_ref, side),
        (left_sib_ref, 1 - side),
        (own_ref, 2 + side),
        (sib_ref, 3 - side),
        (right_own_ref, 4 + side),
        (right_sib_ref, 5 - side),
    ]
    ones = jnp.ones((tokens, LANES), BF16)
    for number, (ref, place) in enumerate(pieces):
        rows = ref[...]
        key_s[place] = dot_t(weight[1], rows).astype(BF16)
        value = dot_t(rows, weight[2]).astype(BF16)
        for pair in range(pairs):
            value_s[place, pair] = jnp.concatenate(
                [value[:, pair * LANES : (pair + 1) * LANES], ones], axis=1
            )
        if number in (2, 3):
            query = (dot_t(rows, weight[0]).astype(BF16).astype(F32) * scale).astype(BF16)
            for pair in range(pairs):
                query_s[number - 2, pair] = query[:, pair * LANES : (pair + 1) * LANES]

    left_half = iota((tokens, LANES), 1) < head_size

    def attend(pair, carry):
        row = pl.multiple_of(pair * LANES, LANES)
        for number, (out_ref, sector) in enumerate(((mine_ref, side), (other_ref, 1 - side))):
            query = query_s[number, pair]
            halves = []
            for half in range(2):
                keep = left_half if half == 0 else jnp.logical_not(left_half)
                masked = jnp.where(keep, query, jnp.zeros_like(query))
                scores = [
                    dot(masked, key_s[sector + k, pl.ds(row, LANES), :]) for k in range(5)
                ]
                top = jnp.max(functools.reduce(jnp.maximum, scores), axis=-1, keepdims=True)
                acc = None
                for k in range(5):
                    part = dot(jnp.exp(scores[k] - top).astype(BF16), value_s[sector + k, pair])
                    acc = part if acc is None else acc + part
                halves.append(acc[:, :LANES] / acc[:, LANES:])
            out_ref[pair] = jnp.where(left_half, halves[0], halves[1]).astype(BF16)
        return carry

    lax.fori_loop(0, pairs, attend, 0)


def attend(places, pieces, weights):
    tokens, width = pieces[0].shape
    rows = weights[0].shape[0]
    cols = rows * len(weights) // 3
    pairs = cols // LANES
    return pl.pallas_call(
        attend_kernel,
        out_shape=[jax.ShapeDtypeStruct((pairs, tokens, LANES), BF16)] * 2,
        in_specs=[SMEM] + [VMEM] * 6 + [pl.BlockSpec(memory_space=pl.ANY)] * len(weights),
        out_specs=[VMEM, VMEM],
        scratch_shapes=[
            pltpu.VMEM((2, pairs, tokens, LANES), BF16),
            pltpu.VMEM((6, cols, tokens), BF16),
            pltpu.VMEM((6, pairs, tokens, 2 * LANES), BF16),
            pltpu.VMEM((len(weights), rows, width), BF16),
            pltpu.SemaphoreType.DMA((len(weights),)),
        ],
        compiler_params=pltpu.CompilerParams(vmem_limit_bytes=ATTEND_VMEM),
        cost_estimate=cost(10, 8, 5 << 20),
        name="attend",
    )(places, *pieces, *weights)


def finish_kernel(side_ref, tokens_ref, mine_ref, other_ref, weight_ref, out_ref):
    side = side_ref[0]
    pairs, tokens, lanes = mine_ref.shape
    width = tokens_ref.shape[1]

    def part(ref, parity):
        rows = jnp.concatenate([ref[pair] for pair in range(pairs)], axis=1)
        return dot(rows, weight_ref[:, parity].reshape(pairs * lanes, width))

    update = part(mine_ref, side) + part(other_ref, 1 - side)
    out_ref[...] = (tokens_ref[...].astype(F32) + update).astype(BF16)


def finish(places, tokens_zero, mine, other, attn_out):
    tokens, width = tokens_zero.shape
    return pl.pallas_call(
        finish_kernel,
        out_shape=jax.ShapeDtypeStruct((tokens, width), BF16),
        in_specs=[SMEM] + [VMEM] * 4,
        out_specs=VMEM,
        compiler_params=pltpu.CompilerParams(vmem_limit_bytes=AGG_VMEM),
        cost_estimate=cost(1, 4),
        name="finish",
    )(places, tokens_zero, mine, other, attn_out.reshape(-1, 2, LANES // 2, width))


def sibling(value):
    length = lax.axis_size("space")
    return lax.ppermute(value, "space", [(i, i ^ 1) for i in range(length)])


def from_chip(value, by):
    length = lax.axis_size("space")
    return lax.ppermute(value, "space", [((i + 2 * by) % length, i) for i in range(length)])


RING = (0, 2, 4, 6, 7, 5, 3, 1)


def around(value, by):
    pairs = []
    for place, chip in enumerate(RING):
        for core in range(2):
            step = by if isinstance(by, int) else by[core]
            pairs.append((2 * chip + core, 2 * RING[(place + step) % len(RING)] + core))
    return lax.ppermute(value, "space", pairs)


def parity_weight(qkv_weight, side, head_size):
    rows = qkv_weight.T
    width = rows.shape[1]
    length = lax.axis_size("space")
    if length != 2 * len(RING) or rows.shape[0] != 3 * head_size:
        gathered = lax.all_gather(rows, "space", axis=0, tiled=True)
        blocks = gathered.reshape(-1, 2, head_size, width)
        picked = lax.dynamic_index_in_dim(blocks, side, 1, keepdims=False)
        return [picked.reshape(-1, width)], [jnp.int32(0)]
    low, middle, high = (rows[i * head_size : (i + 1) * head_size] for i in range(3))
    given = sibling(middle)
    block = jnp.where(
        side == 0,
        jnp.concatenate([low, high, given], axis=0),
        jnp.concatenate([given, low, high], axis=0),
    )
    chip = lax.axis_index("space") // 2
    here = jnp.where(chip % 2 == 0, chip // 2, 7 - chip // 2)

    def place(step):
        at = (here + step) % 8
        return jnp.where(at < 4, 2 * at, 2 * (7 - at) + 1).astype(jnp.int32)

    pieces, places = [block], [place(0)]
    up = down = block
    for step in (1, 2, 3):
        up, down = around(up, 1), around(down, -1)
        pieces += [up, down]
        places += [place(-step), place(step)]
    pieces.append(around(jnp.where(side == 0, up, down), (1, -1)))
    places.append(place(4))
    return pieces, places


def per_device(
    patches,
    var_order,
    embed_weight,
    var_embed,
    agg_keys,
    agg_value,
    agg_out,
    pos_embed,
    norm_gain,
    qkv_weight,
    attn_out,
):
    head_size = embed_weight.shape[2] // agg_keys.shape[0]
    side = (lax.axis_index("space") % 2).astype(jnp.int32)
    weights, spots = parity_weight(qkv_weight, side, head_size)
    places = jnp.stack([side] + spots)
    tokens_zero, normed = aggregate(
        patches, var_order, embed_weight, var_embed, agg_keys, agg_value, agg_out, pos_embed, norm_gain
    )
    left = from_chip(normed, -1)
    right = from_chip(normed, 1)
    pieces = (normed, sibling(normed), left, sibling(left), right, sibling(right))
    mine, other = attend(places, pieces, weights)
    return finish(places, tokens_zero, mine, sibling(other), attn_out)


def solution(mesh):
    in_specs = (
        P(("groups", "space"), None),
        P(),
        P(),
        P(),
        P(),
        P(),
        P(),
        P("space", None),
        P(),
        P(None, "space"),
        P(),
    )
    out_specs = P(("groups", "space"), None)
    return jax.shard_map(
        per_device, mesh=mesh, in_specs=in_specs, out_specs=out_specs, check_vma=False
    )
```

```python
import functools
import math

import jax
import jax.numpy as jnp
from jax import lax
from jax.experimental import pallas as pl
from jax.experimental.pallas import tpu as pltpu
from jax.sharding import PartitionSpec as P

BF16 = jnp.bfloat16
F32 = jnp.float32
LANES = 128
WHOLE_VMEM = 60 * 1024 * 1024
PART_VMEM = 24 * 1024 * 1024
RING = (0, 2, 4, 6, 7, 5, 3, 1)


def dot(left, right):
    return jnp.dot(left, right, preferred_element_type=F32)


def dot_t(left, right):
    return lax.dot_general(left, right, (((1,), (1,)), ((), ())), preferred_element_type=F32)


def chip_at(index, step):
    if step is None:
        return 0
    chip = index // 2
    here = jnp.where(chip % 2 == 0, chip // 2, 7 - chip // 2)
    at = (here + step + 8) % 8
    return jnp.where(at < 4, 2 * at, 2 * (7 - at) + 1)


def iota(shape, dim):
    return lax.broadcasted_iota(jnp.int32, shape, dim)


def fetch(pairs, sems):
    copies = [pltpu.make_async_copy(src, dst, sems.at[i]) for i, (src, dst) in enumerate(pairs)]
    for copy in copies:
        copy.start()
    return [copy.wait for copy in copies]


def table_kernel(
    order_ref,
    embed_hbm,
    var_embed_hbm,
    keys_hbm,
    value_hbm,
    high_ref,
    low_ref,
    row_ref,
    values_ref,
    offset_ref,
    embed_ref,
    var_embed_ref,
    keys_ref,
    value_ref,
    table_ref,
    sems,
):
    var_count, pixels, width = embed_ref.shape
    heads = keys_ref.shape[0]
    spread = var_count * heads
    waits = fetch(
        (
            (var_embed_hbm, var_embed_ref),
            (keys_hbm, keys_ref),
            (embed_hbm, embed_ref),
            (value_hbm, value_ref),
        ),
        sems,
    )
    line = iota((var_count, var_count), 0)
    order = jnp.zeros((var_count, var_count), jnp.int32)
    for j in range(var_count):
        order = jnp.where(line == j, order_ref[j], order)
    select = (order == iota((var_count, var_count), 1)).astype(F32).astype(BF16)
    waits[0]()
    offsets = dot(select, var_embed_ref[...]).astype(BF16)
    waits[1]()
    repeat = (iota((LANES, heads), 0) % heads == iota((LANES, heads), 1)).astype(F32).astype(BF16)
    keys = dot(repeat, keys_ref[...]).astype(BF16)
    waits[2]()
    for j in range(var_count):
        table_ref[j] = embed_ref[order_ref[j]]
    table = table_ref[...].reshape(var_count * pixels, width)
    table_keys = dot_t(table, keys)
    offset_keys = dot_t(offsets, keys)
    high = table_keys.astype(BF16)
    high_ref[...] = high
    low_ref[...] = (table_keys - high.astype(F32)).astype(BF16)
    for block in range(spread // LANES):
        cols = slice(block * LANES, (block + 1) * LANES)
        channel = (iota((var_count, LANES), 1) + block * LANES) // heads
        row_ref[:, cols] = jnp.sum(
            jnp.where(channel == iota((var_count, LANES), 0), offset_keys, 0.0),
            axis=0,
            keepdims=True,
        )
    waits[3]()
    values = dot(table, value_ref[...]).astype(BF16)
    offset_values = dot(offsets, value_ref[...]).astype(BF16)
    half = width // 2
    for side in range(2):
        values_ref[side] = values[:, side * half : (side + 1) * half]
        offset_ref[side] = offset_values[:, side * half : (side + 1) * half]


def spread_offsets(offset_half, heads, head_size, first):
    var_count, half = offset_half.shape
    spread = var_count * heads
    picks = (iota((spread, var_count), 0) // heads == iota((spread, var_count), 1)).astype(F32)
    rows = dot(picks.astype(BF16), offset_half).astype(BF16)
    mine = iota((spread, half), 0) % heads == iota((spread, half), 1) // head_size + first
    return jnp.where(mine, rows, jnp.zeros_like(rows))


def mix_heads(probs, patches, table_values, base, first, pairs, heads, head_size, pixels):
    tokens, spread = probs.shape
    group = math.gcd(spread, 256)
    row_g, col_g = iota((group, group), 0), iota((group, group), 1)
    same = row_g // heads == col_g // pixels
    left_half = iota((tokens, 2 * head_size), 1) < head_size
    values = []
    for pair in range(pairs):
        halves = []
        cols = slice(pair * 2 * head_size, (pair + 1) * 2 * head_size)
        for head in (first + 2 * pair, first + 2 * pair + 1):
            pick = jnp.where(same & (row_g % heads == head), 1.0, 0.0).astype(BF16)
            weights = jnp.concatenate(
                [
                    dot(probs[:, g * group : (g + 1) * group], pick).astype(BF16)
                    for g in range(spread // group)
                ],
                axis=1,
            )
            halves.append(dot(weights * patches, table_values[:, cols]))
        values.append((jnp.where(left_half, halves[0], halves[1]) + base[:, cols]).astype(BF16))
    return jnp.concatenate(values, axis=1)


def early_kernel(
    patches_hbm,
    high_hbm,
    low_hbm,
    row_hbm,
    values_hbm,
    offset_hbm,
    probs_ref,
    half_ref,
    patches_ref,
    high_ref,
    low_ref,
    row_ref,
    values_ref,
    offset_ref,
    sems,
    *,
    heads,
):
    waits = fetch(
        (
            (high_hbm, high_ref),
            (low_hbm, low_ref),
            (row_hbm, row_ref),
            (patches_hbm, patches_ref),
            (offset_hbm.at[0], offset_ref),
            (values_hbm.at[0], values_ref),
        ),
        sems,
    )
    spread = row_ref.shape[1]
    head_size = offset_ref.shape[1] * 2 // heads
    rows = high_ref.shape[0]
    pixels = rows * heads // spread
    scale = 1.0 / math.sqrt(head_size)
    for wait in waits[:4]:
        wait()
    patches = patches_ref[...]
    high, low = high_ref[...], low_ref[...]
    rows_of = iota((rows, LANES), 0) // pixels
    cols_of = iota((rows, LANES), 1) // heads
    scores = []
    for block in range(spread // LANES):
        here = rows_of == cols_of + block * (LANES // heads)
        part = dot(patches, jnp.where(here, high, jnp.zeros_like(high)))
        part = part + dot(patches, jnp.where(here, low, jnp.zeros_like(low)))
        scores.append((part + row_ref[:, block * LANES : (block + 1) * LANES]) * scale)
    top = functools.reduce(jnp.maximum, scores)
    step = heads
    while step < LANES:
        top = jnp.maximum(top, pltpu.roll(top, step, 1))
        step *= 2
    exps = [jnp.exp(s - top) for s in scores]
    total = functools.reduce(jnp.add, exps)
    step = heads
    while step < LANES:
        total = total + pltpu.roll(total, step, 1)
        step *= 2
    probs = jnp.concatenate([(e / total).astype(BF16) for e in exps], axis=1)
    probs_ref[...] = probs
    waits[4]()
    base = dot(probs, spread_offsets(offset_ref[...], heads, head_size, 0))
    waits[5]()
    half_ref[...] = mix_heads(
        probs, patches, values_ref, base, 0, heads // 4, heads, head_size, pixels
    )


def late_kernel(
    patches_hbm,
    probs_hbm,
    half_hbm,
    values_hbm,
    offset_hbm,
    out_w_hbm,
    pos_hbm,
    gain_hbm,
    tokens_ref,
    normed_ref,
    patches_ref,
    probs_ref,
    half_ref,
    values_ref,
    offset_ref,
    out_w_ref,
    pos_ref,
    gain_ref,
    sems,
    *,
    heads,
):
    waits = fetch(
        (
            (probs_hbm, probs_ref),
            (offset_hbm.at[1], offset_ref),
            (patches_hbm, patches_ref),
            (values_hbm.at[1], values_ref),
            (half_hbm, half_ref),
            (out_w_hbm, out_w_ref),
            (pos_hbm, pos_ref),
            (gain_hbm, gain_ref),
        ),
        sems,
    )
    spread = probs_ref.shape[1]
    head_size = out_w_ref.shape[0] // heads
    pixels = patches_ref.shape[1] * heads // spread
    waits[0]()
    waits[1]()
    probs = probs_ref[...]
    base = dot(probs, spread_offsets(offset_ref[...], heads, head_size, heads // 2))
    waits[2]()
    waits[3]()
    late = mix_heads(
        probs,
        patches_ref[...],
        values_ref,
        base,
        heads // 2,
        heads // 4,
        heads,
        head_size,
        pixels,
    )
    for wait in waits[4:]:
        wait()
    values = jnp.concatenate([half_ref[...], late], axis=1)
    tokens_zero = (dot(values, out_w_ref[...]) + pos_ref[...].astype(F32)).astype(BF16)
    tokens_ref[...] = tokens_zero
    full = tokens_zero.astype(F32)
    centred = full - jnp.mean(full, axis=-1, keepdims=True)
    variance = jnp.mean(centred * centred, axis=-1, keepdims=True)
    normed_ref[...] = (centred * lax.rsqrt(variance + 1e-05) * gain_ref[...]).astype(BF16)


def cost(gflops, mib, exps=0):
    return pl.CostEstimate(
        flops=int(gflops * 1e9), bytes_accessed=int(mib * (1 << 20)), transcendentals=exps
    )


VMEM = pl.BlockSpec(memory_space=pltpu.VMEM)
SMEM = pl.BlockSpec(memory_space=pltpu.SMEM)
HBM = pl.BlockSpec(memory_space=pltpu.HBM)


def like(*arrays):
    return [pltpu.VMEM(a.shape, a.dtype) for a in arrays]


def tables(var_order, embed_weight, var_embed, keys, value):
    var_count, pixels, width = embed_weight.shape
    heads = keys.shape[0]
    rows, spread, half = var_count * pixels, var_count * heads, width // 2
    return pl.pallas_call(
        table_kernel,
        out_shape=[
            jax.ShapeDtypeStruct((rows, LANES), BF16),
            jax.ShapeDtypeStruct((rows, LANES), BF16),
            jax.ShapeDtypeStruct((1, spread), F32),
            jax.ShapeDtypeStruct((2, rows, half), BF16),
            jax.ShapeDtypeStruct((2, var_count, half), BF16),
        ],
        in_specs=[SMEM] + [HBM] * 4,
        out_specs=[VMEM] * 5,
        scratch_shapes=like(embed_weight, var_embed, keys, value, embed_weight)
        + [pltpu.SemaphoreType.DMA((4,))],
        compiler_params=pltpu.CompilerParams(vmem_limit_bytes=WHOLE_VMEM),
        cost_estimate=cost(5, 7),
        name="tables",
    )(var_order, embed_weight, var_embed, keys, value)


def early_heads(patches, made, heads):
    high, low, row, values, offset = made
    tokens = patches.shape[0]
    half = values.shape[2]
    return pl.pallas_call(
        functools.partial(early_kernel, heads=heads),
        out_shape=[
            jax.ShapeDtypeStruct((tokens, row.shape[1]), BF16),
            jax.ShapeDtypeStruct((tokens, half), BF16),
        ],
        in_specs=[HBM] * 6,
        out_specs=[VMEM] * 2,
        scratch_shapes=like(patches, high, low, row)
        + [
            pltpu.VMEM(values.shape[1:], BF16),
            pltpu.VMEM(offset.shape[1:], BF16),
            pltpu.SemaphoreType.DMA((6,)),
        ],
        compiler_params=pltpu.CompilerParams(vmem_limit_bytes=WHOLE_VMEM),
        cost_estimate=cost(6, 6, 1 << 18),
        name="early_heads",
    )(patches, high, low, row, values, offset)


def late_heads(patches, probs, early, made, out_w, pos, gain, heads):
    values, offset = made[3:]
    tokens, width = pos.shape
    gain = gain.reshape(1, width)
    return pl.pallas_call(
        functools.partial(late_kernel, heads=heads),
        out_shape=[jax.ShapeDtypeStruct((tokens, width), BF16)] * 2,
        in_specs=[HBM] * 8,
        out_specs=[VMEM] * 2,
        scratch_shapes=like(patches, probs, early)
        + [pltpu.VMEM(values.shape[1:], BF16), pltpu.VMEM(offset.shape[1:], BF16)]
        + like(out_w, pos, gain)
        + [pltpu.SemaphoreType.DMA((8,))],
        compiler_params=pltpu.CompilerParams(vmem_limit_bytes=WHOLE_VMEM),
        cost_estimate=cost(6, 6),
        name="late_heads",
    )(patches, probs, early, values, offset, out_w, pos, gain)


def attend_kernel(*refs, spots):
    count = len(spots)
    weight_refs = refs[6 : 6 + count]
    mine_ref, other_ref, rows_s, query_s, key_s, value_s, weight_s, sems = refs[6 + count :]
    index, plane = lax.axis_index("space"), lax.axis_index("groups")
    side = index % 2
    moves = [(ref, rows_s.at[i]) for i, ref in enumerate(refs[:6])]
    for ref, (step, share) in zip(weight_refs, spots):
        rows = ref.shape[0]
        start = 0 if share is None else pl.multiple_of((plane + share) % 2 * rows, 32)
        moves.append((ref, weight_s.at[chip_at(index, step), pl.ds(start, rows), :]))
    for wait in fetch(moves, sems):
        wait()
    own_ref, sib_ref, left_own_ref, left_sib_ref, right_own_ref, right_sib_ref = (
        rows_s.at[i] for i in range(6)
    )
    tokens, width = own_ref.shape
    pairs = mine_ref.shape[0]
    cols = pairs * LANES
    weight = weight_s[...].reshape(3, cols, width)
    head_size = LANES // 2
    scale = 1.0 / math.sqrt(head_size)
    pieces = [
        (left_own_ref, side),
        (left_sib_ref, 1 - side),
        (own_ref, 2 + side),
        (sib_ref, 3 - side),
        (right_own_ref, 4 + side),
        (right_sib_ref, 5 - side),
    ]
    ones = jnp.ones((tokens, LANES), BF16)
    for number, (ref, place) in enumerate(pieces):
        rows = ref[...]
        key_s[place] = dot_t(weight[1], rows).astype(BF16)
        value = dot_t(rows, weight[2]).astype(BF16)
        for pair in range(pairs):
            value_s[place, pair] = jnp.concatenate(
                [value[:, pair * LANES : (pair + 1) * LANES], ones], axis=1
            )
        if number in (2, 3):
            query = (dot_t(rows, weight[0]).astype(BF16).astype(F32) * scale).astype(BF16)
            for pair in range(pairs):
                query_s[number - 2, pair] = query[:, pair * LANES : (pair + 1) * LANES]

    left_half = iota((tokens, LANES), 1) < head_size

    def attend(pair, carry):
        row = pl.multiple_of(pair * LANES, LANES)
        for number, (out_ref, sector) in enumerate(((mine_ref, side), (other_ref, 1 - side))):
            query = query_s[number, pair]
            halves = []
            for half in range(2):
                keep = left_half if half == 0 else jnp.logical_not(left_half)
                masked = jnp.where(keep, query, jnp.zeros_like(query))
                scores = [
                    dot(masked, key_s[sector + k, pl.ds(row, LANES), :]) for k in range(5)
                ]
                top = jnp.max(functools.reduce(jnp.maximum, scores), axis=-1, keepdims=True)
                acc = None
                for k in range(5):
                    part = dot(jnp.exp(scores[k] - top).astype(BF16), value_s[sector + k, pair])
                    acc = part if acc is None else acc + part
                halves.append(acc[:, :LANES] / acc[:, LANES:])
            out_ref[pair] = jnp.where(left_half, halves[0], halves[1]).astype(BF16)
        return carry

    lax.fori_loop(0, pairs, attend, 0)


def attend(pieces, weights):
    tokens, width = pieces[0].shape
    spots = tuple(spot for _, spot in weights)
    weights = [piece for piece, _ in weights]
    rows = weights[0].shape[0]
    blocks = 1 if len(weights) == 1 else len(RING)
    cols = rows * blocks // 3
    pairs = cols // LANES
    return pl.pallas_call(
        functools.partial(attend_kernel, spots=spots),
        out_shape=[jax.ShapeDtypeStruct((pairs, tokens, LANES), BF16)] * 2,
        in_specs=[HBM] * (6 + len(weights)),
        out_specs=[VMEM, VMEM],
        scratch_shapes=[
            pltpu.VMEM((6, tokens, width), BF16),
            pltpu.VMEM((2, pairs, tokens, LANES), BF16),
            pltpu.VMEM((6, cols, tokens), BF16),
            pltpu.VMEM((6, pairs, tokens, 2 * LANES), BF16),
            pltpu.VMEM((blocks, rows, width), BF16),
            pltpu.SemaphoreType.DMA((6 + len(weights),)),
        ],
        compiler_params=pltpu.CompilerParams(vmem_limit_bytes=PART_VMEM),
        cost_estimate=cost(10, 8, 5 << 20),
        name="attend",
    )(*pieces, *weights)


def finish_kernel(tokens_ref, mine_ref, other_ref, weight_ref, out_ref):
    side = lax.axis_index("space") % 2
    pairs, tokens, lanes = mine_ref.shape
    width = tokens_ref.shape[1]

    def part(ref, parity):
        rows = jnp.concatenate([ref[pair] for pair in range(pairs)], axis=1)
        return dot(rows, weight_ref[:, parity].reshape(pairs * lanes, width))

    update = part(mine_ref, side) + part(other_ref, 1 - side)
    out_ref[...] = (tokens_ref[...].astype(F32) + update).astype(BF16)


def finish(tokens_zero, mine, other, attn_out):
    tokens, width = tokens_zero.shape
    return pl.pallas_call(
        finish_kernel,
        out_shape=jax.ShapeDtypeStruct((tokens, width), BF16),
        in_specs=[VMEM] * 4,
        out_specs=VMEM,
        compiler_params=pltpu.CompilerParams(vmem_limit_bytes=PART_VMEM),
        cost_estimate=cost(1, 4),
        name="finish",
    )(tokens_zero, mine, other, attn_out.reshape(-1, 2, LANES // 2, width))


def sibling(value):
    length = lax.axis_size("space")
    return lax.ppermute(value, "space", [(i, i ^ 1) for i in range(length)])


def from_chip(value, by):
    length = lax.axis_size("space")
    return lax.ppermute(value, "space", [((i + 2 * by) % length, i) for i in range(length)])


def around(value, by):
    pairs = []
    for place, chip in enumerate(RING):
        for core in range(2):
            step = by if isinstance(by, int) else by[core]
            pairs.append((2 * chip + core, 2 * RING[(place + step) % len(RING)] + core))
    return lax.ppermute(value, "space", pairs)


def across(value):
    return lax.ppermute(value, "groups", [(0, 1), (1, 0)])


def together(*values):
    return lax.optimization_barrier(values)


def parity_block(qkv_weight, side, head_size):
    rows = qkv_weight.T
    low, middle, high = (rows[i * head_size : (i + 1) * head_size] for i in range(3))
    given = sibling(middle)
    return jnp.where(
        side == 0,
        jnp.concatenate([low, high, given], axis=0),
        jnp.concatenate([given, low, high], axis=0),
    )


def parity_weight(qkv_weight, side, head_size):
    rows = lax.all_gather(qkv_weight.T, "space", axis=0, tiled=True)
    blocks = rows.reshape(-1, 2, head_size, rows.shape[1])
    picked = lax.dynamic_index_in_dim(blocks, side, 1, keepdims=False)
    return [(picked.reshape(-1, rows.shape[1]), (None, None))]


def per_device(
    patches,
    var_order,
    embed_weight,
    var_embed,
    agg_keys,
    agg_value,
    agg_out,
    pos_embed,
    norm_gain,
    qkv_weight,
    attn_out,
):
    heads = agg_keys.shape[0]
    head_size = embed_weight.shape[2] // heads
    side = lax.axis_index("space") % 2
    ringed = (
        lax.axis_size("space") == 2 * len(RING)
        and lax.axis_size("groups") == 2
        and qkv_weight.shape[1] == 3 * head_size
    )
    if ringed:
        block = parity_block(qkv_weight, side, head_size)
        block, embed_weight = together(block, embed_weight)
        rows = block.shape[0] // 2
        share = lax.dynamic_slice_in_dim(block, lax.axis_index("groups") * rows, rows, 0)
        weights = [(block, (0, None))]
        up1, down1 = around(share, 1), around(share, -1)
    else:
        weights = parity_weight(qkv_weight, side, head_size)
    made = tables(var_order, embed_weight, var_embed, agg_keys, agg_value)
    if ringed:
        patches, up1, down1 = together(patches, up1, down1)
        up2, down2 = around(up1, 1), around(down1, -1)
        weights += [(up1, (-1, 0)), (down1, (1, 0))]
        near = across(up1), across(down1)
    probs, early = early_heads(patches, made, heads)
    if ringed:
        early, up2, down2 = together(early, up2, down2)
        up3, down3 = around(up2, 1), around(down2, -1)
        weights += [(up2, (-2, 0)), (down2, (2, 0))]
    tokens_zero, normed = late_heads(
        patches, probs, early, made, agg_out, pos_embed, norm_gain, heads
    )
    if ringed:
        normed, up3, down3, *near = together(normed, up3, down3, *near)
        weights += [(near[0], (-1, 1)), (near[1], (1, 1))]
        far = around(jnp.where(side == 0, up3, down3), (1, -1))
        next_near = across(up2), across(down2)
    left = from_chip(normed, -1)
    right = from_chip(normed, 1)
    if ringed:
        up3, down3, far, *next_near = together(up3, down3, far, *next_near)
        weights += [(next_near[0], (-2, 1)), (next_near[1], (2, 1))]
        weights += [(up3, (-3, 0)), (down3, (3, 0)), (far, (4, 0))]
        last = across(up3), across(down3), across(far)
        left, right, *last = together(left, right, *last)
        weights += [(last[0], (-3, 1)), (last[1], (3, 1)), (last[2], (4, 1))]
    pieces = (normed, sibling(normed), left, sibling(left), right, sibling(right))
    mine, other = attend(pieces, weights)
    return finish(tokens_zero, mine, sibling(other), attn_out)


def solution(mesh):
    in_specs = (
        P(("groups", "space"), None),
        P(),
        P(),
        P(),
        P(),
        P(),
        P(),
        P("space", None),
        P(),
        P(None, "space"),
        P(),
    )
    out_specs = P(("groups", "space"), None)
    return jax.shard_map(
        per_device, mesh=mesh, in_specs=in_specs, out_specs=out_specs, check_vma=False
    )
```

```python
import functools
import math

import jax
import jax.numpy as jnp
from jax import lax
from jax.experimental import pallas as pl
from jax.experimental.pallas import tpu as pltpu
from jax.sharding import PartitionSpec as P

BF16 = jnp.bfloat16
F32 = jnp.float32
LANES = 128
WHOLE_VMEM = 60 * 1024 * 1024
PART_VMEM = 24 * 1024 * 1024
RING = (0, 2, 4, 6, 7, 5, 3, 1)


def dot(left, right):
    return jnp.dot(left, right, preferred_element_type=F32)


def dot_t(left, right):
    return lax.dot_general(left, right, (((1,), (1,)), ((), ())), preferred_element_type=F32)


def chip_at(index, step):
    if step is None:
        return 0
    chip = index // 2
    here = jnp.where(chip % 2 == 0, chip // 2, 7 - chip // 2)
    at = (here + step + 8) % 8
    return jnp.where(at < 4, 2 * at, 2 * (7 - at) + 1)


def iota(shape, dim):
    return lax.broadcasted_iota(jnp.int32, shape, dim)


def fetch(pairs, sems):
    copies = [pltpu.make_async_copy(src, dst, sems.at[i]) for i, (src, dst) in enumerate(pairs)]
    for copy in copies:
        copy.start()
    return [copy.wait for copy in copies]


def spread_offsets(offset_half, heads, head_size, first):
    var_count, half = offset_half.shape
    spread = var_count * heads
    picks = (iota((spread, var_count), 0) // heads == iota((spread, var_count), 1)).astype(F32)
    rows = dot(picks.astype(BF16), offset_half).astype(BF16)
    mine = iota((spread, half), 0) % heads == iota((spread, half), 1) // head_size + first
    return jnp.where(mine, rows, jnp.zeros_like(rows))


def mix_heads(probs, patches, table_values, base, first, pairs, heads, head_size, pixels):
    tokens, spread = probs.shape
    group = math.gcd(spread, 256)
    row_g, col_g = iota((group, group), 0), iota((group, group), 1)
    same = row_g // heads == col_g // pixels
    left_half = iota((tokens, 2 * head_size), 1) < head_size
    values = []
    for pair in range(pairs):
        halves = []
        cols = slice(pair * 2 * head_size, (pair + 1) * 2 * head_size)
        for head in (first + 2 * pair, first + 2 * pair + 1):
            pick = jnp.where(same & (row_g % heads == head), 1.0, 0.0).astype(BF16)
            weights = jnp.concatenate(
                [
                    dot(probs[:, g * group : (g + 1) * group], pick).astype(BF16)
                    for g in range(spread // group)
                ],
                axis=1,
            )
            halves.append(dot(weights * patches, table_values[:, cols]))
        values.append((jnp.where(left_half, halves[0], halves[1]) + base[:, cols]).astype(BF16))
    return jnp.concatenate(values, axis=1)


def aggregate_kernel(
    order_ref,
    var_embed_hbm,
    keys_hbm,
    embed_hbm,
    patches_hbm,
    value_hbm,
    out_w_hbm,
    pos_hbm,
    gain_hbm,
    tokens_ref,
    normed_ref,
    var_embed_ref,
    keys_ref,
    embed_ref,
    patches_ref,
    value_ref,
    out_w_ref,
    pos_ref,
    gain_ref,
    table_ref,
    values_ref,
    sems,
):
    var_count, pixels, width = embed_ref.shape
    heads = keys_ref.shape[0]
    head_size = width // heads
    rows, spread = var_count * pixels, var_count * heads
    scale = 1.0 / math.sqrt(head_size)
    waits = fetch(
        (
            (var_embed_hbm, var_embed_ref),
            (keys_hbm, keys_ref),
            (embed_hbm, embed_ref),
            (patches_hbm, patches_ref),
            (value_hbm, value_ref),
            (out_w_hbm, out_w_ref),
            (pos_hbm, pos_ref),
            (gain_hbm, gain_ref),
        ),
        sems,
    )
    line = iota((var_count, var_count), 0)
    order = jnp.zeros((var_count, var_count), jnp.int32)
    for j in range(var_count):
        order = jnp.where(line == j, order_ref[j], order)
    select = (order == iota((var_count, var_count), 1)).astype(F32).astype(BF16)
    waits[0]()
    offsets = dot(select, var_embed_ref[...]).astype(BF16)
    waits[1]()
    repeat = (iota((LANES, heads), 0) % heads == iota((LANES, heads), 1)).astype(F32).astype(BF16)
    keys = dot(repeat, keys_ref[...]).astype(BF16)
    offset_keys = dot_t(offsets, keys)
    waits[2]()
    for j in range(var_count):
        table_ref[j] = embed_ref[order_ref[j]]
    table = table_ref[...].reshape(rows, width)
    table_keys = dot_t(table, keys)
    high = table_keys.astype(BF16)
    low = (table_keys - high.astype(F32)).astype(BF16)
    waits[3]()
    patches = patches_ref[...]
    rows_of = iota((rows, LANES), 0) // pixels
    cols_of = iota((rows, LANES), 1) // heads
    channel = iota((var_count, LANES), 1) // heads
    scores = []
    for block in range(spread // LANES):
        first = block * (LANES // heads)
        here = rows_of == cols_of + first
        row = jnp.sum(
            jnp.where(channel + first == iota((var_count, LANES), 0), offset_keys, 0.0),
            axis=0,
            keepdims=True,
        )
        part = dot(patches, jnp.where(here, high, jnp.zeros_like(high)))
        part = part + dot(patches, jnp.where(here, low, jnp.zeros_like(low)))
        scores.append((part + row) * scale)
    waits[4]()
    values_ref[...] = dot(table, value_ref[...]).astype(BF16)
    offset_values = dot(offsets, value_ref[...]).astype(BF16)
    top = functools.reduce(jnp.maximum, scores)
    step = heads
    while step < LANES:
        top = jnp.maximum(top, pltpu.roll(top, step, 1))
        step *= 2
    exps = [jnp.exp(s - top) for s in scores]
    total = functools.reduce(jnp.add, exps)
    step = heads
    while step < LANES:
        total = total + pltpu.roll(total, step, 1)
        step *= 2
    probs = jnp.concatenate([(e / total).astype(BF16) for e in exps], axis=1)
    base = dot(probs, spread_offsets(offset_values, heads, head_size, 0))
    values = mix_heads(
        probs, patches, values_ref, base, 0, heads // 2, heads, head_size, pixels
    )
    for wait in waits[5:]:
        wait()
    tokens_zero = (dot(values, out_w_ref[...]) + pos_ref[...].astype(F32)).astype(BF16)
    tokens_ref[...] = tokens_zero
    full = tokens_zero.astype(F32)
    centred = full - jnp.mean(full, axis=-1, keepdims=True)
    variance = jnp.mean(centred * centred, axis=-1, keepdims=True)
    normed_ref[...] = (centred * lax.rsqrt(variance + 1e-05) * gain_ref[...]).astype(BF16)


def cost(gflops, mib, exps=0):
    return pl.CostEstimate(
        flops=int(gflops * 1e9), bytes_accessed=int(mib * (1 << 20)), transcendentals=exps
    )


VMEM = pl.BlockSpec(memory_space=pltpu.VMEM)
SMEM = pl.BlockSpec(memory_space=pltpu.SMEM)
HBM = pl.BlockSpec(memory_space=pltpu.HBM)


def like(*arrays):
    return [pltpu.VMEM(a.shape, a.dtype) for a in arrays]


def aggregate(var_order, var_embed, keys, embed_weight, patches, value, out_w, pos, gain):
    tokens, width = pos.shape
    var_count, pixels, _ = embed_weight.shape
    arrays = (var_embed, keys, embed_weight, patches, value, out_w, pos, gain.reshape(1, width))
    return pl.pallas_call(
        aggregate_kernel,
        out_shape=[jax.ShapeDtypeStruct((tokens, width), BF16)] * 2,
        in_specs=[SMEM] + [HBM] * len(arrays),
        out_specs=[VMEM] * 2,
        scratch_shapes=like(*arrays)
        + like(embed_weight)
        + [pltpu.VMEM((var_count * pixels, width), BF16)]
        + [pltpu.SemaphoreType.DMA((len(arrays),))],
        compiler_params=pltpu.CompilerParams(vmem_limit_bytes=WHOLE_VMEM),
        cost_estimate=cost(16, 8, 1 << 18),
        name="aggregate",
    )(var_order, *arrays)


def attend_kernel(*refs, spots):
    count = len(spots)
    weight_refs = refs[6 : 6 + count]
    mine_ref, other_ref, rows_s, query_s, key_s, value_s, weight_s, sems = refs[6 + count :]
    index, plane = lax.axis_index("space"), lax.axis_index("groups")
    side = index % 2
    moves = [(ref, rows_s.at[i]) for i, ref in enumerate(refs[:6])]
    for ref, (step, share) in zip(weight_refs, spots):
        rows = ref.shape[0]
        if share == "ring":
            start = pl.multiple_of(plane * (rows // 2), 32)
            moves.append((ref, weight_s.at[chip_at(index, step), pl.ds(start, rows), :]))
        elif share == "swap":
            rows = rows // len(step)
            start = pl.multiple_of((1 - plane) * (2 * rows), 32)
            for i, one in enumerate(step):
                place = weight_s.at[chip_at(index, one), pl.ds(start, rows), :]
                moves.append((ref.at[pl.ds(i * rows, rows), :], place))
        else:
            moves.append((ref, weight_s.at[chip_at(index, step)]))
    for wait in fetch(moves, sems):
        wait()
    own_ref, sib_ref, left_own_ref, left_sib_ref, right_own_ref, right_sib_ref = (
        rows_s.at[i] for i in range(6)
    )
    tokens, width = own_ref.shape
    pairs = mine_ref.shape[0]
    cols = pairs * LANES
    weight = weight_s[...].reshape(3, cols, width)
    head_size = LANES // 2
    scale = 1.0 / math.sqrt(head_size)
    pieces = [
        (left_own_ref, side),
        (left_sib_ref, 1 - side),
        (own_ref, 2 + side),
        (sib_ref, 3 - side),
        (right_own_ref, 4 + side),
        (right_sib_ref, 5 - side),
    ]
    ones = jnp.ones((tokens, LANES), BF16)
    for number, (ref, place) in enumerate(pieces):
        rows = ref[...]
        key_s[place] = dot_t(weight[1], rows).astype(BF16)
        value = dot_t(rows, weight[2]).astype(BF16)
        for pair in range(pairs):
            value_s[place, pair] = jnp.concatenate(
                [value[:, pair * LANES : (pair + 1) * LANES], ones], axis=1
            )
        if number in (2, 3):
            query = (dot_t(rows, weight[0]).astype(BF16).astype(F32) * scale).astype(BF16)
            for pair in range(pairs):
                query_s[number - 2, pair] = query[:, pair * LANES : (pair + 1) * LANES]

    left_half = iota((tokens, LANES), 1) < head_size

    def attend(pair, carry):
        row = pl.multiple_of(pair * LANES, LANES)
        for number, (out_ref, sector) in enumerate(((mine_ref, side), (other_ref, 1 - side))):
            query = query_s[number, pair]
            halves = []
            for half in range(2):
                keep = left_half if half == 0 else jnp.logical_not(left_half)
                masked = jnp.where(keep, query, jnp.zeros_like(query))
                scores = [
                    dot(masked, key_s[sector + k, pl.ds(row, LANES), :]) for k in range(5)
                ]
                top = jnp.max(functools.reduce(jnp.maximum, scores), axis=-1, keepdims=True)
                acc = None
                for k in range(5):
                    part = dot(jnp.exp(scores[k] - top).astype(BF16), value_s[sector + k, pair])
                    acc = part if acc is None else acc + part
                halves.append(acc[:, :LANES] / acc[:, LANES:])
            out_ref[pair] = jnp.where(left_half, halves[0], halves[1]).astype(BF16)
        return carry

    lax.fori_loop(0, pairs, attend, 0)


def attend(pieces, weights):
    tokens, width = pieces[0].shape
    spots = tuple(spot for _, spot in weights)
    weights = [piece for piece, _ in weights]
    rows = weights[0].shape[0]
    blocks = 1 if len(weights) == 1 else len(RING)
    cols = rows * blocks // 3
    pairs = cols // LANES
    return pl.pallas_call(
        functools.partial(attend_kernel, spots=spots),
        out_shape=[jax.ShapeDtypeStruct((pairs, tokens, LANES), BF16)] * 2,
        in_specs=[HBM] * (6 + len(weights)),
        out_specs=[VMEM, VMEM],
        scratch_shapes=[
            pltpu.VMEM((6, tokens, width), BF16),
            pltpu.VMEM((2, pairs, tokens, LANES), BF16),
            pltpu.VMEM((6, cols, tokens), BF16),
            pltpu.VMEM((6, pairs, tokens, 2 * LANES), BF16),
            pltpu.VMEM((blocks, rows, width), BF16),
            pltpu.SemaphoreType.DMA((32,)),
        ],
        compiler_params=pltpu.CompilerParams(vmem_limit_bytes=PART_VMEM),
        cost_estimate=cost(10, 8, 5 << 20),
        name="attend",
    )(*pieces, *weights)


def finish_kernel(tokens_ref, mine_ref, other_ref, weight_ref, out_ref):
    side = lax.axis_index("space") % 2
    pairs, tokens, lanes = mine_ref.shape
    width = tokens_ref.shape[1]

    def part(ref, parity):
        rows = jnp.concatenate([ref[pair] for pair in range(pairs)], axis=1)
        return dot(rows, weight_ref[:, parity].reshape(pairs * lanes, width))

    update = part(mine_ref, side) + part(other_ref, 1 - side)
    out_ref[...] = (tokens_ref[...].astype(F32) + update).astype(BF16)


def finish(tokens_zero, mine, other, attn_out):
    tokens, width = tokens_zero.shape
    return pl.pallas_call(
        finish_kernel,
        out_shape=jax.ShapeDtypeStruct((tokens, width), BF16),
        in_specs=[VMEM] * 4,
        out_specs=VMEM,
        compiler_params=pltpu.CompilerParams(vmem_limit_bytes=PART_VMEM),
        cost_estimate=cost(1, 4),
        name="finish",
    )(tokens_zero, mine, other, attn_out.reshape(-1, 2, LANES // 2, width))


def sibling(value):
    length = lax.axis_size("space")
    return lax.ppermute(value, "space", [(i, i ^ 1) for i in range(length)])


def from_chip(value, by):
    length = lax.axis_size("space")
    return lax.ppermute(value, "space", [((i + 2 * by) % length, i) for i in range(length)])


def around(value, by):
    pairs = []
    for place, chip in enumerate(RING):
        for core in range(2):
            step = by if isinstance(by, int) else by[core]
            pairs.append((2 * chip + core, 2 * RING[(place + step) % len(RING)] + core))
    return lax.ppermute(value, "space", pairs)


def across(value):
    return lax.ppermute(value, "groups", [(0, 1), (1, 0)])


def together(*values):
    return lax.optimization_barrier(values)


def parity_block(qkv_weight, side, head_size):
    rows = qkv_weight.T
    low, middle, high = (rows[i * head_size : (i + 1) * head_size] for i in range(3))
    given = sibling(middle)
    return jnp.where(
        side == 0,
        jnp.concatenate([low, high, given], axis=0),
        jnp.concatenate([given, low, high], axis=0),
    )


def parity_weight(qkv_weight, side, head_size):
    rows = lax.all_gather(qkv_weight.T, "space", axis=0, tiled=True)
    blocks = rows.reshape(-1, 2, head_size, rows.shape[1])
    picked = lax.dynamic_index_in_dim(blocks, side, 1, keepdims=False)
    return [(picked.reshape(-1, rows.shape[1]), (None, None))]


def per_device(
    patches,
    var_order,
    embed_weight,
    var_embed,
    agg_keys,
    agg_value,
    agg_out,
    pos_embed,
    norm_gain,
    qkv_weight,
    attn_out,
):
    heads = agg_keys.shape[0]
    head_size = embed_weight.shape[2] // heads
    side = lax.axis_index("space") % 2
    ringed = (
        lax.axis_size("space") == 2 * len(RING)
        and lax.axis_size("groups") == 2
        and qkv_weight.shape[1] == 3 * head_size
    )
    if ringed:
        block = parity_block(qkv_weight, side, head_size)
        block, embed_weight = together(block, embed_weight)
        third = block.shape[0] // 3
        plane = lax.axis_index("groups")
        share = lax.dynamic_slice_in_dim(block, plane * third, 2 * third, 0)
        early = [around(share, step) for step in (1, -1, 2, -2)]
        weights = [(block, (0, None))]
    else:
        weights = parity_weight(qkv_weight, side, head_size)
    tokens_zero, normed = aggregate(
        var_order, var_embed, agg_keys, embed_weight, patches, agg_value, agg_out, pos_embed, norm_gain
    )
    if ringed:

        def swapped(blocks):
            parts = [lax.dynamic_slice_in_dim(b, plane * third, third, 0) for b in blocks]
            return across(jnp.concatenate(parts, axis=0))

        normed, *early = together(normed, *early)
        weights += [(b, (-step, "ring")) for b, step in zip(early, (1, -1, 2, -2))]
        swap = swapped(early)
        late = [around(early[2], 1), around(early[3], -1)]
        late.append(around(jnp.where(side == 0, early[2], early[3]), (2, -2)))
        left = from_chip(normed, -1)
        right = from_chip(normed, 1)
        swap, *late = together(swap, *late)
        weights += [(b, (-step, "ring")) for b, step in zip(late, (3, -3, 4))]
        weights.append((swap, ((-1, 1, -2, 2), "swap")))
        last = swapped(late)
        left, right, last = together(left, right, last)
        weights.append((last, ((-3, 3, -4), "swap")))
    else:
        left = from_chip(normed, -1)
        right = from_chip(normed, 1)
    pieces = (normed, sibling(normed), left, sibling(left), right, sibling(right))
    mine, other = attend(pieces, weights)
    return finish(tokens_zero, mine, sibling(other), attn_out)


def solution(mesh):
    in_specs = (
        P(("groups", "space"), None),
        P(),
        P(),
        P(),
        P(),
        P(),
        P(),
        P("space", None),
        P(),
        P(None, "space"),
        P(),
    )
    out_specs = P(("groups", "space"), None)
    return jax.shard_map(
        per_device, mesh=mesh, in_specs=in_specs, out_specs=out_specs, check_vma=False
    )
```

```python
import functools
import math

import jax
import jax.numpy as jnp
from jax import lax
from jax.experimental import pallas as pl
from jax.experimental.pallas import tpu as pltpu
from jax.sharding import PartitionSpec as P

BF16 = jnp.bfloat16
F32 = jnp.float32
LANES = 128
WHOLE_VMEM = 60 * 1024 * 1024
PART_VMEM = 24 * 1024 * 1024
RING = (0, 2, 4, 6, 7, 5, 3, 1)


def dot(left, right):
    return jnp.dot(left, right, preferred_element_type=F32)


def dot_t(left, right):
    return lax.dot_general(left, right, (((1,), (1,)), ((), ())), preferred_element_type=F32)


def chip_at(index, step):
    if step is None:
        return 0
    chip = index // 2
    here = jnp.where(chip % 2 == 0, chip // 2, 7 - chip // 2)
    at = (here + step + 8) % 8
    return jnp.where(at < 4, 2 * at, 2 * (7 - at) + 1)


def iota(shape, dim):
    return lax.broadcasted_iota(jnp.int32, shape, dim)


def fetch(pairs, sems):
    copies = [pltpu.make_async_copy(src, dst, sems.at[i]) for i, (src, dst) in enumerate(pairs)]
    for copy in copies:
        copy.start()
    return [copy.wait for copy in copies]


def spread_offsets(offset_half, heads, head_size, first):
    var_count, half = offset_half.shape
    spread = var_count * heads
    picks = (iota((spread, var_count), 0) // heads == iota((spread, var_count), 1)).astype(F32)
    rows = dot(picks.astype(BF16), offset_half).astype(BF16)
    mine = iota((spread, half), 0) % heads == iota((spread, half), 1) // head_size + first
    return jnp.where(mine, rows, jnp.zeros_like(rows))


def mix_heads(probs, patches, table_values, base, first, pairs, heads, head_size, pixels):
    tokens, spread = probs.shape
    group = math.gcd(spread, 256)
    row_g, col_g = iota((group, group), 0), iota((group, group), 1)
    same = row_g // heads == col_g // pixels
    left_half = iota((tokens, 2 * head_size), 1) < head_size
    values = []
    for pair in range(pairs):
        halves = []
        cols = slice(pair * 2 * head_size, (pair + 1) * 2 * head_size)
        for head in (first + 2 * pair, first + 2 * pair + 1):
            pick = jnp.where(same & (row_g % heads == head), 1.0, 0.0).astype(BF16)
            weights = jnp.concatenate(
                [
                    dot(probs[:, g * group : (g + 1) * group], pick).astype(BF16)
                    for g in range(spread // group)
                ],
                axis=1,
            )
            halves.append(dot(weights * patches, table_values[:, cols]))
        values.append((jnp.where(left_half, halves[0], halves[1]) + base[:, cols]).astype(BF16))
    return jnp.concatenate(values, axis=1)


def aggregate_kernel(
    order_ref,
    var_embed_hbm,
    keys_hbm,
    embed_hbm,
    patches_hbm,
    value_hbm,
    out_w_hbm,
    pos_hbm,
    gain_hbm,
    tokens_ref,
    normed_ref,
    var_embed_ref,
    keys_ref,
    embed_ref,
    patches_ref,
    value_ref,
    out_w_ref,
    pos_ref,
    gain_ref,
    table_ref,
    values_ref,
    sems,
):
    var_count, pixels, width = embed_ref.shape
    heads = keys_ref.shape[0]
    head_size = width // heads
    rows, spread = var_count * pixels, var_count * heads
    scale = 1.0 / math.sqrt(head_size)
    waits = fetch(
        (
            (var_embed_hbm, var_embed_ref),
            (keys_hbm, keys_ref),
            (embed_hbm, embed_ref),
            (patches_hbm, patches_ref),
            (value_hbm, value_ref),
            (out_w_hbm, out_w_ref),
            (pos_hbm, pos_ref),
            (gain_hbm, gain_ref),
        ),
        sems,
    )
    line = iota((var_count, var_count), 0)
    order = jnp.zeros((var_count, var_count), jnp.int32)
    for j in range(var_count):
        order = jnp.where(line == j, order_ref[j], order)
    select = (order == iota((var_count, var_count), 1)).astype(F32).astype(BF16)
    waits[0]()
    offsets = dot(select, var_embed_ref[...]).astype(BF16)
    waits[1]()
    repeat = (iota((LANES, heads), 0) % heads == iota((LANES, heads), 1)).astype(F32).astype(BF16)
    keys = dot(repeat, keys_ref[...]).astype(BF16)
    offset_keys = dot_t(offsets, keys)
    waits[2]()
    for j in range(var_count):
        table_ref[j] = embed_ref[order_ref[j]]
    table = table_ref[...].reshape(rows, width)
    table_keys = dot_t(table, keys)
    high = table_keys.astype(BF16)
    low = (table_keys - high.astype(F32)).astype(BF16)
    waits[3]()
    patches = patches_ref[...]
    rows_of = iota((rows, LANES), 0) // pixels
    cols_of = iota((rows, LANES), 1) // heads
    channel = iota((var_count, LANES), 1) // heads
    scores = []
    for block in range(spread // LANES):
        first = block * (LANES // heads)
        here = rows_of == cols_of + first
        row = jnp.sum(
            jnp.where(channel + first == iota((var_count, LANES), 0), offset_keys, 0.0),
            axis=0,
            keepdims=True,
        )
        part = dot(patches, jnp.where(here, high, jnp.zeros_like(high)))
        part = part + dot(patches, jnp.where(here, low, jnp.zeros_like(low)))
        scores.append((part + row) * scale)
    waits[4]()
    values_ref[...] = dot(table, value_ref[...]).astype(BF16)
    offset_values = dot(offsets, value_ref[...]).astype(BF16)
    top = functools.reduce(jnp.maximum, scores)
    step = heads
    while step < LANES:
        top = jnp.maximum(top, pltpu.roll(top, step, 1))
        step *= 2
    exps = [jnp.exp(s - top) for s in scores]
    total = functools.reduce(jnp.add, exps)
    step = heads
    while step < LANES:
        total = total + pltpu.roll(total, step, 1)
        step *= 2
    probs = jnp.concatenate([(e / total).astype(BF16) for e in exps], axis=1)
    base = dot(probs, spread_offsets(offset_values, heads, head_size, 0))
    values = mix_heads(
        probs, patches, values_ref, base, 0, heads // 2, heads, head_size, pixels
    )
    for wait in waits[5:]:
        wait()
    tokens_zero = (dot(values, out_w_ref[...]) + pos_ref[...].astype(F32)).astype(BF16)
    tokens_ref[...] = tokens_zero
    full = tokens_zero.astype(F32)
    centred = full - jnp.mean(full, axis=-1, keepdims=True)
    variance = jnp.mean(centred * centred, axis=-1, keepdims=True)
    normed_ref[...] = (centred * lax.rsqrt(variance + 1e-05) * gain_ref[...]).astype(BF16)


def cost(gflops, mib, exps=0):
    return pl.CostEstimate(
        flops=int(gflops * 1e9), bytes_accessed=int(mib * (1 << 20)), transcendentals=exps
    )


VMEM = pl.BlockSpec(memory_space=pltpu.VMEM)
SMEM = pl.BlockSpec(memory_space=pltpu.SMEM)
HBM = pl.BlockSpec(memory_space=pltpu.HBM)


def like(*arrays):
    return [pltpu.VMEM(a.shape, a.dtype) for a in arrays]


def aggregate(var_order, var_embed, keys, embed_weight, patches, value, out_w, pos, gain):
    tokens, width = pos.shape
    var_count, pixels, _ = embed_weight.shape
    arrays = (var_embed, keys, embed_weight, patches, value, out_w, pos, gain.reshape(1, width))
    return pl.pallas_call(
        aggregate_kernel,
        out_shape=[jax.ShapeDtypeStruct((tokens, width), BF16)] * 2,
        in_specs=[SMEM] + [HBM] * len(arrays),
        out_specs=[VMEM] * 2,
        scratch_shapes=like(*arrays)
        + like(embed_weight)
        + [pltpu.VMEM((var_count * pixels, width), BF16)]
        + [pltpu.SemaphoreType.DMA((len(arrays),))],
        compiler_params=pltpu.CompilerParams(vmem_limit_bytes=WHOLE_VMEM),
        cost_estimate=cost(16, 8, 1 << 18),
        name="aggregate",
    )(var_order, *arrays)


def attend_kernel(*refs, spots):
    count = len(spots)
    weight_refs = refs[6 : 6 + count]
    mine_ref, other_ref, rows_s, query_s, key_s, value_s, weight_s, sems = refs[6 + count :]
    index, plane = lax.axis_index("space"), lax.axis_index("groups")
    side = index % 2
    moves = [(ref, rows_s.at[i]) for i, ref in enumerate(refs[:6])]
    for ref, (step, share) in zip(weight_refs, spots):
        rows = ref.shape[0]
        if share == "ring":
            start = pl.multiple_of(plane * (rows // 2), 32)
            moves.append((ref, weight_s.at[chip_at(index, step), pl.ds(start, rows), :]))
        elif share == "swap":
            rows = rows // len(step)
            start = pl.multiple_of((1 - plane) * (2 * rows), 32)
            for i, one in enumerate(step):
                place = weight_s.at[chip_at(index, one), pl.ds(start, rows), :]
                moves.append((ref.at[pl.ds(i * rows, rows), :], place))
        else:
            moves.append((ref, weight_s.at[chip_at(index, step)]))
    for wait in fetch(moves, sems):
        wait()
    flip = index // 2 % 2 if spots[0][0] is not None else 0
    near, far = 4 - 4 * flip, 4 * flip
    _, tokens, width = rows_s.shape
    pairs = mine_ref.shape[0]
    cols = pairs * LANES
    weight = weight_s[...].reshape(3, cols, width)
    head_size = LANES // 2
    scale = 1.0 / math.sqrt(head_size)
    pieces = (2 + side, 3 - side, near + side, near + 1 - side, far + side, far + 1 - side)
    ones = jnp.ones((tokens, LANES), BF16)
    for number, place in enumerate(pieces):
        rows = rows_s[number]
        key_s[place] = dot_t(weight[1], rows).astype(BF16)
        value = dot_t(rows, weight[2]).astype(BF16)
        for pair in range(pairs):
            value_s[place, pair] = jnp.concatenate(
                [value[:, pair * LANES : (pair + 1) * LANES], ones], axis=1
            )
        if number < 2:
            query = (dot_t(rows, weight[0]).astype(BF16).astype(F32) * scale).astype(BF16)
            for pair in range(pairs):
                query_s[number, pair] = query[:, pair * LANES : (pair + 1) * LANES]

    left_half = iota((tokens, LANES), 1) < head_size

    def attend(pair, carry):
        row = pl.multiple_of(pair * LANES, LANES)
        for number, (out_ref, sector) in enumerate(((mine_ref, side), (other_ref, 1 - side))):
            query = query_s[number, pair]
            halves = []
            for half in range(2):
                keep = left_half if half == 0 else jnp.logical_not(left_half)
                masked = jnp.where(keep, query, jnp.zeros_like(query))
                scores = [
                    dot(masked, key_s[sector + k, pl.ds(row, LANES), :]) for k in range(5)
                ]
                top = jnp.max(functools.reduce(jnp.maximum, scores), axis=-1, keepdims=True)
                acc = None
                for k in range(5):
                    part = dot(jnp.exp(scores[k] - top).astype(BF16), value_s[sector + k, pair])
                    acc = part if acc is None else acc + part
                halves.append(acc[:, :LANES] / acc[:, LANES:])
            out_ref[pair] = jnp.where(left_half, halves[0], halves[1]).astype(BF16)
        return carry

    lax.fori_loop(0, pairs, attend, 0)


def attend(pieces, weights):
    tokens, width = pieces[0].shape
    spots = tuple(spot for _, spot in weights)
    weights = [piece for piece, _ in weights]
    rows = weights[0].shape[0]
    blocks = 1 if len(weights) == 1 else len(RING)
    cols = rows * blocks // 3
    pairs = cols // LANES
    return pl.pallas_call(
        functools.partial(attend_kernel, spots=spots),
        out_shape=[jax.ShapeDtypeStruct((pairs, tokens, LANES), BF16)] * 2,
        in_specs=[HBM] * (6 + len(weights)),
        out_specs=[VMEM, VMEM],
        scratch_shapes=[
            pltpu.VMEM((6, tokens, width), BF16),
            pltpu.VMEM((2, pairs, tokens, LANES), BF16),
            pltpu.VMEM((6, cols, tokens), BF16),
            pltpu.VMEM((6, pairs, tokens, 2 * LANES), BF16),
            pltpu.VMEM((blocks, rows, width), BF16),
            pltpu.SemaphoreType.DMA((32,)),
        ],
        compiler_params=pltpu.CompilerParams(vmem_limit_bytes=PART_VMEM),
        cost_estimate=cost(10, 8, 5 << 20),
        name="attend",
    )(*pieces, *weights)


def finish_kernel(tokens_ref, mine_ref, other_ref, weight_ref, out_ref):
    side = lax.axis_index("space") % 2
    pairs, tokens, lanes = mine_ref.shape
    width = tokens_ref.shape[1]

    def part(ref, parity):
        rows = jnp.concatenate([ref[pair] for pair in range(pairs)], axis=1)
        return dot(rows, weight_ref[:, parity].reshape(pairs * lanes, width))

    update = part(mine_ref, side) + part(other_ref, 1 - side)
    out_ref[...] = (tokens_ref[...].astype(F32) + update).astype(BF16)


def finish(tokens_zero, mine, other, attn_out):
    tokens, width = tokens_zero.shape
    return pl.pallas_call(
        finish_kernel,
        out_shape=jax.ShapeDtypeStruct((tokens, width), BF16),
        in_specs=[VMEM] * 4,
        out_specs=VMEM,
        compiler_params=pltpu.CompilerParams(vmem_limit_bytes=PART_VMEM),
        cost_estimate=cost(1, 4),
        name="finish",
    )(tokens_zero, mine, other, attn_out.reshape(-1, 2, LANES // 2, width))


def sibling(value):
    length = lax.axis_size("space")
    return lax.ppermute(value, "space", [(i, i ^ 1) for i in range(length)])


def from_chip(value, by):
    length = lax.axis_size("space")
    return lax.ppermute(value, "space", [((i + 2 * by) % length, i) for i in range(length)])


def around(value, by):
    pairs = []
    for place, chip in enumerate(RING):
        for core in range(2):
            step = by if isinstance(by, int) else by[core]
            pairs.append((2 * chip + core, 2 * RING[(place + step) % len(RING)] + core))
    return lax.ppermute(value, "space", pairs)


def beside(value):
    return lax.ppermute(value, "space", [(i, i ^ 2) for i in range(2 * len(RING))])


def onward(value):
    length = 2 * len(RING)
    pairs = [(i, (i + (4 if i & 2 == 0 else -4)) % length) for i in range(length)]
    return lax.ppermute(value, "space", pairs)


def across(value):
    return lax.ppermute(value, "groups", [(0, 1), (1, 0)])


def together(*values):
    return lax.optimization_barrier(values)


def parity_block(qkv_weight, side, head_size):
    rows = qkv_weight.T
    low, middle, high = (rows[i * head_size : (i + 1) * head_size] for i in range(3))
    given = sibling(middle)
    return jnp.where(
        side == 0,
        jnp.concatenate([low, high, given], axis=0),
        jnp.concatenate([given, low, high], axis=0),
    )


def parity_weight(qkv_weight, side, head_size):
    rows = lax.all_gather(qkv_weight.T, "space", axis=0, tiled=True)
    blocks = rows.reshape(-1, 2, head_size, rows.shape[1])
    picked = lax.dynamic_index_in_dim(blocks, side, 1, keepdims=False)
    return [(picked.reshape(-1, rows.shape[1]), (None, None))]


def per_device(
    patches,
    var_order,
    embed_weight,
    var_embed,
    agg_keys,
    agg_value,
    agg_out,
    pos_embed,
    norm_gain,
    qkv_weight,
    attn_out,
):
    heads = agg_keys.shape[0]
    head_size = embed_weight.shape[2] // heads
    side = lax.axis_index("space") % 2
    ringed = (
        lax.axis_size("space") == 2 * len(RING)
        and lax.axis_size("groups") == 2
        and qkv_weight.shape[1] == 3 * head_size
    )
    if ringed:
        block = parity_block(qkv_weight, side, head_size)
        block, embed_weight = together(block, embed_weight)
        third = block.shape[0] // 3
        plane = lax.axis_index("groups")
        share = lax.dynamic_slice_in_dim(block, plane * third, 2 * third, 0)
        early = [around(share, step) for step in (1, -1, 2, -2)]
        weights = [(block, (0, None))]
    else:
        weights = parity_weight(qkv_weight, side, head_size)
    tokens_zero, normed = aggregate(
        var_order, var_embed, agg_keys, embed_weight, patches, agg_value, agg_out, pos_embed, norm_gain
    )
    if ringed:

        def swapped(blocks):
            parts = [lax.dynamic_slice_in_dim(b, plane * third, third, 0) for b in blocks]
            return across(jnp.concatenate(parts, axis=0))

        normed, *early = together(normed, *early)
        weights += [(b, (-step, "ring")) for b, step in zip(early, (1, -1, 2, -2))]
        swap = swapped(early)
        late = [around(early[2], 1), around(early[3], -1)]
        late.append(around(jnp.where(side == 0, early[2], early[3]), (2, -2)))
        near = beside(normed)
        far, near_sib = onward(near), sibling(near)
        swap, near_sib, *late = together(swap, near_sib, *late)
        weights += [(b, (-step, "ring")) for b, step in zip(late, (3, -3, 4))]
        weights.append((swap, ((-1, 1, -2, 2), "swap")))
        last = swapped(late)
        far, last = together(far, last)
        weights.append((last, ((-3, 3, -4), "swap")))
    else:
        near, far = from_chip(normed, 1), from_chip(normed, -1)
        near_sib = sibling(near)
    pieces = (normed, sibling(normed), near, near_sib, far, sibling(far))
    mine, other = attend(pieces, weights)
    return finish(tokens_zero, mine, sibling(other), attn_out)


def solution(mesh):
    in_specs = (
        P(("groups", "space"), None),
        P(),
        P(),
        P(),
        P(),
        P(),
        P(),
        P("space", None),
        P(),
        P(None, "space"),
        P(),
    )
    out_specs = P(("groups", "space"), None)
    return jax.shard_map(
        per_device, mesh=mesh, in_specs=in_specs, out_specs=out_specs, check_vma=False
    )
```

```python
import functools
import math

import jax
import jax.numpy as jnp
from jax import lax
from jax.experimental import pallas as pl
from jax.experimental.pallas import tpu as pltpu
from jax.sharding import PartitionSpec as P

BF16 = jnp.bfloat16
F32 = jnp.float32
LANES = 128
WHOLE_VMEM = 60 * 1024 * 1024
PART_VMEM = 24 * 1024 * 1024
RING = (0, 2, 4, 6, 7, 5, 3, 1)


def dot(left, right):
    return jnp.dot(left, right, preferred_element_type=F32)


def dot_t(left, right):
    return lax.dot_general(left, right, (((1,), (1,)), ((), ())), preferred_element_type=F32)


def ring_place(index):
    chip = index // 2
    return jnp.where(chip % 2 == 0, chip // 2, 7 - chip // 2)


def chip_at(index, step):
    if step is None:
        return 0
    here = ring_place(index)
    if step == "beside":
        step = jnp.where(here % 2 == 0, -3, 3)
    elif step == "pair":
        step = jnp.where(here % 2 == 0, 3, -3)
    at = (here + step + 8) % 8
    return jnp.where(at < 4, 2 * at, 2 * (7 - at) + 1)


def iota(shape, dim):
    return lax.broadcasted_iota(jnp.int32, shape, dim)


def fetch(pairs, sems):
    copies = [pltpu.make_async_copy(src, dst, sems.at[i]) for i, (src, dst) in enumerate(pairs)]
    for copy in copies:
        copy.start()
    return [copy.wait for copy in copies]


def spread_offsets(offset_half, heads, head_size, first):
    var_count, half = offset_half.shape
    spread = var_count * heads
    picks = (iota((spread, var_count), 0) // heads == iota((spread, var_count), 1)).astype(F32)
    rows = dot(picks.astype(BF16), offset_half).astype(BF16)
    mine = iota((spread, half), 0) % heads == iota((spread, half), 1) // head_size + first
    return jnp.where(mine, rows, jnp.zeros_like(rows))


def mix_heads(probs, patches, table_values, base, first, pairs, heads, head_size, pixels):
    tokens, spread = probs.shape
    group = math.gcd(spread, 256)
    row_g, col_g = iota((group, group), 0), iota((group, group), 1)
    same = row_g // heads == col_g // pixels
    left_half = iota((tokens, 2 * head_size), 1) < head_size
    values = []
    for pair in range(pairs):
        halves = []
        cols = slice(pair * 2 * head_size, (pair + 1) * 2 * head_size)
        for head in (first + 2 * pair, first + 2 * pair + 1):
            pick = jnp.where(same & (row_g % heads == head), 1.0, 0.0).astype(BF16)
            weights = jnp.concatenate(
                [
                    dot(probs[:, g * group : (g + 1) * group], pick).astype(BF16)
                    for g in range(spread // group)
                ],
                axis=1,
            )
            halves.append(dot(weights * patches, table_values[:, cols]))
        values.append((jnp.where(left_half, halves[0], halves[1]) + base[:, cols]).astype(BF16))
    return jnp.concatenate(values, axis=1)


def aggregate_kernel(
    order_ref,
    var_embed_hbm,
    keys_hbm,
    embed_hbm,
    patches_hbm,
    value_hbm,
    out_w_hbm,
    pos_hbm,
    gain_hbm,
    tokens_ref,
    normed_ref,
    var_embed_ref,
    keys_ref,
    embed_ref,
    patches_ref,
    value_ref,
    out_w_ref,
    pos_ref,
    gain_ref,
    table_ref,
    values_ref,
    sems,
):
    var_count, pixels, width = embed_ref.shape
    heads = keys_ref.shape[0]
    head_size = width // heads
    rows, spread = var_count * pixels, var_count * heads
    scale = 1.0 / math.sqrt(head_size)
    waits = fetch(
        (
            (var_embed_hbm, var_embed_ref),
            (keys_hbm, keys_ref),
            (embed_hbm, embed_ref),
            (patches_hbm, patches_ref),
            (value_hbm, value_ref),
            (out_w_hbm, out_w_ref),
            (pos_hbm, pos_ref),
            (gain_hbm, gain_ref),
        ),
        sems,
    )
    line = iota((var_count, var_count), 0)
    order = jnp.zeros((var_count, var_count), jnp.int32)
    for j in range(var_count):
        order = jnp.where(line == j, order_ref[j], order)
    select = (order == iota((var_count, var_count), 1)).astype(F32).astype(BF16)
    waits[0]()
    offsets = dot(select, var_embed_ref[...]).astype(BF16)
    waits[1]()
    repeat = (iota((LANES, heads), 0) % heads == iota((LANES, heads), 1)).astype(F32).astype(BF16)
    keys = dot(repeat, keys_ref[...]).astype(BF16)
    offset_keys = dot_t(offsets, keys)
    waits[2]()
    for j in range(var_count):
        table_ref[j] = embed_ref[order_ref[j]]
    table = table_ref[...].reshape(rows, width)
    table_keys = dot_t(table, keys)
    high = table_keys.astype(BF16)
    low = (table_keys - high.astype(F32)).astype(BF16)
    waits[3]()
    patches = patches_ref[...]
    rows_of = iota((rows, LANES), 0) // pixels
    cols_of = iota((rows, LANES), 1) // heads
    channel = iota((var_count, LANES), 1) // heads
    scores = []
    for block in range(spread // LANES):
        first = block * (LANES // heads)
        here = rows_of == cols_of + first
        row = jnp.sum(
            jnp.where(channel + first == iota((var_count, LANES), 0), offset_keys, 0.0),
            axis=0,
            keepdims=True,
        )
        part = dot(patches, jnp.where(here, high, jnp.zeros_like(high)))
        part = part + dot(patches, jnp.where(here, low, jnp.zeros_like(low)))
        scores.append((part + row) * scale)
    waits[4]()
    values_ref[...] = dot(table, value_ref[...]).astype(BF16)
    offset_values = dot(offsets, value_ref[...]).astype(BF16)
    top = functools.reduce(jnp.maximum, scores)
    step = heads
    while step < LANES:
        top = jnp.maximum(top, pltpu.roll(top, step, 1))
        step *= 2
    exps = [jnp.exp(s - top) for s in scores]
    total = functools.reduce(jnp.add, exps)
    step = heads
    while step < LANES:
        total = total + pltpu.roll(total, step, 1)
        step *= 2
    probs = jnp.concatenate([(e / total).astype(BF16) for e in exps], axis=1)
    base = dot(probs, spread_offsets(offset_values, heads, head_size, 0))
    values = mix_heads(
        probs, patches, values_ref, base, 0, heads // 2, heads, head_size, pixels
    )
    for wait in waits[5:]:
        wait()
    tokens_zero = (dot(values, out_w_ref[...]) + pos_ref[...].astype(F32)).astype(BF16)
    tokens_ref[...] = tokens_zero
    full = tokens_zero.astype(F32)
    centred = full - jnp.mean(full, axis=-1, keepdims=True)
    variance = jnp.mean(centred * centred, axis=-1, keepdims=True)
    normed_ref[...] = (centred * lax.rsqrt(variance + 1e-05) * gain_ref[...]).astype(BF16)


def cost(gflops, mib, exps=0):
    return pl.CostEstimate(
        flops=int(gflops * 1e9), bytes_accessed=int(mib * (1 << 20)), transcendentals=exps
    )


VMEM = pl.BlockSpec(memory_space=pltpu.VMEM)
SMEM = pl.BlockSpec(memory_space=pltpu.SMEM)
HBM = pl.BlockSpec(memory_space=pltpu.HBM)


def like(*arrays):
    return [pltpu.VMEM(a.shape, a.dtype) for a in arrays]


def aggregate(var_order, var_embed, keys, embed_weight, patches, value, out_w, pos, gain):
    tokens, width = pos.shape
    var_count, pixels, _ = embed_weight.shape
    arrays = (var_embed, keys, embed_weight, patches, value, out_w, pos, gain.reshape(1, width))
    return pl.pallas_call(
        aggregate_kernel,
        out_shape=[jax.ShapeDtypeStruct((tokens, width), BF16)] * 2,
        in_specs=[SMEM] + [HBM] * len(arrays),
        out_specs=[VMEM] * 2,
        scratch_shapes=like(*arrays)
        + like(embed_weight)
        + [pltpu.VMEM((var_count * pixels, width), BF16)]
        + [pltpu.SemaphoreType.DMA((len(arrays),))],
        compiler_params=pltpu.CompilerParams(vmem_limit_bytes=WHOLE_VMEM),
        cost_estimate=cost(16, 8, 1 << 18),
        name="aggregate",
    )(var_order, *arrays)


def attend_kernel(*refs, spots):
    count = len(spots)
    weight_refs = refs[6 : 6 + count]
    mine_ref, other_ref, rows_s, query_s, key_s, value_s, weight_s, sems = refs[6 + count :]
    index, plane = lax.axis_index("space"), lax.axis_index("groups")
    side = index % 2
    moves = [(ref, rows_s.at[i]) for i, ref in enumerate(refs[:6])]
    for ref, (step, share) in zip(weight_refs, spots):
        rows = ref.shape[0]
        if share == "ring":
            start = pl.multiple_of(plane * (rows // 2), 32)
            moves.append((ref, weight_s.at[chip_at(index, step), pl.ds(start, rows), :]))
        elif share == "swap":
            rows = rows // len(step)
            start = pl.multiple_of((1 - plane) * (2 * rows), 32)
            for i, one in enumerate(step):
                place = weight_s.at[chip_at(index, one), pl.ds(start, rows), :]
                moves.append((ref.at[pl.ds(i * rows, rows), :], place))
        else:
            moves.append((ref, weight_s.at[chip_at(index, step)]))
    for wait in fetch(moves, sems):
        wait()
    flip = index // 2 % 2 if spots[0][0] is not None else 0
    near, far = 4 - 4 * flip, 4 * flip
    _, tokens, width = rows_s.shape
    pairs = mine_ref.shape[0]
    cols = pairs * LANES
    weight = weight_s[...].reshape(3, cols, width)
    head_size = LANES // 2
    scale = 1.0 / math.sqrt(head_size)
    pieces = (2 + side, 3 - side, near + side, near + 1 - side, far + side, far + 1 - side)
    ones = jnp.ones((tokens, LANES), BF16)
    for number, place in enumerate(pieces):
        rows = rows_s[number]
        key_s[place] = dot_t(weight[1], rows).astype(BF16)
        value = dot_t(rows, weight[2]).astype(BF16)
        for pair in range(pairs):
            value_s[place, pair] = jnp.concatenate(
                [value[:, pair * LANES : (pair + 1) * LANES], ones], axis=1
            )
        if number < 2:
            query = (dot_t(rows, weight[0]).astype(BF16).astype(F32) * scale).astype(BF16)
            for pair in range(pairs):
                query_s[number, pair] = query[:, pair * LANES : (pair + 1) * LANES]

    left_half = iota((tokens, LANES), 1) < head_size

    def attend(pair, carry):
        row = pl.multiple_of(pair * LANES, LANES)
        for number, (out_ref, sector) in enumerate(((mine_ref, side), (other_ref, 1 - side))):
            query = query_s[number, pair]
            halves = []
            for half in range(2):
                keep = left_half if half == 0 else jnp.logical_not(left_half)
                masked = jnp.where(keep, query, jnp.zeros_like(query))
                scores = [
                    dot(masked, key_s[sector + k, pl.ds(row, LANES), :]) for k in range(5)
                ]
                top = jnp.max(functools.reduce(jnp.maximum, scores), axis=-1, keepdims=True)
                acc = None
                for k in range(5):
                    part = dot(jnp.exp(scores[k] - top).astype(BF16), value_s[sector + k, pair])
                    acc = part if acc is None else acc + part
                halves.append(acc[:, :LANES] / acc[:, LANES:])
            out_ref[pair] = jnp.where(left_half, halves[0], halves[1]).astype(BF16)
        return carry

    lax.fori_loop(0, pairs, attend, 0)


def attend(pieces, weights):
    tokens, width = pieces[0].shape
    spots = tuple(spot for _, spot in weights)
    weights = [piece for piece, _ in weights]
    rows = weights[0].shape[0]
    blocks = 1 if len(weights) == 1 else len(RING)
    cols = rows * blocks // 3
    pairs = cols // LANES
    return pl.pallas_call(
        functools.partial(attend_kernel, spots=spots),
        out_shape=[jax.ShapeDtypeStruct((pairs, tokens, LANES), BF16)] * 2,
        in_specs=[HBM] * (6 + len(weights)),
        out_specs=[VMEM, VMEM],
        scratch_shapes=[
            pltpu.VMEM((6, tokens, width), BF16),
            pltpu.VMEM((2, pairs, tokens, LANES), BF16),
            pltpu.VMEM((6, cols, tokens), BF16),
            pltpu.VMEM((6, pairs, tokens, 2 * LANES), BF16),
            pltpu.VMEM((blocks, rows, width), BF16),
            pltpu.SemaphoreType.DMA((32,)),
        ],
        compiler_params=pltpu.CompilerParams(vmem_limit_bytes=PART_VMEM),
        cost_estimate=cost(10, 8, 5 << 20),
        name="attend",
    )(*pieces, *weights)


def finish_kernel(tokens_ref, mine_ref, other_ref, weight_ref, out_ref):
    side = lax.axis_index("space") % 2
    pairs, tokens, lanes = mine_ref.shape
    width = tokens_ref.shape[1]

    def part(ref, parity):
        rows = jnp.concatenate([ref[pair] for pair in range(pairs)], axis=1)
        return dot(rows, weight_ref[:, parity].reshape(pairs * lanes, width))

    update = part(mine_ref, side) + part(other_ref, 1 - side)
    out_ref[...] = (tokens_ref[...].astype(F32) + update).astype(BF16)


def finish(tokens_zero, mine, other, attn_out):
    tokens, width = tokens_zero.shape
    return pl.pallas_call(
        finish_kernel,
        out_shape=jax.ShapeDtypeStruct((tokens, width), BF16),
        in_specs=[VMEM] * 4,
        out_specs=VMEM,
        compiler_params=pltpu.CompilerParams(vmem_limit_bytes=PART_VMEM),
        cost_estimate=cost(1, 4),
        name="finish",
    )(tokens_zero, mine, other, attn_out.reshape(-1, 2, LANES // 2, width))


def sibling(value):
    length = lax.axis_size("space")
    return lax.ppermute(value, "space", [(i, i ^ 1) for i in range(length)])


def from_chip(value, by):
    length = lax.axis_size("space")
    return lax.ppermute(value, "space", [((i + 2 * by) % length, i) for i in range(length)])


def around(value, by):
    pairs = []
    for place, chip in enumerate(RING):
        for core in range(2):
            step = by if isinstance(by, int) else by[core]
            pairs.append((2 * chip + core, 2 * RING[(place + step) % len(RING)] + core))
    return lax.ppermute(value, "space", pairs)


def crossed(value, bits):
    return lax.ppermute(value, "space", [(i, i ^ bits) for i in range(2 * len(RING))])


def onward(value):
    length = 2 * len(RING)
    pairs = [(i, (i + (4 if i & 2 == 0 else -4)) % length) for i in range(length)]
    return lax.ppermute(value, "space", pairs)


def across(value):
    return lax.ppermute(value, "groups", [(0, 1), (1, 0)])


def together(*values):
    return lax.optimization_barrier(values)


def parity_block(qkv_weight, side, head_size):
    rows = qkv_weight.T
    low, middle, high = (rows[i * head_size : (i + 1) * head_size] for i in range(3))
    given = sibling(middle)
    return jnp.where(
        side == 0,
        jnp.concatenate([low, high, given], axis=0),
        jnp.concatenate([given, low, high], axis=0),
    )


def parity_weight(qkv_weight, side, head_size):
    rows = lax.all_gather(qkv_weight.T, "space", axis=0, tiled=True)
    blocks = rows.reshape(-1, 2, head_size, rows.shape[1])
    picked = lax.dynamic_index_in_dim(blocks, side, 1, keepdims=False)
    return [(picked.reshape(-1, rows.shape[1]), (None, None))]


def per_device(
    patches,
    var_order,
    embed_weight,
    var_embed,
    agg_keys,
    agg_value,
    agg_out,
    pos_embed,
    norm_gain,
    qkv_weight,
    attn_out,
):
    heads = agg_keys.shape[0]
    head_size = embed_weight.shape[2] // heads
    side = lax.axis_index("space") % 2
    ringed = (
        lax.axis_size("space") == 2 * len(RING)
        and lax.axis_size("groups") == 2
        and qkv_weight.shape[1] == 3 * head_size
    )
    if ringed:
        block = parity_block(qkv_weight, side, head_size)
        block, embed_weight = together(block, embed_weight)
        third = block.shape[0] // 3
        plane = lax.axis_index("groups")
        share = lax.dynamic_slice_in_dim(block, plane * third, 2 * third, 0)
        early = [around(share, step) for step in (1, -1, 2, -2)]
        weights = [(block, (0, None))]
    else:
        weights = parity_weight(qkv_weight, side, head_size)
    tokens_zero, normed = aggregate(
        var_order, var_embed, agg_keys, embed_weight, patches, agg_value, agg_out, pos_embed, norm_gain
    )
    if ringed:

        def swapped(blocks):
            parts = [lax.dynamic_slice_in_dim(b, plane * third, third, 0) for b in blocks]
            return across(jnp.concatenate(parts, axis=0))

        normed, *early = together(normed, *early)
        weights += [(b, (-step, "ring")) for b, step in zip(early, (1, -1, 2, -2))]
        swap = swapped(early)
        place = ring_place(lax.axis_index("space"))
        near = crossed(normed, 2)
        pair = crossed(jnp.where(place % 2 == 0, early[2], early[3]), 4)
        near, pair = together(near, pair)
        far, near_sib = onward(near), sibling(near)
        other = jnp.where(place % 4 < 2, early[3], early[2])
        late = [pair, crossed(other, 2), crossed(other, 6)]
        swap, near_sib, *late = together(swap, near_sib, *late)
        weights += [(b, (step, "ring")) for b, step in zip(late, ("pair", "beside", 4))]
        weights.append((swap, ((-1, 1, -2, 2), "swap")))
        last = swapped(late)
        far, last = together(far, last)
        weights.append((last, (("pair", "beside", 4), "swap")))
    else:
        near, far = from_chip(normed, 1), from_chip(normed, -1)
        near_sib = sibling(near)
    pieces = (normed, sibling(normed), near, near_sib, far, sibling(far))
    mine, other = attend(pieces, weights)
    return finish(tokens_zero, mine, sibling(other), attn_out)


def solution(mesh):
    in_specs = (
        P(("groups", "space"), None),
        P(),
        P(),
        P(),
        P(),
        P(),
        P(),
        P("space", None),
        P(),
        P(None, "space"),
        P(),
    )
    out_specs = P(("groups", "space"), None)
    return jax.shard_map(
        per_device, mesh=mesh, in_specs=in_specs, out_specs=out_specs, check_vma=False
    )
```

```python
import functools
import math

import jax
import jax.numpy as jnp
from jax import lax
from jax.experimental import pallas as pl
from jax.experimental.pallas import tpu as pltpu
from jax.sharding import PartitionSpec as P

BF16 = jnp.bfloat16
F32 = jnp.float32
LANES = 128
WHOLE_VMEM = 60 * 1024 * 1024
PART_VMEM = 24 * 1024 * 1024
RING = (0, 2, 4, 6, 7, 5, 3, 1)


def dot(left, right):
    return jnp.dot(left, right, preferred_element_type=F32)


def dot_t(left, right):
    return lax.dot_general(left, right, (((1,), (1,)), ((), ())), preferred_element_type=F32)


def ring_place(index):
    chip = index // 2
    return jnp.where(chip % 2 == 0, chip // 2, 7 - chip // 2)


def chip_at(index, step):
    if step is None:
        return 0
    here = ring_place(index)
    if step == "beside":
        step = jnp.where(here % 2 == 0, -3, 3)
    elif step == "pair":
        step = jnp.where(here % 2 == 0, 3, -3)
    at = (here + step + 8) % 8
    return jnp.where(at < 4, 2 * at, 2 * (7 - at) + 1)


def iota(shape, dim):
    return lax.broadcasted_iota(jnp.int32, shape, dim)


def fetch(pairs, sems):
    copies = [pltpu.make_async_copy(src, dst, sems.at[i]) for i, (src, dst) in enumerate(pairs)]
    for copy in copies:
        copy.start()
    return [copy.wait for copy in copies]


def spread_offsets(offset_half, heads, head_size, first):
    var_count, half = offset_half.shape
    spread = var_count * heads
    picks = (iota((spread, var_count), 0) // heads == iota((spread, var_count), 1)).astype(F32)
    rows = dot(picks.astype(BF16), offset_half).astype(BF16)
    mine = iota((spread, half), 0) % heads == iota((spread, half), 1) // head_size + first
    return jnp.where(mine, rows, jnp.zeros_like(rows))


def mix_heads(probs, patches, table_values, base, first, pairs, heads, head_size, pixels):
    tokens, spread = probs.shape
    group = math.gcd(spread, 256)
    row_g, col_g = iota((group, group), 0), iota((group, group), 1)
    same = row_g // heads == col_g // pixels
    left_half = iota((tokens, 2 * head_size), 1) < head_size
    values = []
    for pair in range(pairs):
        halves = []
        cols = slice(pair * 2 * head_size, (pair + 1) * 2 * head_size)
        for head in (first + 2 * pair, first + 2 * pair + 1):
            pick = jnp.where(same & (row_g % heads == head), 1.0, 0.0).astype(BF16)
            weights = jnp.concatenate(
                [
                    dot(probs[:, g * group : (g + 1) * group], pick).astype(BF16)
                    for g in range(spread // group)
                ],
                axis=1,
            )
            halves.append(dot(weights * patches, table_values[:, cols]))
        values.append((jnp.where(left_half, halves[0], halves[1]) + base[:, cols]).astype(BF16))
    return jnp.concatenate(values, axis=1)


def aggregate_kernel(
    order_ref,
    var_embed_hbm,
    keys_hbm,
    embed_hbm,
    patches_hbm,
    value_hbm,
    out_w_hbm,
    pos_hbm,
    gain_hbm,
    tokens_ref,
    normed_ref,
    var_embed_ref,
    keys_ref,
    embed_ref,
    patches_ref,
    value_ref,
    out_w_ref,
    pos_ref,
    gain_ref,
    table_ref,
    values_ref,
    sems,
):
    var_count, pixels, width = embed_ref.shape
    heads = keys_ref.shape[0]
    head_size = width // heads
    rows, spread = var_count * pixels, var_count * heads
    scale = 1.0 / math.sqrt(head_size)
    waits = fetch(
        (
            (var_embed_hbm, var_embed_ref),
            (keys_hbm, keys_ref),
            (embed_hbm, embed_ref),
            (patches_hbm, patches_ref),
            (value_hbm, value_ref),
            (out_w_hbm, out_w_ref),
            (pos_hbm, pos_ref),
            (gain_hbm, gain_ref),
        ),
        sems,
    )
    line = iota((var_count, var_count), 0)
    order = jnp.zeros((var_count, var_count), jnp.int32)
    for j in range(var_count):
        order = jnp.where(line == j, order_ref[j], order)
    select = (order == iota((var_count, var_count), 1)).astype(F32).astype(BF16)
    waits[0]()
    offsets = dot(select, var_embed_ref[...]).astype(BF16)
    waits[1]()
    repeat = (iota((LANES, heads), 0) % heads == iota((LANES, heads), 1)).astype(F32).astype(BF16)
    keys = dot(repeat, keys_ref[...]).astype(BF16)
    offset_keys = dot_t(offsets, keys)
    waits[2]()
    for j in range(var_count):
        table_ref[j] = embed_ref[order_ref[j]]
    table = table_ref[...].reshape(rows, width)
    table_keys = dot_t(table, keys)
    high = table_keys.astype(BF16)
    low = (table_keys - high.astype(F32)).astype(BF16)
    waits[3]()
    patches = patches_ref[...]
    rows_of = iota((rows, LANES), 0) // pixels
    cols_of = iota((rows, LANES), 1) // heads
    channel = iota((var_count, LANES), 1) // heads
    scores = []
    for block in range(spread // LANES):
        first = block * (LANES // heads)
        here = rows_of == cols_of + first
        row = jnp.sum(
            jnp.where(channel + first == iota((var_count, LANES), 0), offset_keys, 0.0),
            axis=0,
            keepdims=True,
        )
        part = dot(patches, jnp.where(here, high, jnp.zeros_like(high)))
        part = part + dot(patches, jnp.where(here, low, jnp.zeros_like(low)))
        scores.append((part + row) * scale)
    waits[4]()
    values_ref[...] = dot(table, value_ref[...]).astype(BF16)
    offset_values = dot(offsets, value_ref[...]).astype(BF16)
    top = functools.reduce(jnp.maximum, scores)
    step = heads
    while step < LANES:
        top = jnp.maximum(top, pltpu.roll(top, step, 1))
        step *= 2
    exps = [jnp.exp(s - top) for s in scores]
    total = functools.reduce(jnp.add, exps)
    step = heads
    while step < LANES:
        total = total + pltpu.roll(total, step, 1)
        step *= 2
    probs = jnp.concatenate([(e / total).astype(BF16) for e in exps], axis=1)
    base = dot(probs, spread_offsets(offset_values, heads, head_size, 0))
    values = mix_heads(
        probs, patches, values_ref, base, 0, heads // 2, heads, head_size, pixels
    )
    for wait in waits[5:]:
        wait()
    tokens_zero = (dot(values, out_w_ref[...]) + pos_ref[...].astype(F32)).astype(BF16)
    tokens_ref[...] = tokens_zero
    full = tokens_zero.astype(F32)
    centred = full - jnp.mean(full, axis=-1, keepdims=True)
    variance = jnp.mean(centred * centred, axis=-1, keepdims=True)
    normed_ref[...] = (centred * lax.rsqrt(variance + 1e-05) * gain_ref[...]).astype(BF16)


def cost(gflops, mib, exps=0):
    return pl.CostEstimate(
        flops=int(gflops * 1e9), bytes_accessed=int(mib * (1 << 20)), transcendentals=exps
    )


VMEM = pl.BlockSpec(memory_space=pltpu.VMEM)
SMEM = pl.BlockSpec(memory_space=pltpu.SMEM)
HBM = pl.BlockSpec(memory_space=pltpu.HBM)


def like(*arrays):
    return [pltpu.VMEM(a.shape, a.dtype) for a in arrays]


def aggregate(var_order, var_embed, keys, embed_weight, patches, value, out_w, pos, gain):
    tokens, width = pos.shape
    var_count, pixels, _ = embed_weight.shape
    arrays = (var_embed, keys, embed_weight, patches, value, out_w, pos, gain.reshape(1, width))
    return pl.pallas_call(
        aggregate_kernel,
        out_shape=[jax.ShapeDtypeStruct((tokens, width), BF16)] * 2,
        in_specs=[SMEM] + [HBM] * len(arrays),
        out_specs=[VMEM] * 2,
        scratch_shapes=like(*arrays)
        + like(embed_weight)
        + [pltpu.VMEM((var_count * pixels, width), BF16)]
        + [pltpu.SemaphoreType.DMA((len(arrays),))],
        compiler_params=pltpu.CompilerParams(vmem_limit_bytes=WHOLE_VMEM),
        cost_estimate=cost(16, 8, 1 << 18),
        name="aggregate",
    )(var_order, *arrays)


def attend_kernel(*refs, spots):
    count = len(spots)
    weight_refs = refs[6 : 6 + count]
    mine_ref, other_ref, rows_s, query_s, key_s, value_s, weight_s, sems = refs[6 + count :]
    index, plane = lax.axis_index("space"), lax.axis_index("groups")
    side = index % 2
    moves = [(ref, rows_s.at[i]) for i, ref in enumerate(refs[:6])]
    for ref, (step, share) in zip(weight_refs, spots):
        rows = ref.shape[0]
        if share == "ring":
            start = pl.multiple_of(plane * (rows // 2), 32)
            moves.append((ref, weight_s.at[chip_at(index, step), pl.ds(start, rows), :]))
        elif share == "swap":
            rows = rows // len(step)
            start = pl.multiple_of((1 - plane) * (2 * rows), 32)
            for i, one in enumerate(step):
                place = weight_s.at[chip_at(index, one), pl.ds(start, rows), :]
                moves.append((ref.at[pl.ds(i * rows, rows), :], place))
        else:
            moves.append((ref, weight_s.at[chip_at(index, step)]))
    for wait in fetch(moves, sems):
        wait()
    flip = index // 2 % 2 if spots[0][0] is not None else 0
    near, far = 4 - 4 * flip, 4 * flip
    _, tokens, width = rows_s.shape
    pairs = mine_ref.shape[0]
    cols = pairs * LANES
    weight = weight_s[...].reshape(3, cols, width)
    head_size = LANES // 2
    scale = 1.0 / math.sqrt(head_size)
    pieces = (2 + side, 3 - side, near + side, near + 1 - side, far + side, far + 1 - side)
    ones = jnp.ones((tokens, LANES), BF16)
    for number, place in enumerate(pieces):
        rows = rows_s[number]
        key_s[place] = dot_t(weight[1], rows).astype(BF16)
        value = dot_t(rows, weight[2]).astype(BF16)
        for pair in range(pairs):
            value_s[place, pair] = jnp.concatenate(
                [value[:, pair * LANES : (pair + 1) * LANES], ones], axis=1
            )
        if number < 2:
            query = (dot_t(rows, weight[0]).astype(BF16).astype(F32) * scale).astype(BF16)
            for pair in range(pairs):
                query_s[number, pair] = query[:, pair * LANES : (pair + 1) * LANES]

    left_half = iota((tokens, LANES), 1) < head_size

    def attend(pair, carry):
        row = pl.multiple_of(pair * LANES, LANES)
        for number, (out_ref, sector) in enumerate(((mine_ref, side), (other_ref, 1 - side))):
            query = query_s[number, pair]
            halves = []
            for half in range(2):
                keep = left_half if half == 0 else jnp.logical_not(left_half)
                masked = jnp.where(keep, query, jnp.zeros_like(query))
                scores = [
                    dot(masked, key_s[sector + k, pl.ds(row, LANES), :]) for k in range(5)
                ]
                top = jnp.max(functools.reduce(jnp.maximum, scores), axis=-1, keepdims=True)
                acc = None
                for k in range(5):
                    part = dot(jnp.exp(scores[k] - top).astype(BF16), value_s[sector + k, pair])
                    acc = part if acc is None else acc + part
                halves.append(acc[:, :LANES] / acc[:, LANES:])
            out_ref[pair] = jnp.where(left_half, halves[0], halves[1]).astype(BF16)
        return carry

    lax.fori_loop(0, pairs, attend, 0)


def attend(pieces, weights):
    tokens, width = pieces[0].shape
    spots = tuple(spot for _, spot in weights)
    weights = [piece for piece, _ in weights]
    rows = weights[0].shape[0]
    blocks = 1 if len(weights) == 1 else len(RING)
    cols = rows * blocks // 3
    pairs = cols // LANES
    return pl.pallas_call(
        functools.partial(attend_kernel, spots=spots),
        out_shape=[jax.ShapeDtypeStruct((pairs, tokens, LANES), BF16)] * 2,
        in_specs=[HBM] * (6 + len(weights)),
        out_specs=[VMEM, VMEM],
        scratch_shapes=[
            pltpu.VMEM((6, tokens, width), BF16),
            pltpu.VMEM((2, pairs, tokens, LANES), BF16),
            pltpu.VMEM((6, cols, tokens), BF16),
            pltpu.VMEM((6, pairs, tokens, 2 * LANES), BF16),
            pltpu.VMEM((blocks, rows, width), BF16),
            pltpu.SemaphoreType.DMA((32,)),
        ],
        compiler_params=pltpu.CompilerParams(vmem_limit_bytes=PART_VMEM),
        cost_estimate=cost(10, 8, 5 << 20),
        name="attend",
    )(*pieces, *weights)


def finish_kernel(tokens_ref, mine_ref, other_ref, weight_ref, out_ref):
    side = lax.axis_index("space") % 2
    pairs, tokens, lanes = mine_ref.shape
    width = tokens_ref.shape[1]

    def part(ref, parity):
        rows = jnp.concatenate([ref[pair] for pair in range(pairs)], axis=1)
        return dot(rows, weight_ref[:, parity].reshape(pairs * lanes, width))

    update = part(mine_ref, side) + part(other_ref, 1 - side)
    out_ref[...] = (tokens_ref[...].astype(F32) + update).astype(BF16)


def finish(tokens_zero, mine, other, attn_out):
    tokens, width = tokens_zero.shape
    return pl.pallas_call(
        finish_kernel,
        out_shape=jax.ShapeDtypeStruct((tokens, width), BF16),
        in_specs=[VMEM] * 4,
        out_specs=VMEM,
        compiler_params=pltpu.CompilerParams(vmem_limit_bytes=PART_VMEM),
        cost_estimate=cost(1, 4),
        name="finish",
    )(tokens_zero, mine, other, attn_out.reshape(-1, 2, LANES // 2, width))


def sibling(value):
    length = lax.axis_size("space")
    return lax.ppermute(value, "space", [(i, i ^ 1) for i in range(length)])


def from_chip(value, by):
    length = lax.axis_size("space")
    return lax.ppermute(value, "space", [((i + 2 * by) % length, i) for i in range(length)])


def around(value, by):
    pairs = []
    for place, chip in enumerate(RING):
        for core in range(2):
            step = by if isinstance(by, int) else by[core]
            pairs.append((2 * chip + core, 2 * RING[(place + step) % len(RING)] + core))
    return lax.ppermute(value, "space", pairs)


def crossed(value, bits):
    return lax.ppermute(value, "space", [(i, i ^ bits) for i in range(2 * len(RING))])


def onward(value):
    length = 2 * len(RING)
    pairs = [(i, (i + (4 if i & 2 == 0 else -4)) % length) for i in range(length)]
    return lax.ppermute(value, "space", pairs)


def across(value):
    return lax.ppermute(value, "groups", [(0, 1), (1, 0)])


def together(*values):
    return lax.optimization_barrier(values)


def parity_block(qkv_weight, side, head_size):
    rows = qkv_weight.T
    low, middle, high = (rows[i * head_size : (i + 1) * head_size] for i in range(3))
    given = sibling(middle)
    return jnp.where(
        side == 0,
        jnp.concatenate([low, high, given], axis=0),
        jnp.concatenate([given, low, high], axis=0),
    )


def parity_weight(qkv_weight, side, head_size):
    rows = lax.all_gather(qkv_weight.T, "space", axis=0, tiled=True)
    blocks = rows.reshape(-1, 2, head_size, rows.shape[1])
    picked = lax.dynamic_index_in_dim(blocks, side, 1, keepdims=False)
    return [(picked.reshape(-1, rows.shape[1]), (None, None))]


def per_device(
    patches,
    var_order,
    embed_weight,
    var_embed,
    agg_keys,
    agg_value,
    agg_out,
    pos_embed,
    norm_gain,
    qkv_weight,
    attn_out,
):
    heads = agg_keys.shape[0]
    head_size = embed_weight.shape[2] // heads
    side = lax.axis_index("space") % 2
    ringed = (
        lax.axis_size("space") == 2 * len(RING)
        and lax.axis_size("groups") == 2
        and qkv_weight.shape[1] == 3 * head_size
    )
    if ringed:
        block = parity_block(qkv_weight, side, head_size)
        block, embed_weight = together(block, embed_weight)
        third = block.shape[0] // 3
        plane = lax.axis_index("groups")
        share = lax.dynamic_slice_in_dim(block, plane * third, 2 * third, 0)
        early = [around(share, step) for step in (1, -1, 2, -2)]
        weights = [(block, (0, None))]
    else:
        weights = parity_weight(qkv_weight, side, head_size)
    tokens_zero, normed = aggregate(
        var_order, var_embed, agg_keys, embed_weight, patches, agg_value, agg_out, pos_embed, norm_gain
    )
    if ringed:

        def swapped(blocks):
            parts = [lax.dynamic_slice_in_dim(b, plane * third, third, 0) for b in blocks]
            return across(jnp.concatenate(parts, axis=0))

        normed, *early = together(normed, *early)
        weights += [(b, (-step, "ring")) for b, step in zip(early, (1, -1, 2, -2))]
        swap = swapped(early)
        place = ring_place(lax.axis_index("space"))
        near = crossed(normed, 2)
        pair = crossed(jnp.where(place % 2 == 0, early[2], early[3]), 4)
        low = place % 4 < 2
        opposite = crossed(jnp.where(low, early[2], early[3]), 8)
        near, pair, opposite = together(near, pair, opposite)
        far, near_sib = onward(near), sibling(near)
        beside = crossed(jnp.where(low, early[3], early[2]), 2)
        first = swapped([pair, opposite])
        swap, near_sib, beside = together(swap, near_sib, beside)
        second = swapped([beside])
        first, second, far = together(first, second, far)
        weights += [(pair, ("pair", "ring")), (opposite, (4, "ring")), (beside, ("beside", "ring"))]
        weights += [(swap, ((-1, 1, -2, 2), "swap"))]
        weights += [(first, (("pair", 4), "swap")), (second, (("beside",), "swap"))]
    else:
        near, far = from_chip(normed, 1), from_chip(normed, -1)
        near_sib = sibling(near)
    pieces = (normed, sibling(normed), near, near_sib, far, sibling(far))
    mine, other = attend(pieces, weights)
    return finish(tokens_zero, mine, sibling(other), attn_out)


def solution(mesh):
    in_specs = (
        P(("groups", "space"), None),
        P(),
        P(),
        P(),
        P(),
        P(),
        P(),
        P("space", None),
        P(),
        P(None, "space"),
        P(),
    )
    out_specs = P(("groups", "space"), None)
    return jax.shard_map(
        per_device, mesh=mesh, in_specs=in_specs, out_specs=out_specs, check_vma=False
    )
```

```python
import functools
import math

import jax
import jax.numpy as jnp
from jax import lax
from jax.experimental import pallas as pl
from jax.experimental.pallas import tpu as pltpu
from jax.sharding import PartitionSpec as P

BF16 = jnp.bfloat16
F32 = jnp.float32
LANES = 128
WHOLE_VMEM = 60 * 1024 * 1024
PART_VMEM = 24 * 1024 * 1024
RING = (0, 2, 4, 6, 7, 5, 3, 1)


def dot(left, right):
    return jnp.dot(left, right, preferred_element_type=F32)


def dot_t(left, right):
    return lax.dot_general(left, right, (((1,), (1,)), ((), ())), preferred_element_type=F32)


def ring_place(index):
    chip = index // 2
    return jnp.where(chip % 2 == 0, chip // 2, 7 - chip // 2)


def chip_at(index, step):
    if step is None:
        return 0
    here = ring_place(index)
    if step == "beside":
        step = jnp.where(here % 2 == 0, -3, 3)
    elif step == "pair":
        step = jnp.where(here % 2 == 0, 3, -3)
    at = (here + step + 8) % 8
    return jnp.where(at < 4, 2 * at, 2 * (7 - at) + 1)


def iota(shape, dim):
    return lax.broadcasted_iota(jnp.int32, shape, dim)


def over(x, n):
    return x >> (n.bit_length() - 1) if n & (n - 1) == 0 else x // n


def within(x, n):
    return x & (n - 1) if n & (n - 1) == 0 else x % n


def fetch(pairs, sems):
    copies = [pltpu.make_async_copy(src, dst, sems.at[i]) for i, (src, dst) in enumerate(pairs)]
    for copy in copies:
        copy.start()
    return [copy.wait for copy in copies]


def spread_offsets(offset_half, heads, head_size, first):
    var_count, half = offset_half.shape
    spread = var_count * heads
    picks = (over(iota((spread, var_count), 0), heads) == iota((spread, var_count), 1)).astype(F32)
    rows = dot(picks.astype(BF16), offset_half).astype(BF16)
    mine = within(iota((spread, half), 0), heads) == over(iota((spread, half), 1), head_size) + first
    return jnp.where(mine, rows, jnp.zeros_like(rows))


def mix_heads(probs, patches, table_values, base, first, pairs, heads, head_size, pixels):
    tokens, spread = probs.shape
    group = math.gcd(spread, 256)
    row_g, col_g = iota((group, group), 0), iota((group, group), 1)
    same = over(row_g, heads) == over(col_g, pixels)
    head_g = jnp.where(same, within(row_g, heads), -1)
    left_half = iota((tokens, 2 * head_size), 1) < head_size
    values = []
    for pair in range(pairs):
        halves = []
        cols = slice(pair * 2 * head_size, (pair + 1) * 2 * head_size)
        for head in (first + 2 * pair, first + 2 * pair + 1):
            pick = jnp.where(head_g == head, 1.0, 0.0).astype(BF16)
            weights = jnp.concatenate(
                [
                    dot(probs[:, g * group : (g + 1) * group], pick).astype(BF16)
                    for g in range(spread // group)
                ],
                axis=1,
            )
            halves.append(dot(weights * patches, table_values[:, cols]))
        values.append((jnp.where(left_half, halves[0], halves[1]) + base[:, cols]).astype(BF16))
    return jnp.concatenate(values, axis=1)


def aggregate_kernel(
    order_ref,
    var_embed_hbm,
    keys_hbm,
    embed_hbm,
    patches_hbm,
    value_hbm,
    out_w_hbm,
    pos_hbm,
    gain_hbm,
    tokens_ref,
    upper_ref,
    lower_ref,
    var_embed_ref,
    keys_ref,
    embed_ref,
    patches_ref,
    value_ref,
    out_w_ref,
    pos_ref,
    gain_ref,
    table_ref,
    values_ref,
    sems,
):
    var_count, pixels, width = embed_ref.shape
    heads = keys_ref.shape[0]
    head_size = width // heads
    rows, spread = var_count * pixels, var_count * heads
    scale = 1.0 / math.sqrt(head_size)
    waits = fetch(
        (
            (var_embed_hbm, var_embed_ref),
            (keys_hbm, keys_ref),
            (embed_hbm, embed_ref),
            (patches_hbm, patches_ref),
            (value_hbm, value_ref),
            (out_w_hbm, out_w_ref),
            (pos_hbm, pos_ref),
            (gain_hbm, gain_ref),
        ),
        sems,
    )
    line = iota((var_count, var_count), 0)
    order = jnp.zeros((var_count, var_count), jnp.int32)
    for j in range(var_count):
        order = jnp.where(line == j, order_ref[j], order)
    select = (order == iota((var_count, var_count), 1)).astype(F32).astype(BF16)
    waits[0]()
    offsets = dot(select, var_embed_ref[...]).astype(BF16)
    waits[1]()
    repeat = (within(iota((LANES, heads), 0), heads) == iota((LANES, heads), 1)).astype(F32).astype(BF16)
    keys = dot(repeat, keys_ref[...]).astype(BF16)
    offset_keys = dot_t(offsets, keys)
    waits[2]()
    for j in range(var_count):
        table_ref[j] = embed_ref[order_ref[j]]
    table = table_ref[...].reshape(rows, width)
    table_keys = dot_t(table, keys)
    high = table_keys.astype(BF16)
    low = (table_keys - high.astype(F32)).astype(BF16)
    waits[3]()
    patches = patches_ref[...]
    group = math.gcd(spread, 256)
    lines = group // heads * pixels
    same = over(iota((lines, LANES), 0), pixels)
    cols_of = over(iota((lines, LANES), 1), heads)
    channel = over(iota((var_count, LANES), 1), heads)
    scores = []
    for part in range(spread // group):
        here = slice(part * lines, (part + 1) * lines)
        highs, lows, shifts = [], [], []
        for block in range(group // LANES):
            first = block * (LANES // heads)
            match = same == cols_of + first
            highs.append(jnp.where(match, high[here], jnp.zeros_like(high[here])))
            lows.append(jnp.where(match, low[here], jnp.zeros_like(low[here])))
            match = channel + (first + part * (group // heads)) == iota((var_count, LANES), 0)
            shifts.append(jnp.sum(jnp.where(match, offset_keys, 0.0), axis=0, keepdims=True))
        total = dot(patches[:, here], jnp.concatenate(highs, axis=1))
        total = total + dot(patches[:, here], jnp.concatenate(lows, axis=1))
        for block, shift in enumerate(shifts):
            scores.append((total[:, block * LANES : (block + 1) * LANES] + shift) * scale)
    waits[4]()
    values_ref[...] = dot(table, value_ref[...]).astype(BF16)
    offset_values = dot(offsets, value_ref[...]).astype(BF16)
    top = functools.reduce(jnp.maximum, scores)
    step = heads
    while step < LANES:
        top = jnp.maximum(top, pltpu.roll(top, step, 1))
        step *= 2
    exps = [jnp.exp(s - top) for s in scores]
    total = functools.reduce(jnp.add, exps)
    step = heads
    while step < LANES:
        total = total + pltpu.roll(total, step, 1)
        step *= 2
    probs = jnp.concatenate([(e / total).astype(BF16) for e in exps], axis=1)
    base = dot(probs, spread_offsets(offset_values, heads, head_size, 0))
    values = mix_heads(
        probs, patches, values_ref, base, 0, heads // 2, heads, head_size, pixels
    )
    for wait in waits[5:]:
        wait()
    tokens_zero = (dot(values, out_w_ref[...]) + pos_ref[...].astype(F32)).astype(BF16)
    tokens_ref[...] = tokens_zero
    full = tokens_zero.astype(F32)
    centred = full - jnp.mean(full, axis=-1, keepdims=True)
    variance = jnp.mean(centred * centred, axis=-1, keepdims=True)
    normed = (centred * lax.rsqrt(variance + 1e-05) * gain_ref[...]).astype(BF16)
    half = upper_ref.shape[0]
    upper_ref[...] = normed[:half]
    lower_ref[...] = normed[half:]


def cost(gflops, mib, exps=0):
    return pl.CostEstimate(
        flops=int(gflops * 1e9), bytes_accessed=int(mib * (1 << 20)), transcendentals=exps
    )


VMEM = pl.BlockSpec(memory_space=pltpu.VMEM)
SMEM = pl.BlockSpec(memory_space=pltpu.SMEM)
HBM = pl.BlockSpec(memory_space=pltpu.HBM)


def like(*arrays):
    return [pltpu.VMEM(a.shape, a.dtype) for a in arrays]


def aggregate(var_order, var_embed, keys, embed_weight, patches, value, out_w, pos, gain):
    tokens, width = pos.shape
    var_count, pixels, _ = embed_weight.shape
    arrays = (var_embed, keys, embed_weight, patches, value, out_w, pos, gain.reshape(1, width))
    return pl.pallas_call(
        aggregate_kernel,
        out_shape=[
            jax.ShapeDtypeStruct((tokens, width), BF16),
            jax.ShapeDtypeStruct((tokens // 2, width), BF16),
            jax.ShapeDtypeStruct((tokens // 2, width), BF16),
        ],
        in_specs=[SMEM] + [HBM] * len(arrays),
        out_specs=[VMEM] * 3,
        scratch_shapes=like(*arrays)
        + like(embed_weight)
        + [pltpu.VMEM((var_count * pixels, width), BF16)]
        + [pltpu.SemaphoreType.DMA((len(arrays),))],
        compiler_params=pltpu.CompilerParams(vmem_limit_bytes=WHOLE_VMEM),
        cost_estimate=cost(16, 8, 1 << 18),
        name="aggregate",
    )(var_order, *arrays)


def attend_kernel(*refs, spots):
    count = len(spots)
    weight_refs = refs[12 : 12 + count]
    mine_ref, other_ref, rows_s, query_s, key_s, value_s, weight_s, sems = refs[12 + count :]
    index, plane = lax.axis_index("space"), lax.axis_index("groups")
    side = index % 2
    half = rows_s.shape[1] // 2
    moves = [
        (ref, rows_s.at[i // 2, pl.ds(i % 2 * half, half), :]) for i, ref in enumerate(refs[:12])
    ]
    for ref, (step, share) in zip(weight_refs, spots):
        rows = ref.shape[0]
        if share == "ring":
            start = pl.multiple_of(plane * (rows // 2), 32)
            moves.append((ref, weight_s.at[chip_at(index, step), pl.ds(start, rows), :]))
        elif share == "swap":
            rows = rows // len(step)
            start = pl.multiple_of((1 - plane) * (2 * rows), 32)
            for i, one in enumerate(step):
                place = weight_s.at[chip_at(index, one), pl.ds(start, rows), :]
                moves.append((ref.at[pl.ds(i * rows, rows), :], place))
        else:
            moves.append((ref, weight_s.at[chip_at(index, step)]))
    for wait in fetch(moves, sems):
        wait()
    flip = index // 2 % 2 if spots[0][0] is not None else 0
    near, far = 4 - 4 * flip, 4 * flip
    _, tokens, width = rows_s.shape
    pairs = mine_ref.shape[0]
    cols = pairs * LANES
    weight = weight_s[...].reshape(3, cols, width)
    head_size = LANES // 2
    scale = 1.0 / math.sqrt(head_size)
    pieces = (2 + side, 3 - side, near + side, near + 1 - side, far + side, far + 1 - side)
    ones = jnp.ones((tokens, LANES), BF16)
    for number, place in enumerate(pieces):
        rows = rows_s[number]
        key_s[place] = dot_t(weight[1], rows).astype(BF16)
        value = dot_t(rows, weight[2]).astype(BF16)
        for pair in range(pairs):
            value_s[place, pair] = jnp.concatenate(
                [value[:, pair * LANES : (pair + 1) * LANES], ones], axis=1
            )
        if number < 2:
            query = (dot_t(rows, weight[0]).astype(BF16).astype(F32) * scale).astype(BF16)
            for pair in range(pairs):
                query_s[number, pair] = query[:, pair * LANES : (pair + 1) * LANES]

    left_half = iota((tokens, LANES), 1) < head_size

    def attend(pair, carry):
        row = pl.multiple_of(pair * LANES, LANES)
        for number, (out_ref, sector) in enumerate(((mine_ref, side), (other_ref, 1 - side))):
            query = query_s[number, pair]
            halves = []
            for half in range(2):
                keep = left_half if half == 0 else jnp.logical_not(left_half)
                masked = jnp.where(keep, query, jnp.zeros_like(query))
                scores = [
                    dot(masked, key_s[sector + k, pl.ds(row, LANES), :]) for k in range(5)
                ]
                top = jnp.max(functools.reduce(jnp.maximum, scores), axis=-1, keepdims=True)
                acc = None
                for k in range(5):
                    part = dot(jnp.exp(scores[k] - top).astype(BF16), value_s[sector + k, pair])
                    acc = part if acc is None else acc + part
                halves.append(acc[:, :LANES] / acc[:, LANES:])
            out_ref[pair] = jnp.where(left_half, halves[0], halves[1]).astype(BF16)
        return carry

    lax.fori_loop(0, pairs, attend, 0, unroll=True)


def attend(pieces, weights):
    pieces = [half for piece in pieces for half in piece]
    tokens, width = 2 * pieces[0].shape[0], pieces[0].shape[1]
    spots = tuple(spot for _, spot in weights)
    weights = [piece for piece, _ in weights]
    rows = weights[0].shape[0]
    blocks = 1 if len(weights) == 1 else len(RING)
    cols = rows * blocks // 3
    pairs = cols // LANES
    return pl.pallas_call(
        functools.partial(attend_kernel, spots=spots),
        out_shape=[jax.ShapeDtypeStruct((pairs, tokens, LANES), BF16)] * 2,
        in_specs=[HBM] * (12 + len(weights)),
        out_specs=[VMEM, VMEM],
        scratch_shapes=[
            pltpu.VMEM((6, tokens, width), BF16),
            pltpu.VMEM((2, pairs, tokens, LANES), BF16),
            pltpu.VMEM((6, cols, tokens), BF16),
            pltpu.VMEM((6, pairs, tokens, 2 * LANES), BF16),
            pltpu.VMEM((blocks, rows, width), BF16),
            pltpu.SemaphoreType.DMA((32,)),
        ],
        compiler_params=pltpu.CompilerParams(vmem_limit_bytes=PART_VMEM),
        cost_estimate=cost(10, 8, 5 << 20),
        name="attend",
    )(*pieces, *weights)


def finish_kernel(tokens_ref, mine_ref, other_ref, weight_ref, out_ref):
    side = lax.axis_index("space") % 2
    pairs, tokens, lanes = mine_ref.shape
    width = tokens_ref.shape[1]

    def part(ref, parity):
        rows = jnp.concatenate([ref[pair] for pair in range(pairs)], axis=1)
        return dot(rows, weight_ref[:, parity].reshape(pairs * lanes, width))

    update = part(mine_ref, side) + part(other_ref, 1 - side)
    out_ref[...] = (tokens_ref[...].astype(F32) + update).astype(BF16)


def finish(tokens_zero, mine, other, attn_out):
    tokens, width = tokens_zero.shape
    return pl.pallas_call(
        finish_kernel,
        out_shape=jax.ShapeDtypeStruct((tokens, width), BF16),
        in_specs=[VMEM] * 4,
        out_specs=VMEM,
        compiler_params=pltpu.CompilerParams(vmem_limit_bytes=PART_VMEM),
        cost_estimate=cost(1, 4),
        name="finish",
    )(tokens_zero, mine, other, attn_out.reshape(-1, 2, LANES // 2, width))


def sibling(value):
    length = lax.axis_size("space")
    return lax.ppermute(value, "space", [(i, i ^ 1) for i in range(length)])


def from_chip(value, by):
    length = lax.axis_size("space")
    return lax.ppermute(value, "space", [((i + 2 * by) % length, i) for i in range(length)])


def around(value, by):
    pairs = []
    for place, chip in enumerate(RING):
        for core in range(2):
            step = by if isinstance(by, int) else by[core]
            pairs.append((2 * chip + core, 2 * RING[(place + step) % len(RING)] + core))
    return lax.ppermute(value, "space", pairs)


def crossed(value, bits):
    return lax.ppermute(value, "space", [(i, i ^ bits) for i in range(2 * len(RING))])


def onward(value):
    length = 2 * len(RING)
    pairs = [(i, (i + (4 if i & 2 == 0 else -4)) % length) for i in range(length)]
    return lax.ppermute(value, "space", pairs)


def across(value):
    return lax.ppermute(value, "groups", [(0, 1), (1, 0)])


def together(*values):
    return lax.optimization_barrier(values)


def parity_block(qkv_weight, side, head_size):
    rows = qkv_weight.T
    low, middle, high = (rows[i * head_size : (i + 1) * head_size] for i in range(3))
    given = sibling(middle)
    return jnp.where(
        side == 0,
        jnp.concatenate([low, high, given], axis=0),
        jnp.concatenate([given, low, high], axis=0),
    )


def parity_weight(qkv_weight, side, head_size):
    rows = lax.all_gather(qkv_weight.T, "space", axis=0, tiled=True)
    blocks = rows.reshape(-1, 2, head_size, rows.shape[1])
    picked = lax.dynamic_index_in_dim(blocks, side, 1, keepdims=False)
    return [(picked.reshape(-1, rows.shape[1]), (None, None))]


def per_device(
    patches,
    var_order,
    embed_weight,
    var_embed,
    agg_keys,
    agg_value,
    agg_out,
    pos_embed,
    norm_gain,
    qkv_weight,
    attn_out,
):
    heads = agg_keys.shape[0]
    head_size = embed_weight.shape[2] // heads
    side = lax.axis_index("space") % 2
    ringed = (
        lax.axis_size("space") == 2 * len(RING)
        and lax.axis_size("groups") == 2
        and qkv_weight.shape[1] == 3 * head_size
    )
    if ringed:
        block = parity_block(qkv_weight, side, head_size)
        block, embed_weight = together(block, embed_weight)
        third = block.shape[0] // 3
        plane = lax.axis_index("groups")
        share = lax.dynamic_slice_in_dim(block, plane * third, 2 * third, 0)
        early = [around(share, step) for step in (1, -1, 2, -2)]
        weights = [(block, (0, None))]
    else:
        weights = parity_weight(qkv_weight, side, head_size)
    tokens_zero, *normed = aggregate(
        var_order, var_embed, agg_keys, embed_weight, patches, agg_value, agg_out, pos_embed, norm_gain
    )
    if ringed:

        def swapped(blocks):
            parts = [lax.dynamic_slice_in_dim(b, plane * third, third, 0) for b in blocks]
            return across(jnp.concatenate(parts, axis=0))

        upper, lower, *early = together(*normed, *early)
        weights += [(b, (-step, "ring")) for b, step in zip(early, (1, -1, 2, -2))]
        place = ring_place(lax.axis_index("space"))
        low = place % 4 < 2
        near0, near1 = crossed(upper, 2), crossed(lower, 2)
        pair = crossed(jnp.where(place % 2 == 0, early[2], early[3]), 4)
        opposite = crossed(jnp.where(low, early[2], early[3]), 8)
        swap = swapped(early)
        far0, near_sib0 = onward(near0), sibling(near0)
        beside = crossed(jnp.where(low, early[3], early[2]), 2)
        near1, far0, pair, opposite, swap = together(near1, far0, pair, opposite, swap)
        far1, near_sib1 = onward(near1), sibling(near1)
        first = swapped([pair, opposite])
        near_sib1, beside = together(near_sib1, beside)
        second = swapped([beside])
        first, second, far1 = together(first, second, far1)
        weights += [(pair, ("pair", "ring")), (opposite, (4, "ring")), (beside, ("beside", "ring"))]
        weights += [(swap, ((-1, 1, -2, 2), "swap"))]
        weights += [(first, (("pair", 4), "swap")), (second, (("beside",), "swap"))]
        near, near_sib, far = (near0, near1), (near_sib0, near_sib1), (far0, far1)
        normed = (upper, lower)
    else:
        near = [from_chip(half, 1) for half in normed]
        far = [from_chip(half, -1) for half in normed]
        near_sib = [sibling(half) for half in near]
    sib = [sibling(half) for half in normed]
    far_sib = [sibling(half) for half in far]
    pieces = (normed, sib, near, near_sib, far, far_sib)
    mine, other = attend(pieces, weights)
    return finish(tokens_zero, mine, sibling(other), attn_out)


def solution(mesh):
    in_specs = (
        P(("groups", "space"), None),
        P(),
        P(),
        P(),
        P(),
        P(),
        P(),
        P("space", None),
        P(),
        P(None, "space"),
        P(),
    )
    out_specs = P(("groups", "space"), None)
    return jax.shard_map(
        per_device, mesh=mesh, in_specs=in_specs, out_specs=out_specs, check_vma=False
    )
```

```python
import functools
import math

import jax
import jax.numpy as jnp
from jax import lax
from jax.experimental import pallas as pl
from jax.experimental.pallas import tpu as pltpu
from jax.sharding import PartitionSpec as P

BF16 = jnp.bfloat16
F32 = jnp.float32
LANES = 128
WHOLE_VMEM = 60 * 1024 * 1024
PART_VMEM = 24 * 1024 * 1024
RING = (0, 2, 4, 6, 7, 5, 3, 1)


def dot(left, right):
    return jnp.dot(left, right, preferred_element_type=F32)


def dot_t(left, right):
    return lax.dot_general(left, right, (((1,), (1,)), ((), ())), preferred_element_type=F32)


def ring_place(index):
    chip = index // 2
    return jnp.where(chip % 2 == 0, chip // 2, 7 - chip // 2)


def chip_at(index, step):
    if step is None:
        return 0
    here = ring_place(index)
    if step == "beside":
        step = jnp.where(here % 2 == 0, -3, 3)
    elif step == "pair":
        step = jnp.where(here % 2 == 0, 3, -3)
    at = (here + step + 8) % 8
    return jnp.where(at < 4, 2 * at, 2 * (7 - at) + 1)


def iota(shape, dim):
    return lax.broadcasted_iota(jnp.int32, shape, dim)


def over(x, n):
    return x >> (n.bit_length() - 1) if n & (n - 1) == 0 else x // n


def within(x, n):
    return x & (n - 1) if n & (n - 1) == 0 else x % n


def fetch(pairs, sems):
    copies = [pltpu.make_async_copy(src, dst, sems.at[i]) for i, (src, dst) in enumerate(pairs)]
    for copy in copies:
        copy.start()
    return [copy.wait for copy in copies]


def spread_offsets(offset_half, heads, head_size, first):
    var_count, half = offset_half.shape
    spread = var_count * heads
    picks = (over(iota((spread, var_count), 0), heads) == iota((spread, var_count), 1)).astype(F32)
    rows = dot(picks.astype(BF16), offset_half).astype(BF16)
    mine = within(iota((spread, half), 0), heads) == over(iota((spread, half), 1), head_size) + first
    return jnp.where(mine, rows, jnp.zeros_like(rows))


def mix_heads(probs, patches, table_values, base, first, pairs, heads, head_size, pixels):
    tokens, spread = probs.shape
    group = math.gcd(spread, 256)
    row_g, col_g = iota((group, group), 0), iota((group, group), 1)
    same = over(row_g, heads) == over(col_g, pixels)
    head_g = jnp.where(same, within(row_g, heads), -1)
    left_half = iota((tokens, 2 * head_size), 1) < head_size
    values = []
    for pair in range(pairs):
        halves = []
        cols = slice(pair * 2 * head_size, (pair + 1) * 2 * head_size)
        for head in (first + 2 * pair, first + 2 * pair + 1):
            pick = jnp.where(head_g == head, 1.0, 0.0).astype(BF16)
            weights = jnp.concatenate(
                [
                    dot(probs[:, g * group : (g + 1) * group], pick).astype(BF16)
                    for g in range(spread // group)
                ],
                axis=1,
            )
            halves.append(dot(weights * patches, table_values[:, cols]))
        values.append((jnp.where(left_half, halves[0], halves[1]) + base[:, cols]).astype(BF16))
    return jnp.concatenate(values, axis=1)


def aggregate_kernel(
    order_ref,
    var_embed_hbm,
    keys_hbm,
    embed_hbm,
    patches_hbm,
    value_hbm,
    out_w_hbm,
    pos_hbm,
    gain_hbm,
    tokens_ref,
    normed_ref,
    var_embed_ref,
    keys_ref,
    embed_ref,
    patches_ref,
    value_ref,
    out_w_ref,
    pos_ref,
    gain_ref,
    table_ref,
    values_ref,
    sems,
):
    var_count, pixels, width = embed_ref.shape
    heads = keys_ref.shape[0]
    head_size = width // heads
    rows, spread = var_count * pixels, var_count * heads
    scale = 1.0 / math.sqrt(head_size)
    waits = fetch(
        (
            (var_embed_hbm, var_embed_ref),
            (keys_hbm, keys_ref),
            (embed_hbm, embed_ref),
            (patches_hbm, patches_ref),
            (value_hbm, value_ref),
            (out_w_hbm, out_w_ref),
            (pos_hbm, pos_ref),
            (gain_hbm, gain_ref),
        ),
        sems,
    )
    line = iota((var_count, var_count), 0)
    order = jnp.zeros((var_count, var_count), jnp.int32)
    for j in range(var_count):
        order = jnp.where(line == j, order_ref[j], order)
    select = (order == iota((var_count, var_count), 1)).astype(F32).astype(BF16)
    waits[0]()
    offsets = dot(select, var_embed_ref[...]).astype(BF16)
    waits[1]()
    repeat = (within(iota((LANES, heads), 0), heads) == iota((LANES, heads), 1)).astype(F32).astype(BF16)
    keys = dot(repeat, keys_ref[...]).astype(BF16)
    offset_keys = dot_t(offsets, keys)
    waits[2]()
    for j in range(var_count):
        table_ref[j] = embed_ref[order_ref[j]]
    table = table_ref[...].reshape(rows, width)
    table_keys = dot_t(table, keys)
    high = table_keys.astype(BF16)
    low = (table_keys - high.astype(F32)).astype(BF16)
    waits[3]()
    patches = patches_ref[...]
    group = math.gcd(spread, 256)
    lines = group // heads * pixels
    same = over(iota((lines, LANES), 0), pixels)
    cols_of = over(iota((lines, LANES), 1), heads)
    channel = over(iota((var_count, LANES), 1), heads)
    scores = []
    for part in range(spread // group):
        here = slice(part * lines, (part + 1) * lines)
        highs, lows, shifts = [], [], []
        for block in range(group // LANES):
            first = block * (LANES // heads)
            match = same == cols_of + first
            highs.append(jnp.where(match, high[here], jnp.zeros_like(high[here])))
            lows.append(jnp.where(match, low[here], jnp.zeros_like(low[here])))
            match = channel + (first + part * (group // heads)) == iota((var_count, LANES), 0)
            shifts.append(jnp.sum(jnp.where(match, offset_keys, 0.0), axis=0, keepdims=True))
        total = dot(patches[:, here], jnp.concatenate(highs, axis=1))
        total = total + dot(patches[:, here], jnp.concatenate(lows, axis=1))
        for block, shift in enumerate(shifts):
            scores.append((total[:, block * LANES : (block + 1) * LANES] + shift) * scale)
    waits[4]()
    values_ref[...] = dot(table, value_ref[...]).astype(BF16)
    offset_values = dot(offsets, value_ref[...]).astype(BF16)
    top = functools.reduce(jnp.maximum, scores)
    step = heads
    while step < LANES:
        top = jnp.maximum(top, pltpu.roll(top, step, 1))
        step *= 2
    exps = [jnp.exp(s - top) for s in scores]
    total = functools.reduce(jnp.add, exps)
    step = heads
    while step < LANES:
        total = total + pltpu.roll(total, step, 1)
        step *= 2
    probs = jnp.concatenate([(e / total).astype(BF16) for e in exps], axis=1)
    base = dot(probs, spread_offsets(offset_values, heads, head_size, 0))
    values = mix_heads(
        probs, patches, values_ref, base, 0, heads // 2, heads, head_size, pixels
    )
    for wait in waits[5:]:
        wait()
    tokens_zero = (dot(values, out_w_ref[...]) + pos_ref[...].astype(F32)).astype(BF16)
    tokens_ref[...] = tokens_zero
    full = tokens_zero.astype(F32)
    centred = full - jnp.mean(full, axis=-1, keepdims=True)
    variance = jnp.mean(centred * centred, axis=-1, keepdims=True)
    normed_ref[...] = (centred * lax.rsqrt(variance + 1e-05) * gain_ref[...]).astype(BF16)


def cost(gflops, mib, exps=0):
    return pl.CostEstimate(
        flops=int(gflops * 1e9), bytes_accessed=int(mib * (1 << 20)), transcendentals=exps
    )


VMEM = pl.BlockSpec(memory_space=pltpu.VMEM)
SMEM = pl.BlockSpec(memory_space=pltpu.SMEM)
HBM = pl.BlockSpec(memory_space=pltpu.HBM)


def like(*arrays):
    return [pltpu.VMEM(a.shape, a.dtype) for a in arrays]


def aggregate(var_order, var_embed, keys, embed_weight, patches, value, out_w, pos, gain):
    tokens, width = pos.shape
    var_count, pixels, _ = embed_weight.shape
    arrays = (var_embed, keys, embed_weight, patches, value, out_w, pos, gain.reshape(1, width))
    return pl.pallas_call(
        aggregate_kernel,
        out_shape=[jax.ShapeDtypeStruct((tokens, width), BF16)] * 2,
        in_specs=[SMEM] + [HBM] * len(arrays),
        out_specs=[VMEM] * 2,
        scratch_shapes=like(*arrays)
        + like(embed_weight)
        + [pltpu.VMEM((var_count * pixels, width), BF16)]
        + [pltpu.SemaphoreType.DMA((len(arrays),))],
        compiler_params=pltpu.CompilerParams(vmem_limit_bytes=WHOLE_VMEM),
        cost_estimate=cost(16, 8, 1 << 18),
        name="aggregate",
    )(var_order, *arrays)


def attend_kernel(*refs, spots):
    count = len(spots)
    weight_refs = refs[6 : 6 + count]
    mine_ref, other_ref, query_s, key_s, value_s, weight_s, sems = refs[6 + count :]
    index, plane = lax.axis_index("space"), lax.axis_index("groups")
    side = index % 2
    moves = []
    for ref, (step, share) in zip(weight_refs, spots):
        rows = ref.shape[0]
        if share == "ring":
            start = pl.multiple_of(plane * (rows // 2), 32)
            moves.append((ref, weight_s.at[chip_at(index, step), pl.ds(start, rows), :]))
        elif share == "swap":
            rows = rows // len(step)
            start = pl.multiple_of((1 - plane) * (2 * rows), 32)
            for i, one in enumerate(step):
                place = weight_s.at[chip_at(index, one), pl.ds(start, rows), :]
                moves.append((ref.at[pl.ds(i * rows, rows), :], place))
        else:
            moves.append((ref, weight_s.at[chip_at(index, step)]))
    for wait in fetch(moves, sems):
        wait()
    flip = index // 2 % 2 if spots[0][0] is not None else 0
    near, far = 4 - 4 * flip, 4 * flip
    tokens, width = refs[0].shape
    pairs = mine_ref.shape[0]
    cols = pairs * LANES
    weight = weight_s[...].reshape(3 * cols, width)
    head_size = LANES // 2
    scale = 1.0 / math.sqrt(head_size)
    pieces = (2 + side, 3 - side, near + side, near + 1 - side, far + side, far + 1 - side)
    ones = jnp.ones((tokens, LANES), BF16)
    for number, place in enumerate(pieces):
        rows = refs[number][...]
        both = dot_t(rows, weight[cols:]).astype(BF16)
        spot = pl.ds(pl.multiple_of(place * tokens, tokens), tokens)
        for pair in range(pairs):
            lanes = slice(pair * LANES, (pair + 1) * LANES)
            key_s[pair, spot, :] = both[:, :cols][:, lanes]
            value_s[pair, spot, :] = jnp.concatenate([both[:, cols:][:, lanes], ones], axis=1)
        if number < 2:
            query = (dot_t(rows, weight[:cols]).astype(BF16).astype(F32) * scale).astype(BF16)
            for pair in range(pairs):
                query_s[number, pair] = query[:, pair * LANES : (pair + 1) * LANES]

    left_half = iota((tokens, LANES), 1) < head_size

    def attend(pair, carry):
        for number, (out_ref, sector) in enumerate(((mine_ref, side), (other_ref, 1 - side))):
            query = query_s[number, pair]
            halves = []
            for half in range(2):
                keep = left_half if half == 0 else jnp.logical_not(left_half)
                masked = jnp.where(keep, query, jnp.zeros_like(query))
                start = pl.multiple_of(sector * tokens, tokens)
                scores = [
                    dot_t(masked, key_s[pair, pl.ds(start + k * tokens, tokens), :])
                    for k in range(5)
                ]
                top = jnp.max(functools.reduce(jnp.maximum, scores), axis=-1, keepdims=True)
                probs = jnp.concatenate([jnp.exp(s - top).astype(BF16) for s in scores], axis=1)
                acc = dot(probs, value_s[pair, pl.ds(start, 5 * tokens), :])
                halves.append(acc[:, :LANES] / acc[:, LANES:])
            out_ref[pair] = jnp.where(left_half, halves[0], halves[1]).astype(BF16)
        return carry

    lax.fori_loop(0, pairs, attend, 0, unroll=True)


def attend(pieces, weights):
    tokens, width = pieces[0].shape
    spots = tuple(spot for _, spot in weights)
    weights = [piece for piece, _ in weights]
    rows = weights[0].shape[0]
    blocks = 1 if len(weights) == 1 else len(RING)
    cols = rows * blocks // 3
    pairs = cols // LANES
    return pl.pallas_call(
        functools.partial(attend_kernel, spots=spots),
        out_shape=[jax.ShapeDtypeStruct((pairs, tokens, LANES), BF16)] * 2,
        in_specs=[VMEM] * 6 + [HBM] * len(weights),
        out_specs=[VMEM, VMEM],
        scratch_shapes=[
            pltpu.VMEM((2, pairs, tokens, LANES), BF16),
            pltpu.VMEM((pairs, 6 * tokens, LANES), BF16),
            pltpu.VMEM((pairs, 6 * tokens, 2 * LANES), BF16),
            pltpu.VMEM((blocks, rows, width), BF16),
            pltpu.SemaphoreType.DMA((32,)),
        ],
        compiler_params=pltpu.CompilerParams(vmem_limit_bytes=PART_VMEM),
        cost_estimate=cost(10, 8, 5 << 20),
        name="attend",
    )(*pieces, *weights)


def finish_kernel(tokens_ref, mine_ref, other_ref, weight_ref, out_ref):
    side = lax.axis_index("space") % 2
    pairs, tokens, lanes = mine_ref.shape
    width = tokens_ref.shape[1]

    def part(ref, parity):
        rows = jnp.concatenate([ref[pair] for pair in range(pairs)], axis=1)
        return dot(rows, weight_ref[:, parity].reshape(pairs * lanes, width))

    update = part(mine_ref, side) + part(other_ref, 1 - side)
    out_ref[...] = (tokens_ref[...].astype(F32) + update).astype(BF16)


def finish(tokens_zero, mine, other, attn_out):
    tokens, width = tokens_zero.shape
    return pl.pallas_call(
        finish_kernel,
        out_shape=jax.ShapeDtypeStruct((tokens, width), BF16),
        in_specs=[VMEM] * 4,
        out_specs=VMEM,
        compiler_params=pltpu.CompilerParams(vmem_limit_bytes=PART_VMEM),
        cost_estimate=cost(1, 4),
        name="finish",
    )(tokens_zero, mine, other, attn_out.reshape(-1, 2, LANES // 2, width))


def sibling(value):
    length = lax.axis_size("space")
    return lax.ppermute(value, "space", [(i, i ^ 1) for i in range(length)])


def from_chip(value, by):
    length = lax.axis_size("space")
    return lax.ppermute(value, "space", [((i + 2 * by) % length, i) for i in range(length)])


def around(value, by):
    pairs = []
    for place, chip in enumerate(RING):
        for core in range(2):
            step = by if isinstance(by, int) else by[core]
            pairs.append((2 * chip + core, 2 * RING[(place + step) % len(RING)] + core))
    return lax.ppermute(value, "space", pairs)


def crossed(value, bits):
    return lax.ppermute(value, "space", [(i, i ^ bits) for i in range(2 * len(RING))])


def onward(value):
    length = 2 * len(RING)
    pairs = [(i, (i + (4 if i & 2 == 0 else -4)) % length) for i in range(length)]
    return lax.ppermute(value, "space", pairs)


def across(value):
    return lax.ppermute(value, "groups", [(0, 1), (1, 0)])


def together(*values):
    return lax.optimization_barrier(values)


def parity_block(qkv_weight, side, head_size):
    rows = qkv_weight.T
    low, middle, high = (rows[i * head_size : (i + 1) * head_size] for i in range(3))
    given = sibling(middle)
    return jnp.where(
        side == 0,
        jnp.concatenate([low, high, given], axis=0),
        jnp.concatenate([given, low, high], axis=0),
    )


def parity_weight(qkv_weight, side, head_size):
    rows = lax.all_gather(qkv_weight.T, "space", axis=0, tiled=True)
    blocks = rows.reshape(-1, 2, head_size, rows.shape[1])
    picked = lax.dynamic_index_in_dim(blocks, side, 1, keepdims=False)
    return [(picked.reshape(-1, rows.shape[1]), (None, None))]


def per_device(
    patches,
    var_order,
    embed_weight,
    var_embed,
    agg_keys,
    agg_value,
    agg_out,
    pos_embed,
    norm_gain,
    qkv_weight,
    attn_out,
):
    heads = agg_keys.shape[0]
    head_size = embed_weight.shape[2] // heads
    side = lax.axis_index("space") % 2
    ringed = (
        lax.axis_size("space") == 2 * len(RING)
        and lax.axis_size("groups") == 2
        and qkv_weight.shape[1] == 3 * head_size
    )
    if ringed:
        block = parity_block(qkv_weight, side, head_size)
        block, embed_weight = together(block, embed_weight)
        third = block.shape[0] // 3
        plane = lax.axis_index("groups")
        share = lax.dynamic_slice_in_dim(block, plane * third, 2 * third, 0)
        early = [around(share, step) for step in (1, -1, 2, -2)]
        weights = [(block, (0, None))]
    else:
        weights = parity_weight(qkv_weight, side, head_size)
    tokens_zero, normed = aggregate(
        var_order, var_embed, agg_keys, embed_weight, patches, agg_value, agg_out, pos_embed, norm_gain
    )
    if ringed:

        def swapped(blocks):
            parts = [lax.dynamic_slice_in_dim(b, plane * third, third, 0) for b in blocks]
            return across(jnp.concatenate(parts, axis=0))

        normed, *early = together(normed, *early)
        weights += [(b, (-step, "ring")) for b, step in zip(early, (1, -1, 2, -2))]
        swap = swapped(early)
        place = ring_place(lax.axis_index("space"))
        near = crossed(normed, 2)
        pair = crossed(jnp.where(place % 2 == 0, early[2], early[3]), 4)
        low = place % 4 < 2
        opposite = crossed(jnp.where(low, early[2], early[3]), 8)
        near, pair, opposite, swap = together(near, pair, opposite, swap)
        far, near_sib = onward(near), sibling(near)
        beside = crossed(jnp.where(low, early[3], early[2]), 2)
        first = swapped([pair, opposite])
        near_sib, beside = together(near_sib, beside)
        second = swapped([beside])
        first, second, far = together(first, second, far)
        weights += [(pair, ("pair", "ring")), (opposite, (4, "ring")), (beside, ("beside", "ring"))]
        weights += [(swap, ((-1, 1, -2, 2), "swap"))]
        weights += [(first, (("pair", 4), "swap")), (second, (("beside",), "swap"))]
    else:
        near, far = from_chip(normed, 1), from_chip(normed, -1)
        near_sib = sibling(near)
    pieces = (normed, sibling(normed), near, near_sib, far, sibling(far))
    mine, other = attend(pieces, weights)
    return finish(tokens_zero, mine, sibling(other), attn_out)


def solution(mesh):
    in_specs = (
        P(("groups", "space"), None),
        P(),
        P(),
        P(),
        P(),
        P(),
        P(),
        P("space", None),
        P(),
        P(None, "space"),
        P(),
    )
    out_specs = P(("groups", "space"), None)
    return jax.shard_map(
        per_device, mesh=mesh, in_specs=in_specs, out_specs=out_specs, check_vma=False
    )
```

```python
import functools
import math

import jax
import jax.numpy as jnp
from jax import lax
from jax.experimental import pallas as pl
from jax.experimental.pallas import tpu as pltpu
from jax.sharding import PartitionSpec as P

BF16 = jnp.bfloat16
F32 = jnp.float32
LANES = 128
WHOLE_VMEM = 60 * 1024 * 1024
PART_VMEM = 24 * 1024 * 1024
RING = (0, 2, 4, 6, 7, 5, 3, 1)


def dot(left, right):
    return jnp.dot(left, right, preferred_element_type=F32)


def dot_t(left, right):
    return lax.dot_general(left, right, (((1,), (1,)), ((), ())), preferred_element_type=F32)


def ring_place(index):
    chip = index // 2
    return jnp.where(chip % 2 == 0, chip // 2, 7 - chip // 2)


def chip_at(index, step):
    if step is None:
        return 0
    here = ring_place(index)
    if step == "beside":
        step = jnp.where(here % 2 == 0, -3, 3)
    elif step == "pair":
        step = jnp.where(here % 2 == 0, 3, -3)
    at = (here + step + 8) % 8
    return jnp.where(at < 4, 2 * at, 2 * (7 - at) + 1)


def iota(shape, dim):
    return lax.broadcasted_iota(jnp.int32, shape, dim)


def over(x, n):
    return x >> (n.bit_length() - 1) if n & (n - 1) == 0 else x // n


def within(x, n):
    return x & (n - 1) if n & (n - 1) == 0 else x % n


def fetch(pairs, sems):
    copies = [pltpu.make_async_copy(src, dst, sems.at[i]) for i, (src, dst) in enumerate(pairs)]
    for copy in copies:
        copy.start()
    return [copy.wait for copy in copies]


def spread_offsets(offset_half, heads, head_size, first):
    var_count, half = offset_half.shape
    spread = var_count * heads
    picks = (over(iota((spread, var_count), 0), heads) == iota((spread, var_count), 1)).astype(F32)
    rows = dot(picks.astype(BF16), offset_half).astype(BF16)
    mine = within(iota((spread, half), 0), heads) == over(iota((spread, half), 1), head_size) + first
    return jnp.where(mine, rows, jnp.zeros_like(rows))


def mix_heads(probs, patches, table_values, base, first, pairs, heads, head_size, pixels):
    tokens, spread = probs.shape
    group = math.gcd(spread, 256)
    row_g, col_g = iota((group, group), 0), iota((group, group), 1)
    same = over(row_g, heads) == over(col_g, pixels)
    head_g = jnp.where(same, within(row_g, heads), -1)
    left_half = iota((tokens, 2 * head_size), 1) < head_size
    values = []
    for pair in range(pairs):
        halves = []
        cols = slice(pair * 2 * head_size, (pair + 1) * 2 * head_size)
        for head in (first + 2 * pair, first + 2 * pair + 1):
            pick = jnp.where(head_g == head, 1.0, 0.0).astype(BF16)
            weights = jnp.concatenate(
                [
                    dot(probs[:, g * group : (g + 1) * group], pick).astype(BF16)
                    for g in range(spread // group)
                ],
                axis=1,
            )
            halves.append(dot(weights * patches, table_values[:, cols]))
        values.append((jnp.where(left_half, halves[0], halves[1]) + base[:, cols]).astype(BF16))
    return jnp.concatenate(values, axis=1)


def aggregate_kernel(
    order_ref,
    var_embed_hbm,
    keys_hbm,
    embed_hbm,
    patches_hbm,
    value_hbm,
    out_w_hbm,
    pos_hbm,
    gain_hbm,
    tokens_ref,
    normed_ref,
    var_embed_ref,
    keys_ref,
    embed_ref,
    patches_ref,
    value_ref,
    out_w_ref,
    pos_ref,
    gain_ref,
    table_ref,
    values_ref,
    sems,
):
    var_count, pixels, width = embed_ref.shape
    heads = keys_ref.shape[0]
    head_size = width // heads
    rows, spread = var_count * pixels, var_count * heads
    scale = 1.0 / math.sqrt(head_size)
    waits = fetch(
        (
            (var_embed_hbm, var_embed_ref),
            (keys_hbm, keys_ref),
            (embed_hbm, embed_ref),
            (patches_hbm, patches_ref),
            (value_hbm, value_ref),
            (out_w_hbm, out_w_ref),
            (pos_hbm, pos_ref),
            (gain_hbm, gain_ref),
        ),
        sems,
    )
    line = iota((var_count, var_count), 0)
    order = jnp.zeros((var_count, var_count), jnp.int32)
    for j in range(var_count):
        order = jnp.where(line == j, order_ref[j], order)
    select = (order == iota((var_count, var_count), 1)).astype(F32).astype(BF16)
    waits[0]()
    offsets = dot(select, var_embed_ref[...]).astype(BF16)
    waits[1]()
    repeat = (within(iota((LANES, heads), 0), heads) == iota((LANES, heads), 1)).astype(F32).astype(BF16)
    keys = dot(repeat, keys_ref[...]).astype(BF16)
    offset_keys = dot_t(offsets, keys)
    waits[2]()
    for j in range(var_count):
        table_ref[j] = embed_ref[order_ref[j]]
    table = table_ref[...].reshape(rows, width)
    table_keys = dot_t(table, keys)
    high = table_keys.astype(BF16)
    low = (table_keys - high.astype(F32)).astype(BF16)
    waits[3]()
    patches = patches_ref[...]
    group = math.gcd(spread, 256)
    lines = group // heads * pixels
    same = over(iota((lines, LANES), 0), pixels)
    cols_of = over(iota((lines, LANES), 1), heads)
    channel = over(iota((var_count, LANES), 1), heads)
    scores = []
    for part in range(spread // group):
        here = slice(part * lines, (part + 1) * lines)
        highs, lows, shifts = [], [], []
        for block in range(group // LANES):
            first = block * (LANES // heads)
            match = same == cols_of + first
            highs.append(jnp.where(match, high[here], jnp.zeros_like(high[here])))
            lows.append(jnp.where(match, low[here], jnp.zeros_like(low[here])))
            match = channel + (first + part * (group // heads)) == iota((var_count, LANES), 0)
            shifts.append(jnp.sum(jnp.where(match, offset_keys, 0.0), axis=0, keepdims=True))
        total = dot(patches[:, here], jnp.concatenate(highs, axis=1))
        total = total + dot(patches[:, here], jnp.concatenate(lows, axis=1))
        for block, shift in enumerate(shifts):
            scores.append((total[:, block * LANES : (block + 1) * LANES] + shift) * scale)
    waits[4]()
    values_ref[...] = dot(table, value_ref[...]).astype(BF16)
    offset_values = dot(offsets, value_ref[...]).astype(BF16)
    top = functools.reduce(jnp.maximum, scores)
    step = heads
    while step < LANES:
        top = jnp.maximum(top, pltpu.roll(top, step, 1))
        step *= 2
    exps = [jnp.exp(s - top) for s in scores]
    total = functools.reduce(jnp.add, exps)
    step = heads
    while step < LANES:
        total = total + pltpu.roll(total, step, 1)
        step *= 2
    probs = jnp.concatenate([(e / total).astype(BF16) for e in exps], axis=1)
    base = dot(probs, spread_offsets(offset_values, heads, head_size, 0))
    values = mix_heads(
        probs, patches, values_ref, base, 0, heads // 2, heads, head_size, pixels
    )
    for wait in waits[5:]:
        wait()
    tokens_zero = (dot(values, out_w_ref[...]) + pos_ref[...].astype(F32)).astype(BF16)
    tokens_ref[...] = tokens_zero
    full = tokens_zero.astype(F32)
    centred = full - jnp.mean(full, axis=-1, keepdims=True)
    variance = jnp.mean(centred * centred, axis=-1, keepdims=True)
    normed_ref[...] = (centred * lax.rsqrt(variance + 1e-05) * gain_ref[...]).astype(BF16)


def cost(gflops, mib, exps=0):
    return pl.CostEstimate(
        flops=int(gflops * 1e9), bytes_accessed=int(mib * (1 << 20)), transcendentals=exps
    )


VMEM = pl.BlockSpec(memory_space=pltpu.VMEM)
SMEM = pl.BlockSpec(memory_space=pltpu.SMEM)
HBM = pl.BlockSpec(memory_space=pltpu.HBM)


def like(*arrays):
    return [pltpu.VMEM(a.shape, a.dtype) for a in arrays]


def aggregate(var_order, var_embed, keys, embed_weight, patches, value, out_w, pos, gain):
    tokens, width = pos.shape
    var_count, pixels, _ = embed_weight.shape
    arrays = (var_embed, keys, embed_weight, patches, value, out_w, pos, gain.reshape(1, width))
    return pl.pallas_call(
        aggregate_kernel,
        out_shape=[jax.ShapeDtypeStruct((tokens, width), BF16)] * 2,
        in_specs=[SMEM] + [HBM] * len(arrays),
        out_specs=[VMEM] * 2,
        scratch_shapes=like(*arrays)
        + like(embed_weight)
        + [pltpu.VMEM((var_count * pixels, width), BF16)]
        + [pltpu.SemaphoreType.DMA((len(arrays),))],
        compiler_params=pltpu.CompilerParams(vmem_limit_bytes=WHOLE_VMEM),
        cost_estimate=cost(16, 8, 1 << 18),
        name="aggregate",
    )(var_order, *arrays)


def attend_kernel(*refs, spots):
    count = len(spots)
    weight_refs = refs[6 : 6 + count]
    mine_ref, other_ref, query_s, key_s, value_s, weight_s, sems = refs[6 + count :]
    index, plane = lax.axis_index("space"), lax.axis_index("groups")
    side = index % 2
    moves = []
    for ref, (step, share) in zip(weight_refs, spots):
        rows = ref.shape[0]
        if share == "ring":
            start = pl.multiple_of(plane * (rows // 2), 32)
            moves.append((ref, weight_s.at[chip_at(index, step), pl.ds(start, rows), :]))
        elif share == "swap":
            rows = rows // len(step)
            start = pl.multiple_of((1 - plane) * (2 * rows), 32)
            for i, one in enumerate(step):
                place = weight_s.at[chip_at(index, one), pl.ds(start, rows), :]
                moves.append((ref.at[pl.ds(i * rows, rows), :], place))
        else:
            moves.append((ref, weight_s.at[chip_at(index, step)]))
    for wait in fetch(moves, sems):
        wait()
    flip = index // 2 % 2 if spots[0][0] is not None else 0
    near, far = 4 - 4 * flip, 4 * flip
    tokens, width = refs[0].shape
    pairs = mine_ref.shape[0]
    cols = pairs * LANES
    weight = weight_s[...].reshape(3 * cols, width)
    head_size = LANES // 2
    scale = 1.0 / math.sqrt(head_size)
    pieces = (2 + side, 3 - side, near + side, near + 1 - side, far + side, far + 1 - side)
    ones = jnp.ones((tokens, LANES), BF16)
    for number, place in enumerate(pieces):
        rows = refs[number][...]
        both = dot_t(rows, weight[cols:]).astype(BF16)
        spot = pl.ds(pl.multiple_of(place * tokens, tokens), tokens)
        for pair in range(pairs):
            lanes = slice(pair * LANES, (pair + 1) * LANES)
            key_s[pair, spot, :] = both[:, :cols][:, lanes]
            value_s[pair, spot, :] = jnp.concatenate([both[:, cols:][:, lanes], ones], axis=1)
        if number < 2:
            query = (dot_t(rows, weight[:cols]).astype(BF16).astype(F32) * scale).astype(BF16)
            for pair in range(pairs):
                query_s[number, pair] = query[:, pair * LANES : (pair + 1) * LANES]

    left_half = iota((tokens, LANES), 1) < head_size

    def attend(pair, carry):
        for number, (out_ref, sector) in enumerate(((mine_ref, side), (other_ref, 1 - side))):
            query = query_s[number, pair]
            halves = []
            for half in range(2):
                keep = left_half if half == 0 else jnp.logical_not(left_half)
                masked = jnp.where(keep, query, jnp.zeros_like(query))
                start = pl.multiple_of(sector * tokens, tokens)
                scores = [
                    dot_t(masked, key_s[pair, pl.ds(start + k * tokens, tokens), :])
                    for k in range(5)
                ]
                top = jnp.max(functools.reduce(jnp.maximum, scores), axis=-1, keepdims=True)
                probs = jnp.concatenate([jnp.exp(s - top).astype(BF16) for s in scores], axis=1)
                acc = dot(probs, value_s[pair, pl.ds(start, 5 * tokens), :])
                halves.append(acc[:, :LANES] / acc[:, LANES:])
            out_ref[pair] = jnp.where(left_half, halves[0], halves[1]).astype(BF16)
        return carry

    lax.fori_loop(0, pairs, attend, 0, unroll=True)


def attend(pieces, weights):
    tokens, width = pieces[0].shape
    spots = tuple(spot for _, spot in weights)
    weights = [piece for piece, _ in weights]
    rows = weights[0].shape[0]
    blocks = 1 if len(weights) == 1 else len(RING)
    cols = rows * blocks // 3
    pairs = cols // LANES
    return pl.pallas_call(
        functools.partial(attend_kernel, spots=spots),
        out_shape=[jax.ShapeDtypeStruct((pairs, tokens, LANES), BF16)] * 2,
        in_specs=[VMEM] * 6 + [HBM] * len(weights),
        out_specs=[VMEM, VMEM],
        scratch_shapes=[
            pltpu.VMEM((2, pairs, tokens, LANES), BF16),
            pltpu.VMEM((pairs, 6 * tokens, LANES), BF16),
            pltpu.VMEM((pairs, 6 * tokens, 2 * LANES), BF16),
            pltpu.VMEM((blocks, rows, width), BF16),
            pltpu.SemaphoreType.DMA((32,)),
        ],
        compiler_params=pltpu.CompilerParams(vmem_limit_bytes=PART_VMEM),
        cost_estimate=cost(10, 8, 5 << 20),
        name="attend",
    )(*pieces, *weights)


def finish_kernel(tokens_ref, mine_ref, other_ref, weight_ref, out_ref):
    side = lax.axis_index("space") % 2
    pairs, tokens, lanes = mine_ref.shape
    width = tokens_ref.shape[1]

    def part(ref, parity):
        rows = jnp.concatenate([ref[pair] for pair in range(pairs)], axis=1)
        return dot(rows, weight_ref[:, parity].reshape(pairs * lanes, width))

    update = part(mine_ref, side) + part(other_ref, 1 - side)
    out_ref[...] = (tokens_ref[...].astype(F32) + update).astype(BF16)


def finish(tokens_zero, mine, other, attn_out):
    tokens, width = tokens_zero.shape
    return pl.pallas_call(
        finish_kernel,
        out_shape=jax.ShapeDtypeStruct((tokens, width), BF16),
        in_specs=[VMEM] * 4,
        out_specs=VMEM,
        compiler_params=pltpu.CompilerParams(vmem_limit_bytes=PART_VMEM),
        cost_estimate=cost(1, 4),
        name="finish",
    )(tokens_zero, mine, other, attn_out.reshape(-1, 2, LANES // 2, width))


def sibling(value):
    length = lax.axis_size("space")
    return lax.ppermute(value, "space", [(i, i ^ 1) for i in range(length)])


def from_chip(value, by):
    length = lax.axis_size("space")
    return lax.ppermute(value, "space", [((i + 2 * by) % length, i) for i in range(length)])


def around(value, by):
    pairs = []
    for place, chip in enumerate(RING):
        for core in range(2):
            step = by if isinstance(by, int) else by[core]
            pairs.append((2 * chip + core, 2 * RING[(place + step) % len(RING)] + core))
    return lax.ppermute(value, "space", pairs)


def crossed(value, bits):
    return lax.ppermute(value, "space", [(i, i ^ bits) for i in range(2 * len(RING))])


def onward(value):
    length = 2 * len(RING)
    pairs = [(i, (i + (4 if i & 2 == 0 else -4)) % length) for i in range(length)]
    return lax.ppermute(value, "space", pairs)


def across(value):
    return lax.ppermute(value, "groups", [(0, 1), (1, 0)])


def together(*values):
    return lax.optimization_barrier(values)


def parity_block(qkv_weight, side, head_size):
    rows = qkv_weight.T
    low, middle, high = (rows[i * head_size : (i + 1) * head_size] for i in range(3))
    given = sibling(middle)
    return jnp.where(
        side == 0,
        jnp.concatenate([low, high, given], axis=0),
        jnp.concatenate([given, low, high], axis=0),
    )


def parity_weight(qkv_weight, side, head_size):
    rows = lax.all_gather(qkv_weight.T, "space", axis=0, tiled=True)
    blocks = rows.reshape(-1, 2, head_size, rows.shape[1])
    picked = lax.dynamic_index_in_dim(blocks, side, 1, keepdims=False)
    return [(picked.reshape(-1, rows.shape[1]), (None, None))]


def per_device(
    patches,
    var_order,
    embed_weight,
    var_embed,
    agg_keys,
    agg_value,
    agg_out,
    pos_embed,
    norm_gain,
    qkv_weight,
    attn_out,
):
    heads = agg_keys.shape[0]
    head_size = embed_weight.shape[2] // heads
    side = lax.axis_index("space") % 2
    ringed = (
        lax.axis_size("space") == 2 * len(RING)
        and lax.axis_size("groups") == 2
        and qkv_weight.shape[1] == 3 * head_size
    )
    if ringed:
        block = parity_block(qkv_weight, side, head_size)
        block, embed_weight = together(block, embed_weight)
        third = block.shape[0] // 3
        plane = lax.axis_index("groups")
        share = lax.dynamic_slice_in_dim(block, plane * third, 2 * third, 0)
        early = [around(share, step) for step in (1, -1, 2, -2)]
        weights = [(block, (0, None))]
    else:
        weights = parity_weight(qkv_weight, side, head_size)
    tokens_zero, normed = aggregate(
        var_order, var_embed, agg_keys, embed_weight, patches, agg_value, agg_out, pos_embed, norm_gain
    )
    if ringed:

        def swapped(blocks):
            parts = [lax.dynamic_slice_in_dim(b, plane * third, third, 0) for b in blocks]
            return across(jnp.concatenate(parts, axis=0))

        tokens_zero, *early = together(tokens_zero, *early)
        weights += [(b, (-step, "ring")) for b, step in zip(early, (1, -1, 2, -2))]
        swap = swapped(early)
        place = ring_place(lax.axis_index("space"))
        near = crossed(normed, 2)
        pair = crossed(jnp.where(place % 2 == 0, early[2], early[3]), 4)
        low = place % 4 < 2
        opposite = crossed(jnp.where(low, early[2], early[3]), 8)
        near, pair, opposite = together(near, pair, opposite)
        far, near_sib = onward(near), sibling(near)
        beside = crossed(jnp.where(low, early[3], early[2]), 2)
        first = swapped([pair, opposite])
        swap, near_sib, beside = together(swap, near_sib, beside)
        second = swapped([beside])
        first, second, far = together(first, second, far)
        weights += [(pair, ("pair", "ring")), (opposite, (4, "ring")), (beside, ("beside", "ring"))]
        weights += [(swap, ((-1, 1, -2, 2), "swap"))]
        weights += [(first, (("pair", 4), "swap")), (second, (("beside",), "swap"))]
    else:
        near, far = from_chip(normed, 1), from_chip(normed, -1)
        near_sib = sibling(near)
    pieces = (normed, sibling(normed), near, near_sib, far, sibling(far))
    mine, other = attend(pieces, weights)
    return finish(tokens_zero, mine, sibling(other), attn_out)


def solution(mesh):
    in_specs = (
        P(("groups", "space"), None),
        P(),
        P(),
        P(),
        P(),
        P(),
        P(),
        P("space", None),
        P(),
        P(None, "space"),
        P(),
    )
    out_specs = P(("groups", "space"), None)
    return jax.shard_map(
        per_device, mesh=mesh, in_specs=in_specs, out_specs=out_specs, check_vma=False
    )
```

```python
import functools
import math

import jax
import jax.numpy as jnp
from jax import lax
from jax.experimental import pallas as pl
from jax.experimental.pallas import tpu as pltpu
from jax.sharding import PartitionSpec as P

BF16 = jnp.bfloat16
F32 = jnp.float32
LANES = 128
WHOLE_VMEM = 60 * 1024 * 1024
PART_VMEM = 24 * 1024 * 1024
RING = (0, 2, 4, 6, 7, 5, 3, 1)


def dot(left, right):
    return jnp.dot(left, right, preferred_element_type=F32)


def dot_t(left, right):
    return lax.dot_general(left, right, (((1,), (1,)), ((), ())), preferred_element_type=F32)


def ring_place(index):
    chip = index // 2
    return jnp.where(chip % 2 == 0, chip // 2, 7 - chip // 2)


def chip_at(index, step):
    if step is None:
        return 0
    here = ring_place(index)
    if step == "beside":
        step = jnp.where(here % 2 == 0, -3, 3)
    elif step == "pair":
        step = jnp.where(here % 2 == 0, 3, -3)
    at = (here + step + 8) % 8
    return jnp.where(at < 4, 2 * at, 2 * (7 - at) + 1)


def iota(shape, dim):
    return lax.broadcasted_iota(jnp.int32, shape, dim)


def over(x, n):
    return x >> (n.bit_length() - 1) if n & (n - 1) == 0 else x // n


def within(x, n):
    return x & (n - 1) if n & (n - 1) == 0 else x % n


def fetch(pairs, sems):
    copies = [pltpu.make_async_copy(src, dst, sems.at[i]) for i, (src, dst) in enumerate(pairs)]
    for copy in copies:
        copy.start()
    return [copy.wait for copy in copies]


def spread_offsets(offset_half, heads, head_size, first):
    var_count, half = offset_half.shape
    spread = var_count * heads
    picks = (over(iota((spread, var_count), 0), heads) == iota((spread, var_count), 1)).astype(F32)
    rows = dot(picks.astype(BF16), offset_half).astype(BF16)
    mine = within(iota((spread, half), 0), heads) == over(iota((spread, half), 1), head_size) + first
    return jnp.where(mine, rows, jnp.zeros_like(rows))


def mix_heads(probs, patches, table_values, base, first, pairs, heads, head_size, pixels):
    tokens, spread = probs.shape
    group = math.gcd(spread, 256)
    row_g, col_g = iota((group, group), 0), iota((group, group), 1)
    same = over(row_g, heads) == over(col_g, pixels)
    head_g = jnp.where(same, within(row_g, heads), -1)
    left_half = iota((tokens, 2 * head_size), 1) < head_size
    values = []
    for pair in range(pairs):
        halves = []
        cols = slice(pair * 2 * head_size, (pair + 1) * 2 * head_size)
        for head in (first + 2 * pair, first + 2 * pair + 1):
            pick = jnp.where(head_g == head, 1.0, 0.0).astype(BF16)
            weights = jnp.concatenate(
                [
                    dot(probs[:, g * group : (g + 1) * group], pick).astype(BF16)
                    for g in range(spread // group)
                ],
                axis=1,
            )
            halves.append(dot(weights * patches, table_values[:, cols]))
        values.append((jnp.where(left_half, halves[0], halves[1]) + base[:, cols]).astype(BF16))
    return jnp.concatenate(values, axis=1)


def aggregate_kernel(
    order_ref,
    var_embed_hbm,
    keys_hbm,
    embed_hbm,
    patches_hbm,
    value_hbm,
    out_w_hbm,
    pos_hbm,
    gain_hbm,
    tokens_ref,
    normed_ref,
    var_embed_ref,
    keys_ref,
    embed_ref,
    patches_ref,
    value_ref,
    out_w_ref,
    pos_ref,
    gain_ref,
    table_ref,
    values_ref,
    sems,
):
    var_count, pixels, width = embed_ref.shape
    heads = keys_ref.shape[0]
    head_size = width // heads
    rows, spread = var_count * pixels, var_count * heads
    scale = 1.0 / math.sqrt(head_size)
    waits = fetch(
        (
            (var_embed_hbm, var_embed_ref),
            (keys_hbm, keys_ref),
            (embed_hbm, embed_ref),
            (patches_hbm, patches_ref),
            (value_hbm, value_ref),
            (out_w_hbm, out_w_ref),
            (pos_hbm, pos_ref),
            (gain_hbm, gain_ref),
        ),
        sems,
    )
    line = iota((var_count, var_count), 0)
    order = jnp.zeros((var_count, var_count), jnp.int32)
    for j in range(var_count):
        order = jnp.where(line == j, order_ref[j], order)
    select = (order == iota((var_count, var_count), 1)).astype(F32).astype(BF16)
    waits[0]()
    offsets = dot(select, var_embed_ref[...]).astype(BF16)
    waits[1]()
    repeat = (within(iota((LANES, heads), 0), heads) == iota((LANES, heads), 1)).astype(F32).astype(BF16)
    keys = dot(repeat, keys_ref[...]).astype(BF16)
    offset_keys = dot_t(offsets, keys)
    waits[2]()
    for j in range(var_count):
        table_ref[j] = embed_ref[order_ref[j]]
    table = table_ref[...].reshape(rows, width)
    table_keys = dot_t(table, keys)
    high = table_keys.astype(BF16)
    low = (table_keys - high.astype(F32)).astype(BF16)
    waits[3]()
    patches = patches_ref[...]
    group = math.gcd(spread, 256)
    lines = group // heads * pixels
    same = over(iota((lines, LANES), 0), pixels)
    cols_of = over(iota((lines, LANES), 1), heads)
    channel = over(iota((var_count, LANES), 1), heads)
    scores = []
    for part in range(spread // group):
        here = slice(part * lines, (part + 1) * lines)
        highs, lows, shifts = [], [], []
        for block in range(group // LANES):
            first = block * (LANES // heads)
            match = same == cols_of + first
            highs.append(jnp.where(match, high[here], jnp.zeros_like(high[here])))
            lows.append(jnp.where(match, low[here], jnp.zeros_like(low[here])))
            match = channel + (first + part * (group // heads)) == iota((var_count, LANES), 0)
            shifts.append(jnp.sum(jnp.where(match, offset_keys, 0.0), axis=0, keepdims=True))
        total = dot(patches[:, here], jnp.concatenate(highs, axis=1))
        total = total + dot(patches[:, here], jnp.concatenate(lows, axis=1))
        for block, shift in enumerate(shifts):
            scores.append((total[:, block * LANES : (block + 1) * LANES] + shift) * scale)
    waits[4]()
    values_ref[...] = dot(table, value_ref[...]).astype(BF16)
    offset_values = dot(offsets, value_ref[...]).astype(BF16)
    top = functools.reduce(jnp.maximum, scores)
    step = heads
    while step < LANES:
        top = jnp.maximum(top, pltpu.roll(top, step, 1))
        step *= 2
    exps = [jnp.exp(s - top) for s in scores]
    total = functools.reduce(jnp.add, exps)
    step = heads
    while step < LANES:
        total = total + pltpu.roll(total, step, 1)
        step *= 2
    probs = jnp.concatenate([(e / total).astype(BF16) for e in exps], axis=1)
    base = dot(probs, spread_offsets(offset_values, heads, head_size, 0))
    values = mix_heads(
        probs, patches, values_ref, base, 0, heads // 2, heads, head_size, pixels
    )
    for wait in waits[5:]:
        wait()
    tokens_zero = (dot(values, out_w_ref[...]) + pos_ref[...].astype(F32)).astype(BF16)
    tokens_ref[...] = tokens_zero
    full = tokens_zero.astype(F32)
    centred = full - jnp.mean(full, axis=-1, keepdims=True)
    variance = jnp.mean(centred * centred, axis=-1, keepdims=True)
    normed_ref[...] = (centred * lax.rsqrt(variance + 1e-05) * gain_ref[...]).astype(BF16)


def cost(gflops, mib, exps=0):
    return pl.CostEstimate(
        flops=int(gflops * 1e9), bytes_accessed=int(mib * (1 << 20)), transcendentals=exps
    )


VMEM = pl.BlockSpec(memory_space=pltpu.VMEM)
SMEM = pl.BlockSpec(memory_space=pltpu.SMEM)
HBM = pl.BlockSpec(memory_space=pltpu.HBM)


def like(*arrays):
    return [pltpu.VMEM(a.shape, a.dtype) for a in arrays]


def aggregate(var_order, var_embed, keys, embed_weight, patches, value, out_w, pos, gain):
    tokens, width = pos.shape
    var_count, pixels, _ = embed_weight.shape
    arrays = (var_embed, keys, embed_weight, patches, value, out_w, pos, gain.reshape(1, width))
    return pl.pallas_call(
        aggregate_kernel,
        out_shape=[jax.ShapeDtypeStruct((tokens, width), BF16)] * 2,
        in_specs=[SMEM] + [HBM] * len(arrays),
        out_specs=[VMEM] * 2,
        scratch_shapes=like(*arrays)
        + like(embed_weight)
        + [pltpu.VMEM((var_count * pixels, width), BF16)]
        + [pltpu.SemaphoreType.DMA((len(arrays),))],
        compiler_params=pltpu.CompilerParams(vmem_limit_bytes=WHOLE_VMEM),
        cost_estimate=cost(16, 8, 1 << 18),
        name="aggregate",
    )(var_order, *arrays)


def assemble_kernel(*refs, spots):
    weight_refs, out_ref, sems = refs[:-2], refs[-2], refs[-1]
    index, plane = lax.axis_index("space"), lax.axis_index("groups")
    moves = []
    for ref, (step, share) in zip(weight_refs, spots):
        rows = ref.shape[0]
        if share == "ring":
            start = pl.multiple_of(plane * (rows // 2), 32)
            moves.append((ref, out_ref.at[chip_at(index, step), pl.ds(start, rows), :]))
        elif share == "swap":
            rows = rows // len(step)
            start = pl.multiple_of((1 - plane) * (2 * rows), 32)
            for i, one in enumerate(step):
                place = out_ref.at[chip_at(index, one), pl.ds(start, rows), :]
                moves.append((ref.at[pl.ds(i * rows, rows), :], place))
        else:
            moves.append((ref, out_ref.at[chip_at(index, step)]))
    for wait in fetch(moves, sems):
        wait()


def assemble(weights):
    spots = tuple(spot for _, spot in weights)
    weights = [piece for piece, _ in weights]
    blocks = 1 if len(weights) == 1 else len(RING)
    return pl.pallas_call(
        functools.partial(assemble_kernel, spots=spots),
        out_shape=jax.ShapeDtypeStruct((blocks,) + weights[0].shape, BF16),
        in_specs=[HBM] * len(weights),
        out_specs=VMEM,
        scratch_shapes=[pltpu.SemaphoreType.DMA((32,))],
        compiler_params=pltpu.CompilerParams(vmem_limit_bytes=PART_VMEM),
        cost_estimate=cost(1, 6),
        name="assemble",
    )(*weights)


def attend_kernel(*refs, flipped):
    weight_ref, mine_ref, other_ref, query_s, key_s, value_s = refs[6:]
    index = lax.axis_index("space")
    side = index % 2
    flip = index // 2 % 2 if flipped else 0
    near, far = 4 - 4 * flip, 4 * flip
    tokens, width = refs[0].shape
    pairs = mine_ref.shape[0]
    cols = pairs * LANES
    weight = weight_ref[...].reshape(3 * cols, width)
    head_size = LANES // 2
    scale = 1.0 / math.sqrt(head_size)
    pieces = (2 + side, 3 - side, near + side, near + 1 - side, far + side, far + 1 - side)
    ones = jnp.ones((tokens, LANES), BF16)
    for number, place in enumerate(pieces):
        rows = refs[number][...]
        both = dot_t(rows, weight[cols:]).astype(BF16)
        spot = pl.ds(pl.multiple_of(place * tokens, tokens), tokens)
        for pair in range(pairs):
            lanes = slice(pair * LANES, (pair + 1) * LANES)
            key_s[pair, spot, :] = both[:, :cols][:, lanes]
            value_s[pair, spot, :] = jnp.concatenate([both[:, cols:][:, lanes], ones], axis=1)
        if number < 2:
            query = (dot_t(rows, weight[:cols]).astype(BF16).astype(F32) * scale).astype(BF16)
            for pair in range(pairs):
                query_s[number, pair] = query[:, pair * LANES : (pair + 1) * LANES]

    left_half = iota((tokens, LANES), 1) < head_size

    def attend(pair, carry):
        for number, (out_ref, sector) in enumerate(((mine_ref, side), (other_ref, 1 - side))):
            query = query_s[number, pair]
            halves = []
            for half in range(2):
                keep = left_half if half == 0 else jnp.logical_not(left_half)
                masked = jnp.where(keep, query, jnp.zeros_like(query))
                start = pl.multiple_of(sector * tokens, tokens)
                scores = [
                    dot_t(masked, key_s[pair, pl.ds(start + k * tokens, tokens), :])
                    for k in range(5)
                ]
                top = jnp.max(functools.reduce(jnp.maximum, scores), axis=-1, keepdims=True)
                probs = jnp.concatenate([jnp.exp(s - top).astype(BF16) for s in scores], axis=1)
                acc = dot(probs, value_s[pair, pl.ds(start, 5 * tokens), :])
                halves.append(acc[:, :LANES] / acc[:, LANES:])
            out_ref[pair] = jnp.where(left_half, halves[0], halves[1]).astype(BF16)
        return carry

    lax.fori_loop(0, pairs, attend, 0, unroll=True)


def attend(pieces, weight):
    tokens, width = pieces[0].shape
    blocks, rows, _ = weight.shape
    cols = rows * blocks // 3
    pairs = cols // LANES
    return pl.pallas_call(
        functools.partial(attend_kernel, flipped=blocks > 1),
        out_shape=[jax.ShapeDtypeStruct((pairs, tokens, LANES), BF16)] * 2,
        in_specs=[VMEM] * 7,
        out_specs=[VMEM, VMEM],
        scratch_shapes=[
            pltpu.VMEM((2, pairs, tokens, LANES), BF16),
            pltpu.VMEM((pairs, 6 * tokens, LANES), BF16),
            pltpu.VMEM((pairs, 6 * tokens, 2 * LANES), BF16),
        ],
        compiler_params=pltpu.CompilerParams(vmem_limit_bytes=PART_VMEM),
        cost_estimate=cost(10, 8, 5 << 20),
        name="attend",
    )(*pieces, weight)


def finish_kernel(tokens_ref, mine_ref, other_ref, weight_ref, out_ref):
    side = lax.axis_index("space") % 2
    pairs, tokens, lanes = mine_ref.shape
    width = tokens_ref.shape[1]

    def part(ref, parity):
        rows = jnp.concatenate([ref[pair] for pair in range(pairs)], axis=1)
        return dot(rows, weight_ref[:, parity].reshape(pairs * lanes, width))

    update = part(mine_ref, side) + part(other_ref, 1 - side)
    out_ref[...] = (tokens_ref[...].astype(F32) + update).astype(BF16)


def finish(tokens_zero, mine, other, attn_out):
    tokens, width = tokens_zero.shape
    return pl.pallas_call(
        finish_kernel,
        out_shape=jax.ShapeDtypeStruct((tokens, width), BF16),
        in_specs=[VMEM] * 4,
        out_specs=VMEM,
        compiler_params=pltpu.CompilerParams(vmem_limit_bytes=PART_VMEM),
        cost_estimate=cost(1, 4),
        name="finish",
    )(tokens_zero, mine, other, attn_out.reshape(-1, 2, LANES // 2, width))


def sibling(value):
    length = lax.axis_size("space")
    return lax.ppermute(value, "space", [(i, i ^ 1) for i in range(length)])


def from_chip(value, by):
    length = lax.axis_size("space")
    return lax.ppermute(value, "space", [((i + 2 * by) % length, i) for i in range(length)])


def around(value, by):
    pairs = []
    for place, chip in enumerate(RING):
        for core in range(2):
            step = by if isinstance(by, int) else by[core]
            pairs.append((2 * chip + core, 2 * RING[(place + step) % len(RING)] + core))
    return lax.ppermute(value, "space", pairs)


def crossed(value, bits):
    return lax.ppermute(value, "space", [(i, i ^ bits) for i in range(2 * len(RING))])


def onward(value):
    length = 2 * len(RING)
    pairs = [(i, (i + (4 if i & 2 == 0 else -4)) % length) for i in range(length)]
    return lax.ppermute(value, "space", pairs)


def across(value):
    return lax.ppermute(value, "groups", [(0, 1), (1, 0)])


def together(*values):
    return lax.optimization_barrier(values)


def parity_block(qkv_weight, side, head_size):
    rows = qkv_weight.T
    low, middle, high = (rows[i * head_size : (i + 1) * head_size] for i in range(3))
    given = sibling(middle)
    return jnp.where(
        side == 0,
        jnp.concatenate([low, high, given], axis=0),
        jnp.concatenate([given, low, high], axis=0),
    )


def parity_weight(qkv_weight, side, head_size):
    rows = lax.all_gather(qkv_weight.T, "space", axis=0, tiled=True)
    blocks = rows.reshape(-1, 2, head_size, rows.shape[1])
    picked = lax.dynamic_index_in_dim(blocks, side, 1, keepdims=False)
    return [(picked.reshape(-1, rows.shape[1]), (None, None))]


def per_device(
    patches,
    var_order,
    embed_weight,
    var_embed,
    agg_keys,
    agg_value,
    agg_out,
    pos_embed,
    norm_gain,
    qkv_weight,
    attn_out,
):
    heads = agg_keys.shape[0]
    head_size = embed_weight.shape[2] // heads
    side = lax.axis_index("space") % 2
    ringed = (
        lax.axis_size("space") == 2 * len(RING)
        and lax.axis_size("groups") == 2
        and qkv_weight.shape[1] == 3 * head_size
    )
    if ringed:
        block = parity_block(qkv_weight, side, head_size)
        block, embed_weight = together(block, embed_weight)
        third = block.shape[0] // 3
        plane = lax.axis_index("groups")
        share = lax.dynamic_slice_in_dim(block, plane * third, 2 * third, 0)
        early = [around(share, step) for step in (1, -1, 2, -2)]
        weights = [(block, (0, None))]
    else:
        weights = parity_weight(qkv_weight, side, head_size)
    tokens_zero, normed = aggregate(
        var_order, var_embed, agg_keys, embed_weight, patches, agg_value, agg_out, pos_embed, norm_gain
    )
    if ringed:

        def swapped(blocks):
            parts = [lax.dynamic_slice_in_dim(b, plane * third, third, 0) for b in blocks]
            return across(jnp.concatenate(parts, axis=0))

        tokens_zero, *early = together(tokens_zero, *early)
        weights += [(b, (-step, "ring")) for b, step in zip(early, (1, -1, 2, -2))]
        swap = swapped(early)
        place = ring_place(lax.axis_index("space"))
        near = crossed(normed, 2)
        low = place % 4 < 2
        opposite = crossed(jnp.where(low, early[2], early[3]), 8)
        pair = crossed(jnp.where(place % 2 == 0, early[2], early[3]), 4)
        near, opposite, pair = together(near, opposite, pair)
        far, near_sib = onward(near), sibling(near)
        beside = crossed(jnp.where(low, early[3], early[2]), 2)
        first = swapped([pair, opposite])
        swap, near_sib, beside = together(swap, near_sib, beside)
        second = swapped([beside])
        _, _, far = together(first, second, far)
        weights += [(pair, ("pair", "ring")), (opposite, (4, "ring")), (beside, ("beside", "ring"))]
        weights += [(swap, ((-1, 1, -2, 2), "swap"))]
        weights += [(first, (("pair", 4), "swap")), (second, (("beside",), "swap"))]
    else:
        near, far = from_chip(normed, 1), from_chip(normed, -1)
        near_sib = sibling(near)
    pieces = (normed, sibling(normed), near, near_sib, far, sibling(far))
    mine, other = attend(pieces, assemble(weights))
    return finish(tokens_zero, mine, sibling(other), attn_out)


def solution(mesh):
    in_specs = (
        P(("groups", "space"), None),
        P(),
        P(),
        P(),
        P(),
        P(),
        P(),
        P("space", None),
        P(),
        P(None, "space"),
        P(),
    )
    out_specs = P(("groups", "space"), None)
    return jax.shard_map(
        per_device, mesh=mesh, in_specs=in_specs, out_specs=out_specs, check_vma=False
    )
```

```python
import functools
import math

import jax
import jax.numpy as jnp
from jax import lax
from jax.experimental import pallas as pl
from jax.experimental.pallas import tpu as pltpu
from jax.sharding import PartitionSpec as P

BF16 = jnp.bfloat16
F32 = jnp.float32
LANES = 128
WHOLE_VMEM = 60 * 1024 * 1024
PART_VMEM = 24 * 1024 * 1024
RING = (0, 2, 4, 6, 7, 5, 3, 1)


def dot(left, right):
    return jnp.dot(left, right, preferred_element_type=F32)


def dot_t(left, right):
    return lax.dot_general(left, right, (((1,), (1,)), ((), ())), preferred_element_type=F32)


def ring_place(index):
    chip = index // 2
    return jnp.where(chip % 2 == 0, chip // 2, 7 - chip // 2)


def chip_at(index, step):
    if step is None:
        return 0
    here = ring_place(index)
    if step == "beside":
        step = jnp.where(here % 2 == 0, -3, 3)
    elif step == "pair":
        step = jnp.where(here % 2 == 0, 3, -3)
    at = (here + step + 8) % 8
    return jnp.where(at < 4, 2 * at, 2 * (7 - at) + 1)


def iota(shape, dim):
    return lax.broadcasted_iota(jnp.int32, shape, dim)


def over(x, n):
    return x >> (n.bit_length() - 1) if n & (n - 1) == 0 else x // n


def within(x, n):
    return x & (n - 1) if n & (n - 1) == 0 else x % n


def fetch(pairs, sems):
    copies = [pltpu.make_async_copy(src, dst, sems.at[i]) for i, (src, dst) in enumerate(pairs)]
    for copy in copies:
        copy.start()
    return [copy.wait for copy in copies]


def spread_offsets(offset_half, heads, head_size, first):
    var_count, half = offset_half.shape
    spread = var_count * heads
    picks = (over(iota((spread, var_count), 0), heads) == iota((spread, var_count), 1)).astype(F32)
    rows = dot(picks.astype(BF16), offset_half).astype(BF16)
    mine = within(iota((spread, half), 0), heads) == over(iota((spread, half), 1), head_size) + first
    return jnp.where(mine, rows, jnp.zeros_like(rows))


def mix_heads(probs, patches, table_values, base, first, pairs, heads, head_size, pixels):
    tokens, spread = probs.shape
    group = math.gcd(spread, 256)
    row_g, col_g = iota((group, group), 0), iota((group, group), 1)
    same = over(row_g, heads) == over(col_g, pixels)
    head_g = jnp.where(same, within(row_g, heads), -1)
    left_half = iota((tokens, 2 * head_size), 1) < head_size
    values = []
    for pair in range(pairs):
        halves = []
        cols = slice(pair * 2 * head_size, (pair + 1) * 2 * head_size)
        for head in (first + 2 * pair, first + 2 * pair + 1):
            pick = jnp.where(head_g == head, 1.0, 0.0).astype(BF16)
            weights = jnp.concatenate(
                [
                    dot(probs[:, g * group : (g + 1) * group], pick).astype(BF16)
                    for g in range(spread // group)
                ],
                axis=1,
            )
            halves.append(dot(weights * patches, table_values[:, cols]))
        values.append((jnp.where(left_half, halves[0], halves[1]) + base[:, cols]).astype(BF16))
    return jnp.concatenate(values, axis=1)


def aggregate_kernel(
    order_ref,
    var_embed_hbm,
    keys_hbm,
    embed_hbm,
    patches_hbm,
    value_hbm,
    out_w_hbm,
    pos_hbm,
    gain_hbm,
    tokens_ref,
    normed_ref,
    var_embed_ref,
    keys_ref,
    embed_ref,
    patches_ref,
    value_ref,
    out_w_ref,
    pos_ref,
    gain_ref,
    table_ref,
    values_ref,
    sems,
):
    var_count, pixels, width = embed_ref.shape
    heads = keys_ref.shape[0]
    head_size = width // heads
    rows, spread = var_count * pixels, var_count * heads
    scale = 1.0 / math.sqrt(head_size)
    waits = fetch(
        (
            (var_embed_hbm, var_embed_ref),
            (keys_hbm, keys_ref),
            (embed_hbm, embed_ref),
            (patches_hbm, patches_ref),
            (value_hbm, value_ref),
            (out_w_hbm, out_w_ref),
            (pos_hbm, pos_ref),
            (gain_hbm, gain_ref),
        ),
        sems,
    )
    line = iota((var_count, var_count), 0)
    order = jnp.zeros((var_count, var_count), jnp.int32)
    for j in range(var_count):
        order = jnp.where(line == j, order_ref[j], order)
    select = (order == iota((var_count, var_count), 1)).astype(F32).astype(BF16)
    waits[0]()
    offsets = dot(select, var_embed_ref[...]).astype(BF16)
    waits[1]()
    repeat = (within(iota((LANES, heads), 0), heads) == iota((LANES, heads), 1)).astype(F32).astype(BF16)
    keys = dot(repeat, keys_ref[...]).astype(BF16)
    offset_keys = dot_t(offsets, keys)
    waits[2]()
    for j in range(var_count):
        table_ref[j] = embed_ref[order_ref[j]]
    table = table_ref[...].reshape(rows, width)
    table_keys = dot_t(table, keys)
    high = table_keys.astype(BF16)
    low = (table_keys - high.astype(F32)).astype(BF16)
    waits[3]()
    patches = patches_ref[...]
    group = math.gcd(spread, 256)
    lines = group // heads * pixels
    same = over(iota((lines, LANES), 0), pixels)
    cols_of = over(iota((lines, LANES), 1), heads)
    channel = over(iota((var_count, LANES), 1), heads)
    scores = []
    for part in range(spread // group):
        here = slice(part * lines, (part + 1) * lines)
        highs, lows, shifts = [], [], []
        for block in range(group // LANES):
            first = block * (LANES // heads)
            match = same == cols_of + first
            highs.append(jnp.where(match, high[here], jnp.zeros_like(high[here])))
            lows.append(jnp.where(match, low[here], jnp.zeros_like(low[here])))
            match = channel + (first + part * (group // heads)) == iota((var_count, LANES), 0)
            shifts.append(jnp.sum(jnp.where(match, offset_keys, 0.0), axis=0, keepdims=True))
        total = dot(patches[:, here], jnp.concatenate(highs, axis=1))
        total = total + dot(patches[:, here], jnp.concatenate(lows, axis=1))
        for block, shift in enumerate(shifts):
            scores.append((total[:, block * LANES : (block + 1) * LANES] + shift) * scale)
    waits[4]()
    values_ref[...] = dot(table, value_ref[...]).astype(BF16)
    offset_values = dot(offsets, value_ref[...]).astype(BF16)
    top = functools.reduce(jnp.maximum, scores)
    step = heads
    while step < LANES:
        top = jnp.maximum(top, pltpu.roll(top, step, 1))
        step *= 2
    exps = [jnp.exp(s - top) for s in scores]
    total = functools.reduce(jnp.add, exps)
    step = heads
    while step < LANES:
        total = total + pltpu.roll(total, step, 1)
        step *= 2
    probs = jnp.concatenate([(e / total).astype(BF16) for e in exps], axis=1)
    base = dot(probs, spread_offsets(offset_values, heads, head_size, 0))
    values = mix_heads(
        probs, patches, values_ref, base, 0, heads // 2, heads, head_size, pixels
    )
    for wait in waits[5:]:
        wait()
    tokens_zero = (dot(values, out_w_ref[...]) + pos_ref[...].astype(F32)).astype(BF16)
    tokens_ref[...] = tokens_zero
    full = tokens_zero.astype(F32)
    centred = full - jnp.mean(full, axis=-1, keepdims=True)
    variance = jnp.mean(centred * centred, axis=-1, keepdims=True)
    normed_ref[...] = (centred * lax.rsqrt(variance + 1e-05) * gain_ref[...]).astype(BF16)


def cost(gflops, mib, exps=0):
    return pl.CostEstimate(
        flops=int(gflops * 1e9), bytes_accessed=int(mib * (1 << 20)), transcendentals=exps
    )


VMEM = pl.BlockSpec(memory_space=pltpu.VMEM)
SMEM = pl.BlockSpec(memory_space=pltpu.SMEM)
HBM = pl.BlockSpec(memory_space=pltpu.HBM)


def like(*arrays):
    return [pltpu.VMEM(a.shape, a.dtype) for a in arrays]


def aggregate(var_order, var_embed, keys, embed_weight, patches, value, out_w, pos, gain):
    tokens, width = pos.shape
    var_count, pixels, _ = embed_weight.shape
    arrays = (var_embed, keys, embed_weight, patches, value, out_w, pos, gain.reshape(1, width))
    return pl.pallas_call(
        aggregate_kernel,
        out_shape=[jax.ShapeDtypeStruct((tokens, width), BF16)] * 2,
        in_specs=[SMEM] + [HBM] * len(arrays),
        out_specs=[VMEM] * 2,
        scratch_shapes=like(*arrays)
        + like(embed_weight)
        + [pltpu.VMEM((var_count * pixels, width), BF16)]
        + [pltpu.SemaphoreType.DMA((len(arrays),))],
        compiler_params=pltpu.CompilerParams(vmem_limit_bytes=WHOLE_VMEM),
        cost_estimate=cost(16, 8, 1 << 18),
        name="aggregate",
    )(var_order, *arrays)


def assemble_kernel(*refs, spots):
    weight_refs, out_ref, sems = refs[:-2], refs[-2], refs[-1]
    index, plane = lax.axis_index("space"), lax.axis_index("groups")
    moves = []
    for ref, parts in zip(weight_refs, spots):
        for first, rows, step, start0, start1 in parts:
            start = pl.multiple_of(jnp.where(plane == 0, start0, start1), 32)
            place = out_ref.at[chip_at(index, step), pl.ds(start, rows), :]
            moves.append((ref.at[pl.ds(first, rows), :], place))
    for wait in fetch(moves, sems):
        wait()


def assemble(weights):
    spots = tuple(spot for _, spot in weights)
    weights = [piece for piece, _ in weights]
    blocks = 1 if len(weights) == 1 else len(RING)
    return pl.pallas_call(
        functools.partial(assemble_kernel, spots=spots),
        out_shape=jax.ShapeDtypeStruct((blocks,) + weights[0].shape, BF16),
        in_specs=[HBM] * len(weights),
        out_specs=VMEM,
        scratch_shapes=[pltpu.SemaphoreType.DMA((32,))],
        compiler_params=pltpu.CompilerParams(vmem_limit_bytes=PART_VMEM),
        cost_estimate=cost(1, 6),
        name="assemble",
    )(*weights)


def attend_kernel(*refs, flipped):
    weight_ref, mine_ref, other_ref, query_s, key_s, value_s = refs[6:]
    index = lax.axis_index("space")
    side = index % 2
    flip = index // 2 % 2 if flipped else 0
    near, far = 4 - 4 * flip, 4 * flip
    tokens, width = refs[0].shape
    pairs = mine_ref.shape[0]
    cols = pairs * LANES
    weight = weight_ref[...].reshape(3 * cols, width)
    head_size = LANES // 2
    scale = 1.0 / math.sqrt(head_size)
    pieces = (2 + side, 3 - side, near + side, near + 1 - side, far + side, far + 1 - side)
    ones = jnp.ones((tokens, LANES), BF16)
    for number, place in enumerate(pieces):
        rows = refs[number][...]
        both = dot_t(rows, weight[cols:]).astype(BF16)
        spot = pl.ds(pl.multiple_of(place * tokens, tokens), tokens)
        for pair in range(pairs):
            lanes = slice(pair * LANES, (pair + 1) * LANES)
            key_s[pair, spot, :] = both[:, :cols][:, lanes]
            value_s[pair, spot, :] = jnp.concatenate([both[:, cols:][:, lanes], ones], axis=1)
        if number < 2:
            query = (dot_t(rows, weight[:cols]).astype(BF16).astype(F32) * scale).astype(BF16)
            for pair in range(pairs):
                query_s[number, pair] = query[:, pair * LANES : (pair + 1) * LANES]

    left_half = iota((tokens, LANES), 1) < head_size

    def attend(pair, carry):
        for number, (out_ref, sector) in enumerate(((mine_ref, side), (other_ref, 1 - side))):
            query = query_s[number, pair]
            halves = []
            for half in range(2):
                keep = left_half if half == 0 else jnp.logical_not(left_half)
                masked = jnp.where(keep, query, jnp.zeros_like(query))
                start = pl.multiple_of(sector * tokens, tokens)
                scores = [
                    dot_t(masked, key_s[pair, pl.ds(start + k * tokens, tokens), :])
                    for k in range(5)
                ]
                top = jnp.max(functools.reduce(jnp.maximum, scores), axis=-1, keepdims=True)
                probs = jnp.concatenate([jnp.exp(s - top).astype(BF16) for s in scores], axis=1)
                acc = dot(probs, value_s[pair, pl.ds(start, 5 * tokens), :])
                halves.append(acc[:, :LANES] / acc[:, LANES:])
            out_ref[pair] = jnp.where(left_half, halves[0], halves[1]).astype(BF16)
        return carry

    lax.fori_loop(0, pairs, attend, 0, unroll=True)


def attend(pieces, weight):
    tokens, width = pieces[0].shape
    blocks, rows, _ = weight.shape
    cols = rows * blocks // 3
    pairs = cols // LANES
    return pl.pallas_call(
        functools.partial(attend_kernel, flipped=blocks > 1),
        out_shape=[jax.ShapeDtypeStruct((pairs, tokens, LANES), BF16)] * 2,
        in_specs=[VMEM] * 7,
        out_specs=[VMEM, VMEM],
        scratch_shapes=[
            pltpu.VMEM((2, pairs, tokens, LANES), BF16),
            pltpu.VMEM((pairs, 6 * tokens, LANES), BF16),
            pltpu.VMEM((pairs, 6 * tokens, 2 * LANES), BF16),
        ],
        compiler_params=pltpu.CompilerParams(vmem_limit_bytes=PART_VMEM),
        cost_estimate=cost(10, 8, 5 << 20),
        name="attend",
    )(*pieces, weight)


def finish_kernel(tokens_ref, mine_ref, other_ref, weight_ref, out_ref):
    side = lax.axis_index("space") % 2
    pairs, tokens, lanes = mine_ref.shape
    width = tokens_ref.shape[1]

    def part(ref, parity):
        rows = jnp.concatenate([ref[pair] for pair in range(pairs)], axis=1)
        return dot(rows, weight_ref[:, parity].reshape(pairs * lanes, width))

    update = part(mine_ref, side) + part(other_ref, 1 - side)
    out_ref[...] = (tokens_ref[...].astype(F32) + update).astype(BF16)


def finish(tokens_zero, mine, other, attn_out):
    tokens, width = tokens_zero.shape
    return pl.pallas_call(
        finish_kernel,
        out_shape=jax.ShapeDtypeStruct((tokens, width), BF16),
        in_specs=[VMEM] * 4,
        out_specs=VMEM,
        compiler_params=pltpu.CompilerParams(vmem_limit_bytes=PART_VMEM),
        cost_estimate=cost(1, 4),
        name="finish",
    )(tokens_zero, mine, other, attn_out.reshape(-1, 2, LANES // 2, width))


def sibling(value):
    length = lax.axis_size("space")
    return lax.ppermute(value, "space", [(i, i ^ 1) for i in range(length)])


def from_chip(value, by):
    length = lax.axis_size("space")
    return lax.ppermute(value, "space", [((i + 2 * by) % length, i) for i in range(length)])


def around(value, by):
    pairs = []
    for place, chip in enumerate(RING):
        for core in range(2):
            step = by if isinstance(by, int) else by[core]
            pairs.append((2 * chip + core, 2 * RING[(place + step) % len(RING)] + core))
    return lax.ppermute(value, "space", pairs)


def crossed(value, bits):
    return lax.ppermute(value, "space", [(i, i ^ bits) for i in range(2 * len(RING))])


def onward(value):
    length = 2 * len(RING)
    pairs = [(i, (i + (4 if i & 2 == 0 else -4)) % length) for i in range(length)]
    return lax.ppermute(value, "space", pairs)


def across(value):
    return lax.ppermute(value, "groups", [(0, 1), (1, 0)])


def together(*values):
    return lax.optimization_barrier(values)


def parity_block(qkv_weight, side, head_size):
    rows = qkv_weight.T
    low, middle, high = (rows[i * head_size : (i + 1) * head_size] for i in range(3))
    given = sibling(middle)
    return jnp.where(
        side == 0,
        jnp.concatenate([low, high, given], axis=0),
        jnp.concatenate([given, low, high], axis=0),
    )


def parity_weight(qkv_weight, side, head_size):
    rows = lax.all_gather(qkv_weight.T, "space", axis=0, tiled=True)
    blocks = rows.reshape(-1, 2, head_size, rows.shape[1])
    picked = lax.dynamic_index_in_dim(blocks, side, 1, keepdims=False)
    picked = picked.reshape(-1, rows.shape[1])
    return [(picked, ((0, picked.shape[0], None, 0, 0),))]


def per_device(
    patches,
    var_order,
    embed_weight,
    var_embed,
    agg_keys,
    agg_value,
    agg_out,
    pos_embed,
    norm_gain,
    qkv_weight,
    attn_out,
):
    heads = agg_keys.shape[0]
    head_size = embed_weight.shape[2] // heads
    side = lax.axis_index("space") % 2
    ringed = (
        lax.axis_size("space") == 2 * len(RING)
        and lax.axis_size("groups") == 2
        and qkv_weight.shape[1] == 3 * head_size
    )
    if ringed:
        block = parity_block(qkv_weight, side, head_size)
        block, embed_weight = together(block, embed_weight)
        third = block.shape[0] // 3
        plane = lax.axis_index("groups")
        share = lax.dynamic_slice_in_dim(block, plane * third, 2 * third, 0)
        early = [around(share, step) for step in (1, -1, 2, -2)]
        weights = [(block, ((0, 3 * third, 0, 0, 0),))]
    else:
        weights = parity_weight(qkv_weight, side, head_size)
    tokens_zero, normed = aggregate(
        var_order, var_embed, agg_keys, embed_weight, patches, agg_value, agg_out, pos_embed, norm_gain
    )
    if ringed:

        def swapped(blocks, *whole):
            parts = [lax.dynamic_slice_in_dim(b, plane * third, third, 0) for b in blocks]
            parts += whole
            return across(jnp.concatenate(parts, axis=0))

        tokens_zero, *early = together(tokens_zero, *early)
        ring = [((0, 2 * third, step, 0, third),) for step in (-1, 1, -2, 2, "pair", "beside")]
        weights += list(zip(early, ring))
        swap = swapped(early)
        place = ring_place(lax.axis_index("space"))
        near = crossed(normed, 2)
        low = place % 4 < 2
        opposite = jnp.where(low, early[2], early[3])
        opposite = lax.dynamic_slice_in_dim(opposite, plane * (third // 2), 3 * third // 2, 0)
        opposite = crossed(opposite, 8)
        pair = crossed(jnp.where(place % 2 == 0, early[2], early[3]), 4)
        near, opposite, pair = together(near, opposite, pair)
        far, near_sib = onward(near), sibling(near)
        beside = crossed(jnp.where(low, early[3], early[2]), 2)
        first = swapped([pair], opposite)
        swap, near_sib, beside = together(swap, near_sib, beside)
        second = swapped([beside])
        _, _, far = together(first, second, far)
        half = 3 * third // 2
        swaps = [(i * third, third, step, 2 * third, 0) for i, step in enumerate((-1, 1, -2, 2))]
        weights += [(pair, ring[4]), (beside, ring[5]), (opposite, ((0, half, 4, 0, half),))]
        weights += [(swap, tuple(swaps)), (second, ((0, third, "beside", 2 * third, 0),))]
        weights += [(first, ((0, third, "pair", 2 * third, 0), (third, half, 4, half, 0)))]
    else:
        near, far = from_chip(normed, 1), from_chip(normed, -1)
        near_sib = sibling(near)
    pieces = (normed, sibling(normed), near, near_sib, far, sibling(far))
    mine, other = attend(pieces, assemble(weights))
    return finish(tokens_zero, mine, sibling(other), attn_out)


def solution(mesh):
    in_specs = (
        P(("groups", "space"), None),
        P(),
        P(),
        P(),
        P(),
        P(),
        P(),
        P("space", None),
        P(),
        P(None, "space"),
        P(),
    )
    out_specs = P(("groups", "space"), None)
    return jax.shard_map(
        per_device, mesh=mesh, in_specs=in_specs, out_specs=out_specs, check_vma=False
    )
```

```python
import functools
import math

import jax
import jax.numpy as jnp
from jax import lax
from jax.experimental import pallas as pl
from jax.experimental.pallas import tpu as pltpu
from jax.sharding import PartitionSpec as P

BF16 = jnp.bfloat16
F32 = jnp.float32
LANES = 128
WHOLE_VMEM = 60 * 1024 * 1024
PART_VMEM = 24 * 1024 * 1024
RING = (0, 2, 4, 6, 7, 5, 3, 1)


def dot(left, right):
    return jnp.dot(left, right, preferred_element_type=F32)


def dot_t(left, right):
    return lax.dot_general(left, right, (((1,), (1,)), ((), ())), preferred_element_type=F32)


def ring_place(index):
    chip = index // 2
    return jnp.where(chip % 2 == 0, chip // 2, 7 - chip // 2)


def chip_at(index, step):
    if step is None:
        return 0
    here = ring_place(index)
    if step == "beside":
        step = jnp.where(here % 2 == 0, -3, 3)
    elif step == "pair":
        step = jnp.where(here % 2 == 0, 3, -3)
    at = (here + step + 8) % 8
    return jnp.where(at < 4, 2 * at, 2 * (7 - at) + 1)


def iota(shape, dim):
    return lax.broadcasted_iota(jnp.int32, shape, dim)


def over(x, n):
    return x >> (n.bit_length() - 1) if n & (n - 1) == 0 else x // n


def within(x, n):
    return x & (n - 1) if n & (n - 1) == 0 else x % n


def fetch(pairs, sems):
    copies = [pltpu.make_async_copy(src, dst, sems.at[i]) for i, (src, dst) in enumerate(pairs)]
    for copy in copies:
        copy.start()
    return [copy.wait for copy in copies]


def spread_offsets(offset_half, heads, head_size, first):
    var_count, half = offset_half.shape
    spread = var_count * heads
    picks = (over(iota((spread, var_count), 0), heads) == iota((spread, var_count), 1)).astype(F32)
    rows = dot(picks.astype(BF16), offset_half).astype(BF16)
    mine = within(iota((spread, half), 0), heads) == over(iota((spread, half), 1), head_size) + first
    return jnp.where(mine, rows, jnp.zeros_like(rows))


def mix_heads(probs, patches, table_values, base, first, pairs, heads, head_size, pixels):
    tokens, spread = probs.shape
    group = math.gcd(spread, 256)
    row_g, col_g = iota((group, group), 0), iota((group, group), 1)
    same = over(row_g, heads) == over(col_g, pixels)
    head_g = jnp.where(same, within(row_g, heads), -1)
    left_half = iota((tokens, 2 * head_size), 1) < head_size
    values = []
    for pair in range(pairs):
        halves = []
        cols = slice(pair * 2 * head_size, (pair + 1) * 2 * head_size)
        for head in (first + 2 * pair, first + 2 * pair + 1):
            pick = jnp.where(head_g == head, 1.0, 0.0).astype(BF16)
            weights = jnp.concatenate(
                [
                    dot(probs[:, g * group : (g + 1) * group], pick).astype(BF16)
                    for g in range(spread // group)
                ],
                axis=1,
            )
            halves.append(dot(weights * patches, table_values[:, cols]))
        values.append((jnp.where(left_half, halves[0], halves[1]) + base[:, cols]).astype(BF16))
    return jnp.concatenate(values, axis=1)


def aggregate_kernel(
    order_ref,
    var_embed_hbm,
    keys_hbm,
    embed_hbm,
    patches_hbm,
    value_hbm,
    out_w_hbm,
    pos_hbm,
    gain_hbm,
    tokens_ref,
    normed_ref,
    var_embed_ref,
    keys_ref,
    embed_ref,
    patches_ref,
    value_ref,
    out_w_ref,
    pos_ref,
    gain_ref,
    table_ref,
    values_ref,
    sems,
):
    var_count, pixels, width = embed_ref.shape
    heads = keys_ref.shape[0]
    head_size = width // heads
    rows, spread = var_count * pixels, var_count * heads
    scale = 1.0 / math.sqrt(head_size)
    waits = fetch(
        (
            (var_embed_hbm, var_embed_ref),
            (keys_hbm, keys_ref),
            (embed_hbm, embed_ref),
            (patches_hbm, patches_ref),
            (value_hbm, value_ref),
            (out_w_hbm, out_w_ref),
            (pos_hbm, pos_ref),
            (gain_hbm, gain_ref),
        ),
        sems,
    )
    line = iota((var_count, var_count), 0)
    order = jnp.zeros((var_count, var_count), jnp.int32)
    for j in range(var_count):
        order = jnp.where(line == j, order_ref[j], order)
    select = (order == iota((var_count, var_count), 1)).astype(F32).astype(BF16)
    waits[0]()
    offsets = dot(select, var_embed_ref[...]).astype(BF16)
    waits[1]()
    repeat = (within(iota((LANES, heads), 0), heads) == iota((LANES, heads), 1)).astype(F32).astype(BF16)
    keys = dot(repeat, keys_ref[...]).astype(BF16)
    offset_keys = dot_t(offsets, keys)
    waits[2]()
    for j in range(var_count):
        table_ref[j] = embed_ref[order_ref[j]]
    table = table_ref[...].reshape(rows, width)
    table_keys = dot_t(table, keys)
    high = table_keys.astype(BF16)
    low = (table_keys - high.astype(F32)).astype(BF16)
    waits[3]()
    patches = patches_ref[...]
    group = math.gcd(spread, 256)
    lines = group // heads * pixels
    same = over(iota((lines, LANES), 0), pixels)
    cols_of = over(iota((lines, LANES), 1), heads)
    channel = over(iota((var_count, LANES), 1), heads)
    scores = []
    for part in range(spread // group):
        here = slice(part * lines, (part + 1) * lines)
        highs, lows, shifts = [], [], []
        for block in range(group // LANES):
            first = block * (LANES // heads)
            match = same == cols_of + first
            highs.append(jnp.where(match, high[here], jnp.zeros_like(high[here])))
            lows.append(jnp.where(match, low[here], jnp.zeros_like(low[here])))
            match = channel + (first + part * (group // heads)) == iota((var_count, LANES), 0)
            shifts.append(jnp.sum(jnp.where(match, offset_keys, 0.0), axis=0, keepdims=True))
        total = dot(patches[:, here], jnp.concatenate(highs, axis=1))
        total = total + dot(patches[:, here], jnp.concatenate(lows, axis=1))
        for block, shift in enumerate(shifts):
            scores.append((total[:, block * LANES : (block + 1) * LANES] + shift) * scale)
    waits[4]()
    values_ref[...] = dot(table, value_ref[...]).astype(BF16)
    offset_values = dot(offsets, value_ref[...]).astype(BF16)
    top = functools.reduce(jnp.maximum, scores)
    step = heads
    while step < LANES:
        top = jnp.maximum(top, pltpu.roll(top, step, 1))
        step *= 2
    exps = [jnp.exp(s - top) for s in scores]
    total = functools.reduce(jnp.add, exps)
    step = heads
    while step < LANES:
        total = total + pltpu.roll(total, step, 1)
        step *= 2
    probs = jnp.concatenate([(e / total).astype(BF16) for e in exps], axis=1)
    base = dot(probs, spread_offsets(offset_values, heads, head_size, 0))
    values = mix_heads(
        probs, patches, values_ref, base, 0, heads // 2, heads, head_size, pixels
    )
    for wait in waits[5:]:
        wait()
    tokens_zero = (dot(values, out_w_ref[...]) + pos_ref[...].astype(F32)).astype(BF16)
    tokens_ref[...] = tokens_zero
    full = tokens_zero.astype(F32)
    centred = full - jnp.mean(full, axis=-1, keepdims=True)
    variance = jnp.mean(centred * centred, axis=-1, keepdims=True)
    normed_ref[...] = (centred * lax.rsqrt(variance + 1e-05) * gain_ref[...]).astype(BF16)


def cost(gflops, mib, exps=0):
    return pl.CostEstimate(
        flops=int(gflops * 1e9), bytes_accessed=int(mib * (1 << 20)), transcendentals=exps
    )


VMEM = pl.BlockSpec(memory_space=pltpu.VMEM)
SMEM = pl.BlockSpec(memory_space=pltpu.SMEM)
HBM = pl.BlockSpec(memory_space=pltpu.HBM)


def like(*arrays):
    return [pltpu.VMEM(a.shape, a.dtype) for a in arrays]


def aggregate(var_order, var_embed, keys, embed_weight, patches, value, out_w, pos, gain):
    tokens, width = pos.shape
    var_count, pixels, _ = embed_weight.shape
    arrays = (var_embed, keys, embed_weight, patches, value, out_w, pos, gain.reshape(1, width))
    return pl.pallas_call(
        aggregate_kernel,
        out_shape=[jax.ShapeDtypeStruct((tokens, width), BF16)] * 2,
        in_specs=[SMEM] + [HBM] * len(arrays),
        out_specs=[VMEM] * 2,
        scratch_shapes=like(*arrays)
        + like(embed_weight)
        + [pltpu.VMEM((var_count * pixels, width), BF16)]
        + [pltpu.SemaphoreType.DMA((len(arrays),))],
        compiler_params=pltpu.CompilerParams(vmem_limit_bytes=WHOLE_VMEM),
        cost_estimate=cost(16, 8, 1 << 18),
        name="aggregate",
    )(var_order, *arrays)


def assemble_kernel(*refs, spots):
    weight_refs, out_ref, sems = refs[:-2], refs[-2], refs[-1]
    index, plane = lax.axis_index("space"), lax.axis_index("groups")
    moves = []
    for ref, parts in zip(weight_refs, spots):
        for first, rows, step, start0, start1 in parts:
            start = pl.multiple_of(jnp.where(plane == 0, start0, start1), 32)
            place = out_ref.at[chip_at(index, step), pl.ds(start, rows), :]
            moves.append((ref.at[pl.ds(first, rows), :], place))
    for wait in fetch(moves, sems):
        wait()


def assemble(weights):
    spots = tuple(spot for _, spot in weights)
    weights = [piece for piece, _ in weights]
    blocks = 1 if len(weights) == 1 else len(RING)
    return pl.pallas_call(
        functools.partial(assemble_kernel, spots=spots),
        out_shape=jax.ShapeDtypeStruct((blocks,) + weights[0].shape, BF16),
        in_specs=[HBM] * len(weights),
        out_specs=VMEM,
        scratch_shapes=[pltpu.SemaphoreType.DMA((32,))],
        compiler_params=pltpu.CompilerParams(vmem_limit_bytes=PART_VMEM),
        cost_estimate=cost(1, 6),
        name="assemble",
    )(*weights)


def attend_kernel(*refs, flipped):
    weight_ref, mine_ref, other_ref, query_s, key_s, value_s = refs[6:]
    index = lax.axis_index("space")
    side = index % 2
    flip = index // 2 % 2 if flipped else 0
    near, far = 4 - 4 * flip, 4 * flip
    tokens, width = refs[0].shape
    pairs = mine_ref.shape[0]
    cols = pairs * LANES
    weight = weight_ref[...].reshape(3 * cols, width)
    head_size = LANES // 2
    scale = 1.0 / math.sqrt(head_size)
    pieces = (2 + side, 3 - side, near + side, near + 1 - side, far + side, far + 1 - side)
    ones = jnp.ones((tokens, LANES), BF16)
    for number, place in enumerate(pieces):
        rows = refs[number][...]
        both = dot_t(rows, weight[cols:]).astype(BF16)
        spot = pl.ds(pl.multiple_of(place * tokens, tokens), tokens)
        for pair in range(pairs):
            lanes = slice(pair * LANES, (pair + 1) * LANES)
            key_s[pair, spot, :] = both[:, :cols][:, lanes]
            value_s[pair, spot, :] = jnp.concatenate([both[:, cols:][:, lanes], ones], axis=1)
        if number < 2:
            query = (dot_t(rows, weight[:cols]).astype(BF16).astype(F32) * scale).astype(BF16)
            for pair in range(pairs):
                query_s[number, pair] = query[:, pair * LANES : (pair + 1) * LANES]

    left_half = iota((tokens, LANES), 1) < head_size

    def attend(pair, carry):
        for number, (out_ref, sector) in enumerate(((mine_ref, side), (other_ref, 1 - side))):
            query = query_s[number, pair]
            halves = []
            for half in range(2):
                keep = left_half if half == 0 else jnp.logical_not(left_half)
                masked = jnp.where(keep, query, jnp.zeros_like(query))
                start = pl.multiple_of(sector * tokens, tokens)
                scores = [
                    dot_t(masked, key_s[pair, pl.ds(start + k * tokens, tokens), :])
                    for k in range(5)
                ]
                top = jnp.max(functools.reduce(jnp.maximum, scores), axis=-1, keepdims=True)
                probs = jnp.concatenate([jnp.exp(s - top).astype(BF16) for s in scores], axis=1)
                acc = dot(probs, value_s[pair, pl.ds(start, 5 * tokens), :])
                halves.append(acc[:, :LANES] / acc[:, LANES:])
            out_ref[pair] = jnp.where(left_half, halves[0], halves[1]).astype(BF16)
        return carry

    lax.fori_loop(0, pairs, attend, 0, unroll=True)


def attend(pieces, weight):
    tokens, width = pieces[0].shape
    blocks, rows, _ = weight.shape
    cols = rows * blocks // 3
    pairs = cols // LANES
    return pl.pallas_call(
        functools.partial(attend_kernel, flipped=blocks > 1),
        out_shape=[jax.ShapeDtypeStruct((pairs, tokens, LANES), BF16)] * 2,
        in_specs=[VMEM] * 7,
        out_specs=[VMEM, VMEM],
        scratch_shapes=[
            pltpu.VMEM((2, pairs, tokens, LANES), BF16),
            pltpu.VMEM((pairs, 6 * tokens, LANES), BF16),
            pltpu.VMEM((pairs, 6 * tokens, 2 * LANES), BF16),
        ],
        compiler_params=pltpu.CompilerParams(vmem_limit_bytes=PART_VMEM),
        cost_estimate=cost(10, 8, 5 << 20),
        name="attend",
    )(*pieces, weight)


def finish_kernel(tokens_ref, mine_ref, other_ref, weight_ref, out_ref):
    side = lax.axis_index("space") % 2
    pairs, tokens, lanes = mine_ref.shape
    width = tokens_ref.shape[1]

    def part(ref, parity):
        rows = jnp.concatenate([ref[pair] for pair in range(pairs)], axis=1)
        return dot(rows, weight_ref[:, parity].reshape(pairs * lanes, width))

    update = part(mine_ref, side) + part(other_ref, 1 - side)
    out_ref[...] = (tokens_ref[...].astype(F32) + update).astype(BF16)


def finish(tokens_zero, mine, other, attn_out):
    tokens, width = tokens_zero.shape
    return pl.pallas_call(
        finish_kernel,
        out_shape=jax.ShapeDtypeStruct((tokens, width), BF16),
        in_specs=[VMEM] * 4,
        out_specs=VMEM,
        compiler_params=pltpu.CompilerParams(vmem_limit_bytes=PART_VMEM),
        cost_estimate=cost(1, 4),
        name="finish",
    )(tokens_zero, mine, other, attn_out.reshape(-1, 2, LANES // 2, width))


def sibling(value):
    length = lax.axis_size("space")
    return lax.ppermute(value, "space", [(i, i ^ 1) for i in range(length)])


def from_chip(value, by):
    length = lax.axis_size("space")
    return lax.ppermute(value, "space", [((i + 2 * by) % length, i) for i in range(length)])


def around(value, by):
    pairs = []
    for place, chip in enumerate(RING):
        for core in range(2):
            step = by if isinstance(by, int) else by[core]
            pairs.append((2 * chip + core, 2 * RING[(place + step) % len(RING)] + core))
    return lax.ppermute(value, "space", pairs)


def crossed(value, bits):
    return lax.ppermute(value, "space", [(i, i ^ bits) for i in range(2 * len(RING))])


def onward(value):
    length = 2 * len(RING)
    pairs = [(i, (i + (4 if i & 2 == 0 else -4)) % length) for i in range(length)]
    return lax.ppermute(value, "space", pairs)


def across(value):
    return lax.ppermute(value, "groups", [(0, 1), (1, 0)])


def together(*values):
    return lax.optimization_barrier(values)


def parity_block(qkv_weight, side, head_size):
    rows = qkv_weight.T
    low, middle, high = (rows[i * head_size : (i + 1) * head_size] for i in range(3))
    given = sibling(middle)
    return jnp.where(
        side == 0,
        jnp.concatenate([low, high, given], axis=0),
        jnp.concatenate([given, low, high], axis=0),
    )


def parity_weight(qkv_weight, side, head_size):
    rows = lax.all_gather(qkv_weight.T, "space", axis=0, tiled=True)
    blocks = rows.reshape(-1, 2, head_size, rows.shape[1])
    picked = lax.dynamic_index_in_dim(blocks, side, 1, keepdims=False)
    picked = picked.reshape(-1, rows.shape[1])
    return [(picked, ((0, picked.shape[0], None, 0, 0),))]


def per_device(
    patches,
    var_order,
    embed_weight,
    var_embed,
    agg_keys,
    agg_value,
    agg_out,
    pos_embed,
    norm_gain,
    qkv_weight,
    attn_out,
):
    heads = agg_keys.shape[0]
    head_size = embed_weight.shape[2] // heads
    side = lax.axis_index("space") % 2
    ringed = (
        lax.axis_size("space") == 2 * len(RING)
        and lax.axis_size("groups") == 2
        and qkv_weight.shape[1] == 3 * head_size
    )
    if ringed:
        block = parity_block(qkv_weight, side, head_size)
        block, embed_weight = together(block, embed_weight)
        third = block.shape[0] // 3
        plane = lax.axis_index("groups")
        share = lax.dynamic_slice_in_dim(block, plane * third, 2 * third, 0)
        early = [around(share, step) for step in (1, -1, 2, -2)]
        weights = [(block, ((0, 3 * third, 0, 0, 0),))]
    else:
        weights = parity_weight(qkv_weight, side, head_size)
    tokens_zero, normed = aggregate(
        var_order, var_embed, agg_keys, embed_weight, patches, agg_value, agg_out, pos_embed, norm_gain
    )
    if ringed:

        def swapped(blocks, *whole):
            parts = [lax.dynamic_slice_in_dim(b, plane * third, third, 0) for b in blocks]
            parts += whole
            return across(jnp.concatenate(parts, axis=0))

        tokens_zero, *early = together(tokens_zero, *early)
        ring = [((0, 2 * third, step, 0, third),) for step in (-1, 1, -2, 2, "pair", "beside")]
        weights += list(zip(early, ring))
        swap = swapped(early)
        place = ring_place(lax.axis_index("space"))
        near = crossed(normed, 2)
        low = place % 4 < 2
        opposite = jnp.where(low, early[2], early[3])
        opposite = lax.dynamic_slice_in_dim(opposite, plane * (third // 2), 3 * third // 2, 0)
        opposite = crossed(opposite, 8)
        pair = crossed(jnp.where(place % 2 == 0, early[2], early[3]), 4)
        beside = jnp.where(low, early[3], early[2])
        near, opposite, pair, beside = together(near, opposite, pair, beside)
        far, near_sib, beside = onward(near), sibling(near), crossed(beside, 2)
        first = swapped([pair], opposite)
        swap, near_sib, beside = together(swap, near_sib, beside)
        second = swapped([beside])
        _, _, far = together(first, second, far)
        half = 3 * third // 2
        swaps = [(i * third, third, step, 2 * third, 0) for i, step in enumerate((-1, 1, -2, 2))]
        weights += [(pair, ring[4]), (beside, ring[5]), (opposite, ((0, half, 4, 0, half),))]
        weights += [(swap, tuple(swaps)), (second, ((0, third, "beside", 2 * third, 0),))]
        weights += [(first, ((0, third, "pair", 2 * third, 0), (third, half, 4, half, 0)))]
    else:
        near, far = from_chip(normed, 1), from_chip(normed, -1)
        near_sib = sibling(near)
    pieces = (normed, sibling(normed), near, near_sib, far, sibling(far))
    mine, other = attend(pieces, assemble(weights))
    return finish(tokens_zero, mine, sibling(other), attn_out)


def solution(mesh):
    in_specs = (
        P(("groups", "space"), None),
        P(),
        P(),
        P(),
        P(),
        P(),
        P(),
        P("space", None),
        P(),
        P(None, "space"),
        P(),
    )
    out_specs = P(("groups", "space"), None)
    return jax.shard_map(
        per_device, mesh=mesh, in_specs=in_specs, out_specs=out_specs, check_vma=False
    )
```
